32 devices in a mesh: dp: 2 (over core), mp: 4 (over y, x), hidden: 4 (over z).
Axes of the slice: x: 2, y: 2, z: 4, core: 2. Of those that a mesh axis runs over, the one named last changes fastest.
Arguments:
- stored: bfloat16 [768, 32768], P('mp', ('dp', 'hidden')), may hold values from -51 to 51
- positions: int32 [32768], P(('dp', 'hidden')), may hold values from 0 to 1211, as said below
- segments: int32 [32768], P(('dp', 'hidden', 'mp')), may hold values from 0 to 8, as said below
- present: int32 [32768], P(('dp', 'hidden', 'mp')), may hold values from 0 to 1, as said below
- norm_gains: float32 [2, 768], P(None, 'mp'), may hold values from 0.1 to 1.9
- norm_biases: float32 [2, 768], P(None, 'mp'), may hold values from -3 to 3
- input_proj: bfloat16 [768, 3, 768], P('mp', None, 'hidden'), may hold values from -0.3125 to 0.3125
- input_bias: bfloat16 [2, 768], P(None, 'hidden'), may hold values from -3 to 3
- output_proj: bfloat16 [768, 768], P('hidden', 'mp'), may hold values from -0.875 to 0.875
- output_bias: bfloat16 [768], P('mp'), may hold values from -3 to 3
- expand_weight: bfloat16 [768, 3072], P('mp', 'hidden'), may hold values from -0.21875 to 0.21875
- expand_bias: bfloat16 [3072], P('hidden'), may hold values from -3 to 3
- reduce_weight: bfloat16 [768, 3072], P('mp', 'hidden'), may hold values from -0.109375 to 0.109375
- reduce_bias: bfloat16 [768], P('mp'), may hold values from -3 to 3
- cotangent: bfloat16 [768, 32768], P('mp', ('dp', 'hidden')), may hold values from -6 to 6
Outputs:
- output: bfloat16 [768, 32768], P('mp', ('dp', 'hidden'))
- d_stored: float32 [768, 32768], P('mp', ('dp', 'hidden'))
- d_norm_gains: float32 [2, 768], P(None, ('mp', 'dp', 'hidden'))
- d_norm_biases: float32 [2, 768], P(None, ('mp', 'dp', 'hidden'))
- d_input_proj: float32 [768, 3, 768], P(('mp', 'dp'), None, 'hidden')
- d_input_bias: float32 [2, 768], P(None, ('hidden', 'dp'))
- d_output_proj: float32 [768, 768], P(('hidden', 'dp'), 'mp')
- d_output_bias: float32 [768], P(('mp', 'dp'))
- d_expand_weight: float32 [768, 3072], P(('mp', 'dp'), 'hidden')
- d_expand_bias: float32 [3072], P(('hidden', 'dp'))
- d_reduce_weight: float32 [768, 3072], P(('mp', 'dp'), 'hidden')
- d_reduce_bias: float32 [768], P(('mp', 'dp'))
The draws below stay inside these ranges and needn't reach their ends.
Inputs may be any that keep to these rules, and one draw needn't show every extreme that they name: `segments`: within each packed row of 1024 tokens the clip numbers never fall; every clip but the last of a row holds 128 to 512 tokens; padding tokens carry 8. `present`: padding is the tail of every packed row, 1 to 128 tokens. `positions`: consecutive within a clip; a clip's positions stay below 1212; padding tokens carry 1212 - 1.
All inputs are finite; a program needn't handle non-finite values.
Results may differ from the reference program's by a relative error of at most 0.014.
The reference program's roundings to bfloat16 on the way count: a program that leaves them out, or rounds other values in their place, can miss the bound.
Values may be sent and summed in bfloat16 or wider, within the bound.
A program may use at most 384 MiB of HBM per device.

```python
import math
import jax
import jax.numpy as jnp
from jax import lax

D = 768
HEADS = 12
HD = 64
FF = 3072
SEQ = 1024
POSN = 1212
TOKENS = 32768


def clip_layout(key):
    base_key = jax.random.fold_in(key, 101)
    key_length, key_padding, key_offset = jax.random.split(base_key, 3)
    row_total = TOKENS // SEQ
    lengths = jax.random.randint(key_length, (row_total, 8), SEQ // 8, SEQ // 2 + 1)
    clip_ends = jnp.cumsum(lengths, axis=1)
    clip_starts = clip_ends - lengths
    padding = jax.random.randint(key_padding, (row_total, 1), 1, SEQ // 8 + 1)
    offsets = jax.random.randint(key_offset, (row_total, 8), 0, POSN - lengths + 1)
    places = jnp.arange(SEQ, dtype=jnp.int32)[None, :]
    clip_index = jnp.sum((clip_ends[:, None, :] <= places[:, :, None]).astype(jnp.int32), axis=2)
    clip_index = jnp.minimum(clip_index, 7)
    present = (places < SEQ - padding).astype(jnp.int32)
    first_place = jnp.take_along_axis(clip_starts, clip_index, axis=1)
    clip_offset = jnp.take_along_axis(offsets, clip_index, axis=1)
    positions = jnp.where(present == 1, clip_offset + places - first_place, POSN - 1)
    segments = jnp.where(present == 1, clip_index, 8)
    return (segments.reshape(-1).astype(jnp.int32), present.reshape(-1), positions.reshape(-1).astype(jnp.int32))


def draw_segments(key, part):
    return clip_layout(key)[0]


def draw_present(key, part):
    return clip_layout(key)[1]


def draw_positions(key, part):
    return clip_layout(key)[2]


def draw_stored(key, part):
    base_key = jax.random.fold_in(key, 5)
    key_main, key_columns, key_rows = jax.random.split(base_key, 3)
    columns = jnp.arange(D, dtype=jnp.float32)
    column_scale = jnp.exp(columns * (math.log(3.0) / D)) * jax.random.uniform(key_columns, (D,), jnp.float32, 0.7, 1.4)
    row_scale = jnp.exp(jax.random.uniform(key_rows, (TOKENS, 1), jnp.float32, math.log(0.5), math.log(2.0)))
    main_part = jnp.clip(jax.random.normal(key_main, (TOKENS, D), jnp.float32), -6.0, 6.0)
    return (main_part * row_scale * column_scale[None, :]).T.astype(jnp.bfloat16)


def block_levels(own_key, dims, shards, least, largest):
    def one(position, shards_of):
        heights = jax.random.uniform(jax.random.fold_in(jax.random.fold_in(own_key, 6), position), (shards_of,), jnp.float32, least / len(shards), largest / len(shards))
        return jnp.repeat(jnp.exp(heights), dims[position] // shards_of).reshape((-1,) + (1,) * (len(dims) - position - 1))

    factor_of = one(*shards[0])
    for cut in shards[1:]:
        factor_of = factor_of * one(*cut)
    return factor_of


def scatter_about(key, dims, scale, limit, pieces=(), kind=jnp.bfloat16):
    values = jax.random.normal(key, dims, jnp.float32) * scale
    if len(pieces) > 0:
        values = block_levels(key, dims, pieces, -0.22, 0.18) * values
    return jnp.clip(values, min=-limit, max=limit).astype(kind)


def setup_inputs(seed: int = 0) -> dict:
    keys = jax.random.split(jax.random.key(seed), 16)
    stored = draw_stored(jax.random.fold_in(keys[15], 71), 0)
    positions = draw_positions(jax.random.fold_in(keys[15], 71), 0)
    segments = draw_segments(jax.random.fold_in(keys[15], 71), 0)
    present = draw_present(jax.random.fold_in(keys[15], 71), 0)
    norm_gains = jnp.clip(1.0 + 0.18 * jax.random.normal(keys[4], (2, D), jnp.float32), 0.1, 1.9)
    norm_biases = scatter_about(keys[5], (2, D), 0.5, 3.0, ((1, 4),), jnp.float32)
    input_proj = scatter_about(keys[6], (D, 3, D), (D // 2) ** -0.5, 0.3125, ((0, 4), (2, 4)))
    input_bias = scatter_about(keys[7], (2, D), 0.5, 3.0, ((1, 4),))
    output_proj = scatter_about(keys[8], (D, D), (D // 16) ** -0.5, 0.875, ((0, 4), (1, 4)))
    output_bias = scatter_about(keys[9], (D,), 0.5, 3.0, ((0, 4),))
    expand_weight = scatter_about(keys[10], (D, FF), D ** -0.5, 0.21875, ((0, 4), (1, 4)))
    expand_bias = scatter_about(keys[11], (FF,), 0.5, 3.0, ((0, 4),))
    reduce_weight = scatter_about(keys[12], (D, FF), FF ** -0.5, 0.109375, ((0, 4), (1, 4)))
    reduce_bias = scatter_about(keys[13], (D,), 0.5, 3.0, ((0, 4),))
    cotangent = scatter_about(keys[14], (D, TOKENS), 1.0, 6.0, ((0, 4), (1, 8)))
    return {"stored": stored, "positions": positions, "segments": segments, "present": present, "norm_gains": norm_gains, "norm_biases": norm_biases, "input_proj": input_proj, "input_bias": input_bias, "output_proj": output_proj, "output_bias": output_bias, "expand_weight": expand_weight, "expand_bias": expand_bias, "reduce_weight": reduce_weight, "reduce_bias": reduce_bias, "cotangent": cotangent}


@jax.custom_vjp
def low(v):
    return lax.optimization_barrier(v.astype(jnp.bfloat16)).astype(jnp.float32)

@jax.custom_vjp
def low_back(v):
    return v

def low_keep(v):
    return (low(v), None)

def low_pass(kept, grad):
    return (grad,)

def back_keep(v):
    return (v, None)

def back_low(kept, grad):
    return (low(grad),)
low.defvjp(low_keep, low_pass)
low_back.defvjp(back_keep, back_low)
norm_eps = 1e-06
masked_score = -1e+30
top_precision = lax.Precision.HIGHEST

def layer_norm(values, gain_row, shift_row):
    average = lax.optimization_barrier(jnp.mean(values, axis=-1, keepdims=True))
    spread = lax.optimization_barrier(jnp.mean(values * values, axis=-1, keepdims=True)) - average * average
    normed = (values - average) * lax.rsqrt(spread + norm_eps)
    return normed * gain_row + shift_row

def position_table(positions):
    columns = jnp.arange(D, dtype=jnp.int32)
    half_width = D // 2
    freq_rates = jnp.exp((columns % half_width).astype(jnp.float32) * (-math.log(10000.0) / half_width))
    angles = positions.astype(jnp.float32)[:, None] * freq_rates[None, :]
    return jnp.where(columns[None, :] < half_width, jnp.sin(angles), jnp.cos(angles))

def attend_row(packed):
    row_data, seg_row, present_row = packed
    head_grid = row_data.reshape(SEQ, 3, HEADS, HD)
    scores = jnp.einsum('qhd,khd->hqk', head_grid[:, 0], head_grid[:, 1], precision=top_precision) * HD ** (-0.5)
    scores = low_back(scores)
    places = jnp.arange(SEQ, dtype=jnp.int32)
    same_clip = (seg_row[:, None] == seg_row[None, :]) & (present_row[None, :] == 1)
    allowed = same_clip | (places[:, None] == places[None, :])
    scores = jnp.where(allowed[None], scores, masked_score)
    row_max = lax.optimization_barrier(jnp.max(scores, axis=2, keepdims=True))
    weights = jnp.exp(scores - row_max)
    weights_low = low(weights / lax.optimization_barrier(jnp.sum(weights, axis=2, keepdims=True)))
    block_out = jnp.einsum('hqk,khd->qhd', weights_low, head_grid[:, 2], precision=top_precision)
    return block_out.reshape(SEQ, HEADS * HD)

def layer_forward(stored_rows, gains, shifts, input_proj, input_bias, output_proj, output_bias, expand_weight, expand_bias, reduce_weight, reduce_bias, pos_table, seg_rows, present_rows):
    embedded = stored_rows + pos_table
    first = low(layer_norm(embedded, gains[0], shifts[0]))
    bias_rows = jnp.stack([input_bias[0], jnp.zeros_like(input_bias[0]), input_bias[1]])
    qkv = jnp.einsum('td,dkc->tkc', first, input_proj, precision=top_precision) + bias_rows
    qkv = low(low_back(qkv))
    row_total = stored_rows.shape[0] // SEQ
    attended = lax.map(jax.checkpoint(attend_row), (qkv.reshape(row_total, SEQ, 3 * D), seg_rows.reshape(row_total, SEQ), present_rows.reshape(row_total, SEQ)))
    attended = low(low_back(attended.reshape(row_total * SEQ, D)))
    branch = jnp.dot(attended, output_proj, precision=top_precision, preferred_element_type=jnp.float32) + output_bias
    middle = embedded + low_back(branch)
    second = low(layer_norm(middle, gains[1], shifts[1]))
    pre_act = low_back(jnp.dot(second, expand_weight, precision=top_precision, preferred_element_type=jnp.float32) + expand_bias)
    act_low = low(jax.nn.gelu(pre_act, approximate=False))
    mlp_out = jnp.dot(act_low, reduce_weight.T, precision=top_precision, preferred_element_type=jnp.float32) + reduce_bias
    return middle + low_back(mlp_out)

def reference(stored, positions, segments, present, norm_gains, norm_biases, input_proj, input_bias, output_proj, output_bias, expand_weight, expand_bias, reduce_weight, reduce_bias, cotangent):
    row_total = TOKENS // SEQ
    group_rows = math.gcd(row_total, max(1, 4096 // SEQ))
    group_count = row_total // group_rows
    group_span = group_rows * SEQ
    params = tuple((item.astype(jnp.float32) for item in (norm_gains, norm_biases, input_proj, input_bias, output_proj, output_bias, expand_weight, expand_bias, reduce_weight, reduce_bias)))

    def by_group(array):
        return array.reshape((group_count, group_span) + array.shape[1:])

    def one_group(totals, packed):
        rows_in, pos_in, seg_in, present_in, cot_in = packed
        pos_table = position_table(pos_in)

        def layer_fn(rows_f, *weights):
            return layer_forward(rows_f, *weights, pos_table, seg_in, present_in)
        result, pull_back = jax.vjp(layer_fn, rows_in.astype(jnp.float32), *params)
        grads = pull_back(cot_in.astype(jnp.float32))
        totals = tuple((total_grad + new_grad for total_grad, new_grad in zip(totals, grads[1:])))
        return (totals, (result.astype(jnp.bfloat16), grads[0]))
    zero_grads = tuple((jnp.zeros(item.shape, jnp.float32) for item in params))
    totals, (results, row_grads) = lax.scan(one_group, zero_grads, (by_group(stored.T), by_group(positions), by_group(segments), by_group(present), by_group(cotangent.T)))
    return (results.reshape(TOKENS, D).T, row_grads.reshape(TOKENS, D).T, totals[0], totals[1], totals[2], totals[3], totals[4], totals[5], totals[6], totals[7], totals[8], totals[9])
```

```python
import functools
import math

import jax
import jax.numpy as jnp
from jax import lax
from jax.experimental import pallas as pl
from jax.experimental.pallas import tpu as pltpu
from jax.sharding import PartitionSpec as P

D = 768
HEADS = 12
HD = 64
SEQ = 1024
FB = 256
QB = 256
PAIR = 2 * HD
PAIRS = HEADS // 2
EPS = 1e-06
MASKED = -1e30
F32 = jnp.float32
BF16 = jnp.bfloat16
VMEM_LIMIT = 60 * 1024 * 1024

NN = (((1,), (0,)), ((), ()))
NT = (((1,), (1,)), ((), ()))


def mm(a, b, dims=NN):
    return lax.dot_general(a, b, dims, preferred_element_type=F32)


def whole(shape):
    return pl.BlockSpec(shape, lambda *_: (0,) * len(shape), pipeline_mode=pl.Buffered(1))


def params(**kw):
    return pltpu.CompilerParams(vmem_limit_bytes=VMEM_LIMIT, **kw)


def lane_sums(x):
    total = x[:, 0:128]
    for j in range(1, x.shape[1] // 128):
        total = total + x[:, j * 128 : (j + 1) * 128]
    return total


def norm_stats(e):
    average = jnp.sum(e, axis=0, keepdims=True) * (1.0 / D)
    spread = jnp.sum(e * e, axis=0, keepdims=True) * (1.0 / D) - average * average
    return average, lax.rsqrt(spread + EPS)


def project_kernel(x_ref, tab_ref, g_ref, b_ref, w_ref, wb_ref, et_ref, ft_ref, qkv_ref, f_ref):
    def norm_cols(j, _):
        cols = pl.ds(pl.multiple_of(j * 256, 256), 256)
        e = x_ref[:, cols].astype(F32) + tab_ref[:, cols]
        et_ref[:, cols] = e
        average, inv = norm_stats(e)
        f = ((e - average) * inv * g_ref[...] + b_ref[...]).astype(BF16)
        ft_ref[:, cols] = f
        f_ref[cols, :] = f.T
        return 0

    lax.fori_loop(0, SEQ // 256, norm_cols, 0)

    def cols_of(n, scale):
        cols = pl.ds(pl.multiple_of(n * 256, 256), 256)
        y = (mm(f_ref[...], w_ref[:, cols]) + wb_ref[:, cols]).astype(BF16)
        qkv_ref[:, cols] = y * jnp.asarray(scale, BF16)
        return 0

    lax.fori_loop(0, D // 256, lambda n, c: cols_of(n, HD**-0.5), 0)
    lax.fori_loop(D // 256, 3 * D // 256, lambda n, c: cols_of(n, 1.0), 0)


def project(xt, table, gain, shift, w1, bias_row):
    return pl.pallas_call(
        project_kernel,
        out_shape=(
            jax.ShapeDtypeStruct((D, SEQ), F32),
            jax.ShapeDtypeStruct((D, SEQ), BF16),
            jax.ShapeDtypeStruct((SEQ, 3 * D), BF16),
        ),
        scratch_shapes=[pltpu.VMEM((SEQ, D), BF16)],
        compiler_params=params(),
        name="project",
    )(xt, table, gain, shift, w1, bias_row)


def fill_bias(bias_ref, key_ref, seg_ref):
    def rows_of(i, _):
        rows = pl.ds(pl.multiple_of(i * 256, 256), 256)
        same = key_ref[rows, :] == seg_ref[...]
        row_id = lax.broadcasted_iota(jnp.int32, (256, SEQ), 0) + i * 256
        col_id = lax.broadcasted_iota(jnp.int32, (256, SEQ), 1)
        bias_ref[rows, :] = jnp.where(same | (row_id == col_id), 0.0, MASKED)
        return 0

    lax.fori_loop(0, SEQ // 256, rows_of, 0)


def attend_kernel(q_ref, k_ref, v_ref, key_ref, seg_ref, at_ref, lse_ref, bias_ref, vt_ref):
    @pl.when(pl.program_id(0) == 0)
    def _():
        fill_bias(bias_ref, key_ref, seg_ref)

    vt_ref[...] = v_ref[...].T
    low = lax.broadcasted_iota(jnp.int32, (QB, PAIR), 1) < HD
    lse_ref[...] = jnp.zeros_like(lse_ref)

    def block(j, _):
        cols = pl.ds(pl.multiple_of(j * QB, QB), QB)
        q = q_ref[cols, :]
        for hh in range(2):
            qm = jnp.where(low if hh == 0 else ~low, q, jnp.zeros_like(q))
            s = mm(k_ref[...], qm, NT) + bias_ref[:, cols]
            top = jnp.max(s, axis=0, keepdims=True)
            p = jnp.exp(s - top)
            total = jnp.sum(p, axis=0, keepdims=True)
            o = mm(vt_ref[hh * HD : (hh + 1) * HD, :], p.astype(BF16)) / total
            at_ref[hh * HD : (hh + 1) * HD, cols] = o.astype(BF16)
            lse_ref[0, hh : hh + 1, cols] = top + jnp.log(total)
        return 0

    lax.fori_loop(0, SEQ // QB, block, 0)


def attend(qkv, key_col, seg_row):
    part = lambda k: pl.BlockSpec((SEQ, PAIR), lambda p: (0, k * PAIRS + p))
    return pl.pallas_call(
        attend_kernel,
        grid=(PAIRS,),
        in_specs=[part(0), part(1), part(2), whole((SEQ, 1)), whole((1, SEQ))],
        out_specs=(
            pl.BlockSpec((PAIR, SEQ), lambda p: (p, 0)),
            pl.BlockSpec((1, 8, SEQ), lambda p: (p, 0, 0)),
        ),
        out_shape=(
            jax.ShapeDtypeStruct((D, SEQ), BF16),
            jax.ShapeDtypeStruct((PAIRS, 8, SEQ), F32),
        ),
        scratch_shapes=[pltpu.VMEM((SEQ, SEQ), F32), pltpu.VMEM((PAIR, SEQ), BF16)],
        compiler_params=params(),
        name="attend",
    )(qkv, qkv, qkv, key_col, seg_row)


def feed_kernel(
    at_ref, et_ref, ct_ref, w2_ref, b2_ref, g_ref, b_ref, we_ref, be_ref, wr_ref, br_ref,
    out_ref, dmid_ref, do_ref, dwr_ref, dwe_ref, dbe_ref, dw2_ref, db_ref, dg_ref,
    s_ref, st_ref, c_ref, ot_ref, ds_ref, mid_ref, bt_ref,
):
    step = pl.program_id(0)

    @pl.when(step == 0)
    def _():
        w2t = w2_ref[...].T

        def cols_of(j, _):
            cols = pl.ds(pl.multiple_of(j * 256, 256), 256)
            mid = et_ref[:, cols] + (mm(w2t, at_ref[:, cols]) + b2_ref[...])
            mid_ref[:, cols] = mid
            average, inv = norm_stats(mid)
            s = ((mid - average) * inv * g_ref[...] + b_ref[...]).astype(BF16)
            st_ref[:, cols] = s
            s_ref[cols, :] = s.T
            c_ref[cols, :] = ct_ref[:, cols].T
            return 0

        lax.fori_loop(0, SEQ // 256, cols_of, 0)

    pre = mm(s_ref[...], we_ref[...]) + be_ref[...]
    cdf = 0.5 * (1.0 + lax.erf(pre * (1.0 / math.sqrt(2.0))))
    act = (pre * cdf).astype(BF16)
    slope = cdf + pre * jnp.exp(-0.5 * pre * pre) * (1.0 / math.sqrt(2.0 * math.pi))
    grad = (mm(c_ref[...], wr_ref[...]) * slope).astype(BF16)
    dwr_ref[...] = mm(ct_ref[...], act).astype(BF16)
    dwe_ref[...] = mm(st_ref[...], grad).astype(BF16)
    dbe_ref[...] = jnp.sum(grad.astype(F32), axis=0, keepdims=True)
    o = mm(wr_ref[...], act, NT)
    ds = mm(we_ref[...], grad, NT)

    @pl.when(step == 0)
    def _():
        ot_ref[...] = o
        ds_ref[...] = ds

    @pl.when(step > 0)
    def _():
        ot_ref[...] += o
        ds_ref[...] += ds

    @pl.when(step == pl.num_programs(0) - 1)
    def _():
        dg_ref[...] = jnp.zeros_like(dg_ref)

        def cols_of(j, _):
            cols = pl.ds(pl.multiple_of(j * 256, 256), 256)
            mid = mid_ref[:, cols]
            out_ref[:, cols] = (mid + (ot_ref[:, cols] + br_ref[...])).astype(BF16)
            average, inv = norm_stats(mid)
            normed = (mid - average) * inv
            ds = ds_ref[:, cols]
            scaled = ds * g_ref[...]
            total = jnp.sum(scaled, axis=0, keepdims=True) * (1.0 / D)
            crossed = jnp.sum(scaled * normed, axis=0, keepdims=True) * (1.0 / D)
            dmid = ct_ref[:, cols].astype(F32) + inv * (scaled - total - normed * crossed)
            dmid_ref[:, cols] = dmid
            low = dmid.astype(BF16)
            bt_ref[:, cols] = low
            do_ref[cols, :] = mm(w2_ref[...], low).astype(BF16).T
            dg_ref[0] += lane_sums(ds * normed)
            dg_ref[1] += lane_sums(ds)
            return 0

        lax.fori_loop(0, SEQ // 256, cols_of, 0)
        ones = jnp.ones((8, SEQ), BF16)
        db_ref[0] = mm(ones, ct_ref[...], NT)
        db_ref[1] = mm(ones, bt_ref[...], NT)

        def rows_of(j, _):
            rows = pl.ds(pl.multiple_of(j * 256, 256), 256)
            dw2_ref[rows, :] = mm(at_ref[rows, :], bt_ref[...], NT).astype(BF16)
            return 0

        lax.fori_loop(0, D // 256, rows_of, 0)


def feed(at, et, ct, w2, b2, gain, shift, we, be, wr, br):
    ff = we.shape[1]
    cols = pl.BlockSpec((D, FB), lambda f: (0, f))
    row = pl.BlockSpec((1, FB), lambda f: (0, f))
    sds = jax.ShapeDtypeStruct
    return pl.pallas_call(
        feed_kernel,
        grid=(ff // FB,),
        in_specs=[
            whole((D, SEQ)), whole((D, SEQ)), whole((D, SEQ)), whole((D, D)), whole((D, 1)), whole((D, 1)),
            whole((D, 1)), cols, row, cols, whole((D, 1)),
        ],
        out_specs=(
            whole((D, SEQ)), whole((D, SEQ)), whole((SEQ, D)), cols, cols, row, whole((D, D)),
            whole((2, 8, D)), whole((2, D, 128)),
        ),
        out_shape=(
            sds((D, SEQ), BF16), sds((D, SEQ), F32), sds((SEQ, D), BF16), sds((D, ff), BF16), sds((D, ff), BF16),
            sds((1, ff), F32), sds((D, D), BF16), sds((2, 8, D), F32), sds((2, D, 128), F32),
        ),
        scratch_shapes=[
            pltpu.VMEM((SEQ, D), BF16), pltpu.VMEM((D, SEQ), BF16), pltpu.VMEM((SEQ, D), BF16),
            pltpu.VMEM((D, SEQ), F32), pltpu.VMEM((D, SEQ), F32), pltpu.VMEM((D, SEQ), F32),
            pltpu.VMEM((D, SEQ), BF16),
        ],
        compiler_params=params(),
        name="feed",
    )(at, et, ct, w2, b2, gain, shift, we, be, wr, br)


def attend_back_kernel(
    q_ref, k_ref, v_ref, do_ref, lse_ref, key_ref, seg_ref, dqt_ref, dk_ref, dv_ref, bias_ref, kt_ref, dka_ref, dva_ref
):
    @pl.when(pl.program_id(0) == 0)
    def _():
        fill_bias(bias_ref, key_ref, seg_ref)

    kt_ref[...] = k_ref[...].T
    low = lax.broadcasted_iota(jnp.int32, (QB, PAIR), 1) < HD
    dka_ref[...] = jnp.zeros_like(dka_ref)
    dva_ref[...] = jnp.zeros_like(dva_ref)

    def block(j, _):
        cols = pl.ds(pl.multiple_of(j * QB, QB), QB)
        q = q_ref[cols, :]
        do = do_ref[cols, :]
        for hh in range(2):
            keep = low if hh == 0 else ~low
            qm = jnp.where(keep, q, jnp.zeros_like(q))
            dom = jnp.where(keep, do, jnp.zeros_like(do))
            p = jnp.exp(mm(k_ref[...], qm, NT) + bias_ref[:, cols] - lse_ref[0, hh : hh + 1, cols])
            t = p * mm(v_ref[...], dom, NT)
            ds = (t - p * jnp.sum(t, axis=0, keepdims=True)).astype(BF16)
            dva_ref[...] += mm(p.astype(BF16), dom)
            dka_ref[...] += mm(ds, qm)
            dq = mm(kt_ref[hh * HD : (hh + 1) * HD, :], ds) * HD**-0.5
            dqt_ref[hh * HD : (hh + 1) * HD, cols] = dq.astype(BF16)
        return 0

    lax.fori_loop(0, SEQ // QB, block, 0)
    dk_ref[...] = dka_ref[...].astype(BF16)
    dv_ref[...] = dva_ref[...].astype(BF16)


def attend_back(qkv, do, lse, key_col, seg_row):
    part = lambda k: pl.BlockSpec((SEQ, PAIR), lambda p: (0, k * PAIRS + p))
    return pl.pallas_call(
        attend_back_kernel,
        grid=(PAIRS,),
        in_specs=[
            part(0), part(1), part(2), part(0), pl.BlockSpec((1, 8, SEQ), lambda p: (p, 0, 0)),
            whole((SEQ, 1)), whole((1, SEQ)),
        ],
        out_specs=(pl.BlockSpec((PAIR, SEQ), lambda p: (p, 0)), part(0), part(0)),
        out_shape=(
            jax.ShapeDtypeStruct((D, SEQ), BF16),
            jax.ShapeDtypeStruct((SEQ, D), BF16),
            jax.ShapeDtypeStruct((SEQ, D), BF16),
        ),
        scratch_shapes=[
            pltpu.VMEM((SEQ, SEQ), F32), pltpu.VMEM((PAIR, SEQ), BF16),
            pltpu.VMEM((SEQ, PAIR), F32), pltpu.VMEM((SEQ, PAIR), F32),
        ],
        compiler_params=params(),
        name="attend_back",
    )(qkv, qkv, qkv, do, lse, key_col, seg_row)


def project_back_kernel(
    ft_ref, dqt_ref, dk_ref, dv_ref, w_ref, et_ref, dmid_ref, g_ref,
    dw_ref, dx_ref, db_ref, dg_ref, df_ref,
):
    df_ref[...] = jnp.zeros_like(df_ref)

    def cols_of(n, _):
        off = pl.multiple_of(n * 256, 256)
        cols = pl.ds(off, 256)
        dq = dqt_ref[cols, :]
        dk = dk_ref[:, cols]
        dv = dv_ref[:, cols]
        dw_ref[:, cols] = mm(ft_ref[...], dq, NT).astype(BF16)
        dw_ref[:, pl.ds(pl.multiple_of(off + D, 256), 256)] = mm(ft_ref[...], dk).astype(BF16)
        dw_ref[:, pl.ds(pl.multiple_of(off + 2 * D, 256), 256)] = mm(ft_ref[...], dv).astype(BF16)
        df_ref[...] += mm(w_ref[:, cols], dq)
        df_ref[...] += mm(w_ref[:, pl.ds(pl.multiple_of(off + D, 256), 256)], dk, NT)
        df_ref[...] += mm(w_ref[:, pl.ds(pl.multiple_of(off + 2 * D, 256), 256)], dv, NT)
        return 0

    lax.fori_loop(0, D // 256, cols_of, 0)
    ones = jnp.ones((8, SEQ), BF16)
    db_ref[0] = mm(ones, dqt_ref[...], NT)
    db_ref[1] = mm(ones, dv_ref[...])
    dg_ref[...] = jnp.zeros_like(dg_ref)

    def norm_cols(j, _):
        cols = pl.ds(pl.multiple_of(j * 256, 256), 256)
        e = et_ref[:, cols]
        average, inv = norm_stats(e)
        normed = (e - average) * inv
        df = df_ref[:, cols]
        scaled = df * g_ref[...]
        total = jnp.sum(scaled, axis=0, keepdims=True) * (1.0 / D)
        crossed = jnp.sum(scaled * normed, axis=0, keepdims=True) * (1.0 / D)
        dx_ref[:, cols] = (dmid_ref[:, cols] + inv * (scaled - total - normed * crossed)).astype(BF16)
        dg_ref[0] += lane_sums(df * normed)
        dg_ref[1] += lane_sums(df)
        return 0

    lax.fori_loop(0, SEQ // 256, norm_cols, 0)


def project_back(ft, dqt, dk, dv, w1, et, dmid, gain):
    sds = jax.ShapeDtypeStruct
    return pl.pallas_call(
        project_back_kernel,
        out_shape=(sds((D, 3 * D), BF16), sds((D, SEQ), BF16), sds((2, 8, D), F32), sds((2, D, 128), F32)),
        scratch_shapes=[pltpu.VMEM((D, SEQ), F32)],
        compiler_params=params(),
        name="project_back",
    )(ft, dqt, dk, dv, w1, et, dmid, gain)


def position_table(positions):
    rows = jnp.arange(D, dtype=jnp.int32)
    half = D // 2
    rates = jnp.exp((rows % half).astype(F32) * (-math.log(10000.0) / half))
    angles = rates[:, None] * positions.astype(F32)[None, :]
    return jnp.where(rows[:, None] < half, jnp.sin(angles), jnp.cos(angles))


GATHER = ("hidden", "mp", "dp")


def local(
    stored, positions, segments, present, norm_gains, norm_biases, input_proj, input_bias, output_proj,
    output_bias, expand_weight, expand_bias, reduce_weight, reduce_bias, cotangent,
):
    mp, hid, dp = lax.axis_size("mp"), lax.axis_size("hidden"), lax.axis_size("dp")
    m = lax.axis_index("mp")
    d = lax.axis_index("dp")
    rows_mp = D // mp
    half = rows_mp // dp
    cut = lambda w: lax.dynamic_slice_in_dim(w, d * half, half, 0)
    hcols = D // hid
    w1 = cut(input_proj).reshape(-1)
    we = cut(expand_weight).reshape(-1)
    wr = cut(reduce_weight).reshape(-1)
    w2 = lax.dynamic_slice_in_dim(output_proj, d * (hcols // dp), hcols // dp, 0).reshape(-1)
    sizes = [w1.size, w2.size, we.size, wr.size]
    flat = jnp.concatenate([w1, w2, we, wr]).reshape(-1, D)
    full = lax.all_gather(flat, GATHER, axis=0, tiled=True).reshape(hid, mp, dp, -1)
    o0, o1, o2 = sizes[0], sizes[0] + sizes[1], sizes[0] + sizes[1] + sizes[2]
    w1f = full[..., :o0].reshape(hid, D, 3, hcols).transpose(1, 2, 0, 3).reshape(D, 3 * D)
    w2f = full[..., o0:o1].reshape(hid, mp, dp, hcols // dp, rows_mp).transpose(0, 2, 3, 1, 4).reshape(D, D)
    fcols = expand_weight.shape[1]
    wef = full[..., o1:o2].reshape(hid, D, fcols).transpose(1, 0, 2).reshape(D, -1)
    wrf = full[..., o2:].reshape(hid, D, fcols).transpose(1, 0, 2).reshape(D, -1)
    gains, shifts = (lax.all_gather(t, "mp", axis=1, tiled=True) for t in (norm_gains, norm_biases))
    b2, br = (lax.all_gather(t, "mp", axis=0, tiled=True).astype(F32)[:, None] for t in (output_bias, reduce_bias))
    b1 = lax.all_gather(input_bias, "hidden", axis=1, tiled=True).astype(F32)
    be = lax.all_gather(expand_bias, "hidden", axis=0, tiled=True).astype(F32)[None]
    bias_row = jnp.concatenate([b1[0], jnp.zeros_like(b1[0]), b1[1]])[None]
    xt = lax.all_to_all(stored, "mp", split_axis=1, concat_axis=0, tiled=True)
    ct = lax.all_to_all(cotangent, "mp", split_axis=1, concat_axis=0, tiled=True)
    table = position_table(lax.dynamic_slice_in_dim(positions, m * SEQ, SEQ))
    key_col = jnp.where(present == 1, segments, -1)[:, None]
    seg_row = segments[None, :]

    et, ft, qkv = project(xt, table, gains[0][:, None], shifts[0][:, None], w1f, bias_row)
    at, lse = attend(qkv, key_col, seg_row)
    out_t, dmid, do, dwr, dwe, dbe, dw2, db_feed, dg_second = feed(
        at, et, ct, w2f, b2, gains[1][:, None], shifts[1][:, None], wef, be, wrf, br
    )
    dqt, dk, dv = attend_back(qkv, do, lse, key_col, seg_row)
    dw1, dx, db_proj, dg_first = project_back(ft, dqt, dk, dv, w1f, et, dmid, gains[0][:, None])

    output = lax.all_to_all(out_t, "mp", split_axis=0, concat_axis=1, tiled=True)
    d_stored = lax.all_to_all(dx, "mp", split_axis=0, concat_axis=1, tiled=True).astype(F32)

    n_parts = hid * mp * dp
    p1 = dw1.reshape(D, 3, hid, hcols).transpose(2, 0, 1, 3).reshape(n_parts, -1)
    p2 = dw2.reshape(hid, dp, hcols // dp, mp, rows_mp).transpose(0, 3, 1, 2, 4).reshape(n_parts, -1)
    pe = dwe.reshape(D, hid, fcols).transpose(1, 0, 2).reshape(n_parts, -1)
    pr = dwr.reshape(D, hid, fcols).transpose(1, 0, 2).reshape(n_parts, -1)
    packed = jnp.concatenate([p1, p2, pe, pr], axis=1).reshape(-1, D)
    mine = lax.psum_scatter(packed, GATHER, scatter_dimension=0, tiled=True).reshape(-1).astype(F32)
    d_input = mine[:o0].reshape(half, 3, hcols)
    d_output = mine[o0:o1].reshape(hcols // dp, rows_mp)
    d_expand = mine[o1:o2].reshape(half, fcols)
    d_reduce = mine[o2:].reshape(half, fcols)
    dg = jnp.stack([jnp.sum(dg_first, axis=2), jnp.sum(dg_second, axis=2)])
    vectors = jnp.concatenate(
        [dg.reshape(-1), db_proj[:, 0].reshape(-1), db_feed[:, 0].reshape(-1), dbe.reshape(-1)]
    )
    vectors = lax.psum(vectors, ("dp", "mp", "hidden"))
    h = lax.axis_index("hidden")
    dg = vectors[: 4 * D].reshape(2, 2, D)
    piece = D // n_parts
    dg = lax.dynamic_slice_in_dim(dg, ((m * dp + d) * hid + h) * piece, piece, 2)
    db_proj = vectors[4 * D : 6 * D].reshape(2, D)
    db_proj = lax.dynamic_slice_in_dim(db_proj, (h * dp + d) * (hcols // dp), hcols // dp, 1)
    db_feed = lax.dynamic_slice_in_dim(vectors[6 * D : 8 * D].reshape(2, D), (m * dp + d) * half, half, 1)
    dbe = lax.dynamic_slice_in_dim(vectors[8 * D :], (h * dp + d) * (fcols // dp), fcols // dp)
    return (
        output, d_stored, dg[:, 0], dg[:, 1], d_input, db_proj, d_output, db_feed[1], d_expand, dbe, d_reduce,
        db_feed[0],
    )


def solution(mesh):
    placed = (
        P("mp", ("dp", "hidden")),
        P(("dp", "hidden")),
        P(("dp", "hidden", "mp")),
        P(("dp", "hidden", "mp")),
        P(None, "mp"),
        P(None, "mp"),
        P("mp", None, "hidden"),
        P(None, "hidden"),
        P("hidden", "mp"),
        P("mp"),
        P("mp", "hidden"),
        P("hidden"),
        P("mp", "hidden"),
        P("mp"),
        P("mp", ("dp", "hidden")),
    )
    return jax.shard_map(
        local,
        mesh=mesh,
        in_specs=placed,
        out_specs=(
            P("mp", ("dp", "hidden")),
            P("mp", ("dp", "hidden")),
            P(None, ("mp", "dp", "hidden")),
            P(None, ("mp", "dp", "hidden")),
            P(("mp", "dp"), None, "hidden"),
            P(None, ("hidden", "dp")),
            P(("hidden", "dp"), "mp"),
            P(("mp", "dp")),
            P(("mp", "dp"), "hidden"),
            P(("hidden", "dp")),
            P(("mp", "dp"), "hidden"),
            P(("mp", "dp")),
        ),
        check_vma=False,
    )
```

```python
import functools
import math

import jax
import jax.numpy as jnp
from jax import lax
from jax.experimental import pallas as pl
from jax.experimental.pallas import tpu as pltpu
from jax.sharding import PartitionSpec as P

D = 768
HEADS = 12
HD = 64
SEQ = 1024
FB = 256
QB = 256
PAIR = 2 * HD
PAIRS = HEADS // 2
EPS = 1e-06
MASKED = -1e30
F32 = jnp.float32
BF16 = jnp.bfloat16
VMEM_LIMIT = 60 * 1024 * 1024

NN = (((1,), (0,)), ((), ()))
NT = (((1,), (1,)), ((), ()))


def mm(a, b, dims=NN):
    return lax.dot_general(a, b, dims, preferred_element_type=F32)


def whole(shape):
    return pl.BlockSpec(shape, lambda *_: (0,) * len(shape), pipeline_mode=pl.Buffered(1))


def params(**kw):
    return pltpu.CompilerParams(vmem_limit_bytes=VMEM_LIMIT, **kw)


def lane_sums(x):
    total = x[:, 0:128]
    for j in range(1, x.shape[1] // 128):
        total = total + x[:, j * 128 : (j + 1) * 128]
    return total


def norm_stats(e):
    average = jnp.sum(e, axis=0, keepdims=True) * (1.0 / D)
    spread = jnp.sum(e * e, axis=0, keepdims=True) * (1.0 / D) - average * average
    return average, lax.rsqrt(spread + EPS)


def project_kernel(x_ref, tab_ref, p_ref, wn_ref, wb_ref, et_ref, ft_ref, qkv_ref, w_ref, f_ref):
    hid = wn_ref.shape[0]
    wide = D // hid
    for hh in range(hid):
        for k in range(3):
            w_ref[:, k * D + hh * wide : k * D + (hh + 1) * wide] = wn_ref[hh, :, k * wide : (k + 1) * wide]

    def norm_cols(j, _):
        cols = pl.ds(pl.multiple_of(j * 256, 256), 256)
        e = x_ref[:, cols].astype(F32) + tab_ref[:, cols]
        et_ref[:, cols] = e
        average, inv = norm_stats(e)
        f = ((e - average) * inv * p_ref[:, 0:1] + p_ref[:, 1:2]).astype(BF16)
        ft_ref[:, cols] = f
        f_ref[cols, :] = f.T
        return 0

    lax.fori_loop(0, SEQ // 256, norm_cols, 0)

    def cols_of(n, scale):
        cols = pl.ds(pl.multiple_of(n * 256, 256), 256)
        y = (mm(f_ref[...], w_ref[:, cols]) + wb_ref[:, cols]).astype(BF16)
        qkv_ref[:, cols] = y * jnp.asarray(scale, BF16)
        return 0

    lax.fori_loop(0, D // 256, lambda n, c: cols_of(n, HD**-0.5), 0)
    lax.fori_loop(D // 256, 3 * D // 256, lambda n, c: cols_of(n, 1.0), 0)


def project(xt, table, cols, w1, bias_row):
    return pl.pallas_call(
        project_kernel,
        out_shape=(
            jax.ShapeDtypeStruct((D, SEQ), F32),
            jax.ShapeDtypeStruct((D, SEQ), BF16),
            jax.ShapeDtypeStruct((SEQ, 3 * D), BF16),
            jax.ShapeDtypeStruct((D, 3 * D), BF16),
        ),
        scratch_shapes=[pltpu.VMEM((SEQ, D), BF16)],
        compiler_params=params(),
        name="project",
    )(xt, table, cols, w1, bias_row)


def fill_bias(bias_ref, key_ref, seg_ref):
    def rows_of(i, _):
        rows = pl.ds(pl.multiple_of(i * 256, 256), 256)
        same = key_ref[rows, :] == seg_ref[...]
        row_id = lax.broadcasted_iota(jnp.int32, (256, SEQ), 0) + i * 256
        col_id = lax.broadcasted_iota(jnp.int32, (256, SEQ), 1)
        bias_ref[rows, :] = jnp.where(same | (row_id == col_id), 0.0, MASKED)
        return 0

    lax.fori_loop(0, SEQ // 256, rows_of, 0)


def attend_kernel(q_ref, k_ref, v_ref, key_ref, seg_ref, at_ref, lse_ref, bias_ref, vt_ref):
    @pl.when(pl.program_id(0) == 0)
    def _():
        fill_bias(bias_ref, key_ref, seg_ref)

    vt_ref[...] = v_ref[...].T
    low = lax.broadcasted_iota(jnp.int32, (QB, PAIR), 1) < HD
    lse_ref[...] = jnp.zeros_like(lse_ref)

    def block(j, _):
        cols = pl.ds(pl.multiple_of(j * QB, QB), QB)
        q = q_ref[cols, :]
        for hh in range(2):
            qm = jnp.where(low if hh == 0 else ~low, q, jnp.zeros_like(q))
            s = mm(k_ref[...], qm, NT) + bias_ref[:, cols]
            top = jnp.max(s, axis=0, keepdims=True)
            p = jnp.exp(s - top)
            total = jnp.sum(p, axis=0, keepdims=True)
            o = mm(vt_ref[hh * HD : (hh + 1) * HD, :], p.astype(BF16)) / total
            at_ref[hh * HD : (hh + 1) * HD, cols] = o.astype(BF16)
            lse_ref[0, hh : hh + 1, cols] = top + jnp.log(total)
        return 0

    lax.fori_loop(0, SEQ // QB, block, 0)


def attend(qkv, key_col, seg_row):
    part = lambda k: pl.BlockSpec((SEQ, PAIR), lambda p: (0, k * PAIRS + p))
    return pl.pallas_call(
        attend_kernel,
        grid=(PAIRS,),
        in_specs=[part(0), part(1), part(2), whole((SEQ, 1)), whole((1, SEQ))],
        out_specs=(
            pl.BlockSpec((PAIR, SEQ), lambda p: (p, 0)),
            pl.BlockSpec((1, 8, SEQ), lambda p: (p, 0, 0)),
        ),
        out_shape=(
            jax.ShapeDtypeStruct((D, SEQ), BF16),
            jax.ShapeDtypeStruct((PAIRS, 8, SEQ), F32),
        ),
        scratch_shapes=[pltpu.VMEM((SEQ, SEQ), F32), pltpu.VMEM((PAIR, SEQ), BF16)],
        compiler_params=params(),
        name="attend",
    )(qkv, qkv, qkv, key_col, seg_row)


def feed_kernel(
    at_ref, et_ref, ct_ref, w2n_ref, p_ref, we_ref, be_ref, wr_ref,
    out_ref, dmid_ref, do_ref, dwr_ref, dwe_ref, dbe_ref, dw2_ref, db_ref, dg_ref,
    s_ref, st_ref, c_ref, ot_ref, ds_ref, mid_ref, bt_ref, w2_ref,
):
    step = pl.program_id(0)

    @pl.when(step == 0)
    def _():
        mp = w2n_ref.shape[0]
        wide = D // mp
        for j in range(mp):
            w2_ref[:, j * wide : (j + 1) * wide] = w2n_ref[j]
        w2t = w2_ref[...].T

        def cols_of(j, _):
            cols = pl.ds(pl.multiple_of(j * 256, 256), 256)
            mid = et_ref[:, cols] + (mm(w2t, at_ref[:, cols]) + p_ref[:, 4:5])
            mid_ref[:, cols] = mid
            average, inv = norm_stats(mid)
            s = ((mid - average) * inv * p_ref[:, 2:3] + p_ref[:, 3:4]).astype(BF16)
            st_ref[:, cols] = s
            s_ref[cols, :] = s.T
            c_ref[cols, :] = ct_ref[:, cols].T
            return 0

        lax.fori_loop(0, SEQ // 256, cols_of, 0)

    pre = mm(s_ref[...], we_ref[...]) + be_ref[...]
    cdf = 0.5 * (1.0 + lax.erf(pre * (1.0 / math.sqrt(2.0))))
    act = (pre * cdf).astype(BF16)
    slope = cdf + pre * jnp.exp(-0.5 * pre * pre) * (1.0 / math.sqrt(2.0 * math.pi))
    grad = (mm(c_ref[...], wr_ref[...]) * slope).astype(BF16)
    dwr_ref[...] = mm(ct_ref[...], act).astype(BF16)
    dwe_ref[...] = mm(st_ref[...], grad).astype(BF16)
    dbe_ref[...] = jnp.sum(grad.astype(F32), axis=0, keepdims=True)
    o = mm(wr_ref[...], act, NT)
    ds = mm(we_ref[...], grad, NT)

    @pl.when(step == 0)
    def _():
        ot_ref[...] = o
        ds_ref[...] = ds

    @pl.when(step > 0)
    def _():
        ot_ref[...] += o
        ds_ref[...] += ds

    @pl.when(step == pl.num_programs(0) - 1)
    def _():
        dg_ref[...] = jnp.zeros_like(dg_ref)

        def cols_of(j, _):
            cols = pl.ds(pl.multiple_of(j * 256, 256), 256)
            mid = mid_ref[:, cols]
            out_ref[:, cols] = (mid + (ot_ref[:, cols] + p_ref[:, 5:6])).astype(BF16)
            average, inv = norm_stats(mid)
            normed = (mid - average) * inv
            ds = ds_ref[:, cols]
            scaled = ds * p_ref[:, 2:3]
            total = jnp.sum(scaled, axis=0, keepdims=True) * (1.0 / D)
            crossed = jnp.sum(scaled * normed, axis=0, keepdims=True) * (1.0 / D)
            dmid = ct_ref[:, cols].astype(F32) + inv * (scaled - total - normed * crossed)
            dmid_ref[:, cols] = dmid
            low = dmid.astype(BF16)
            bt_ref[:, cols] = low
            do_ref[cols, :] = mm(w2_ref[...], low).astype(BF16).T
            dg_ref[0] += lane_sums(ds * normed)
            dg_ref[1] += lane_sums(ds)
            return 0

        lax.fori_loop(0, SEQ // 256, cols_of, 0)
        ones = jnp.ones((8, SEQ), BF16)
        db_ref[0] = mm(ones, ct_ref[...], NT)
        db_ref[1] = mm(ones, bt_ref[...], NT)

        wide = D // dw2_ref.shape[0]
        for j in range(dw2_ref.shape[0]):
            dw2_ref[j] = mm(at_ref[...], bt_ref[j * wide : (j + 1) * wide, :], NT).astype(BF16)


def feed(at, et, ct, w2, small, we, be, wr):
    ff = we.shape[1]
    cols = pl.BlockSpec((D, FB), lambda f: (0, f))
    row = pl.BlockSpec((1, FB), lambda f: (0, f))
    sds = jax.ShapeDtypeStruct
    return pl.pallas_call(
        feed_kernel,
        grid=(ff // FB,),
        in_specs=[
            whole((D, SEQ)), whole((D, SEQ)), whole((D, SEQ)), whole(w2.shape), whole((D, 128)), cols, row, cols,
        ],
        out_specs=(
            whole((D, SEQ)), whole((D, SEQ)), whole((SEQ, D)), cols, cols, row, whole(w2.shape),
            whole((2, 8, D)), whole((2, D, 128)),
        ),
        out_shape=(
            sds((D, SEQ), BF16), sds((D, SEQ), F32), sds((SEQ, D), BF16), sds((D, ff), BF16), sds((D, ff), BF16),
            sds((1, ff), F32), sds(w2.shape, BF16), sds((2, 8, D), F32), sds((2, D, 128), F32),
        ),
        scratch_shapes=[
            pltpu.VMEM((SEQ, D), BF16), pltpu.VMEM((D, SEQ), BF16), pltpu.VMEM((SEQ, D), BF16),
            pltpu.VMEM((D, SEQ), F32), pltpu.VMEM((D, SEQ), F32), pltpu.VMEM((D, SEQ), F32),
            pltpu.VMEM((D, SEQ), BF16), pltpu.VMEM((D, D), BF16),
        ],
        compiler_params=params(),
        name="feed",
    )(at, et, ct, w2, small, we, be, wr)


def attend_back_kernel(
    q_ref, k_ref, v_ref, do_ref, lse_ref, key_ref, seg_ref, dqt_ref, dk_ref, dv_ref, bias_ref, kt_ref, dka_ref, dva_ref
):
    @pl.when(pl.program_id(0) == 0)
    def _():
        fill_bias(bias_ref, key_ref, seg_ref)

    kt_ref[...] = k_ref[...].T
    low = lax.broadcasted_iota(jnp.int32, (QB, PAIR), 1) < HD
    dka_ref[...] = jnp.zeros_like(dka_ref)
    dva_ref[...] = jnp.zeros_like(dva_ref)

    def block(j, _):
        cols = pl.ds(pl.multiple_of(j * QB, QB), QB)
        q = q_ref[cols, :]
        do = do_ref[cols, :]
        for hh in range(2):
            keep = low if hh == 0 else ~low
            qm = jnp.where(keep, q, jnp.zeros_like(q))
            dom = jnp.where(keep, do, jnp.zeros_like(do))
            p = jnp.exp(mm(k_ref[...], qm, NT) + bias_ref[:, cols] - lse_ref[0, hh : hh + 1, cols])
            t = p * mm(v_ref[...], dom, NT)
            ds = (t - p * jnp.sum(t, axis=0, keepdims=True)).astype(BF16)
            dva_ref[...] += mm(p.astype(BF16), dom)
            dka_ref[...] += mm(ds, qm)
            dq = mm(kt_ref[hh * HD : (hh + 1) * HD, :], ds) * HD**-0.5
            dqt_ref[hh * HD : (hh + 1) * HD, cols] = dq.astype(BF16)
        return 0

    lax.fori_loop(0, SEQ // QB, block, 0)
    dk_ref[...] = dka_ref[...].astype(BF16)
    dv_ref[...] = dva_ref[...].astype(BF16)


def attend_back(qkv, do, lse, key_col, seg_row):
    part = lambda k: pl.BlockSpec((SEQ, PAIR), lambda p: (0, k * PAIRS + p))
    return pl.pallas_call(
        attend_back_kernel,
        grid=(PAIRS,),
        in_specs=[
            part(0), part(1), part(2), part(0), pl.BlockSpec((1, 8, SEQ), lambda p: (p, 0, 0)),
            whole((SEQ, 1)), whole((1, SEQ)),
        ],
        out_specs=(pl.BlockSpec((PAIR, SEQ), lambda p: (p, 0)), part(0), part(0)),
        out_shape=(
            jax.ShapeDtypeStruct((D, SEQ), BF16),
            jax.ShapeDtypeStruct((SEQ, D), BF16),
            jax.ShapeDtypeStruct((SEQ, D), BF16),
        ),
        scratch_shapes=[
            pltpu.VMEM((SEQ, SEQ), F32), pltpu.VMEM((PAIR, SEQ), BF16),
            pltpu.VMEM((SEQ, PAIR), F32), pltpu.VMEM((SEQ, PAIR), F32),
        ],
        compiler_params=params(),
        name="attend_back",
    )(qkv, qkv, qkv, do, lse, key_col, seg_row)


def project_back_kernel(
    ft_ref, dqt_ref, dk_ref, dv_ref, w_ref, et_ref, dmid_ref, p_ref,
    dwn_ref, dx_ref, db_ref, dg_ref, df_ref, dw_ref,
):
    df_ref[...] = jnp.zeros_like(df_ref)

    def cols_of(n, _):
        off = pl.multiple_of(n * 256, 256)
        cols = pl.ds(off, 256)
        dq = dqt_ref[cols, :]
        dk = dk_ref[:, cols]
        dv = dv_ref[:, cols]
        dw_ref[:, cols] = mm(ft_ref[...], dq, NT).astype(BF16)
        dw_ref[:, pl.ds(pl.multiple_of(off + D, 256), 256)] = mm(ft_ref[...], dk).astype(BF16)
        dw_ref[:, pl.ds(pl.multiple_of(off + 2 * D, 256), 256)] = mm(ft_ref[...], dv).astype(BF16)
        df_ref[...] += mm(w_ref[:, cols], dq)
        df_ref[...] += mm(w_ref[:, pl.ds(pl.multiple_of(off + D, 256), 256)], dk, NT)
        df_ref[...] += mm(w_ref[:, pl.ds(pl.multiple_of(off + 2 * D, 256), 256)], dv, NT)
        return 0

    lax.fori_loop(0, D // 256, cols_of, 0)
    hid = dwn_ref.shape[0]
    wide = D // hid
    for hh in range(hid):
        for k in range(3):
            dwn_ref[hh, :, k * wide : (k + 1) * wide] = dw_ref[:, k * D + hh * wide : k * D + (hh + 1) * wide]
    ones = jnp.ones((8, SEQ), BF16)
    db_ref[0] = mm(ones, dqt_ref[...], NT)
    db_ref[1] = mm(ones, dv_ref[...])
    dg_ref[...] = jnp.zeros_like(dg_ref)

    def norm_cols(j, _):
        cols = pl.ds(pl.multiple_of(j * 256, 256), 256)
        e = et_ref[:, cols]
        average, inv = norm_stats(e)
        normed = (e - average) * inv
        df = df_ref[:, cols]
        scaled = df * p_ref[:, 0:1]
        total = jnp.sum(scaled, axis=0, keepdims=True) * (1.0 / D)
        crossed = jnp.sum(scaled * normed, axis=0, keepdims=True) * (1.0 / D)
        dx_ref[:, cols] = (dmid_ref[:, cols] + inv * (scaled - total - normed * crossed)).astype(BF16)
        dg_ref[0] += lane_sums(df * normed)
        dg_ref[1] += lane_sums(df)
        return 0

    lax.fori_loop(0, SEQ // 256, norm_cols, 0)


def project_back(ft, dqt, dk, dv, w1, et, dmid, cols, hid):
    sds = jax.ShapeDtypeStruct
    return pl.pallas_call(
        project_back_kernel,
        out_shape=(
            sds((hid, D, 3 * D // hid), BF16), sds((D, SEQ), BF16), sds((2, 8, D), F32), sds((2, D, 128), F32)
        ),
        scratch_shapes=[pltpu.VMEM((D, SEQ), F32), pltpu.VMEM((D, 3 * D), BF16)],
        compiler_params=params(),
        name="project_back",
    )(ft, dqt, dk, dv, w1, et, dmid, cols)


def position_table(positions):
    rows = jnp.arange(D, dtype=jnp.int32)
    half = D // 2
    rates = jnp.exp((rows % half).astype(F32) * (-math.log(10000.0) / half))
    angles = rates[:, None] * positions.astype(F32)[None, :]
    return jnp.where(rows[:, None] < half, jnp.sin(angles), jnp.cos(angles))


MESH = pl.DeviceIdType.MESH


class Wire:
    def __init__(self, send, recv):
        self.send_sem, self.recv_sem, self.count, self.sent = send, recv, 0, []
        self.me = (lax.axis_index("dp"), lax.axis_index("mp"), lax.axis_index("hidden"))
        self.size = (lax.axis_size("dp"), lax.axis_size("mp"), lax.axis_size("hidden"))

    def peer(self, axis, offset):
        where = list(self.me)
        where[axis] = lax.rem(where[axis] + offset, self.size[axis])
        return tuple(where)

    def origin(self, axis, offset):
        return lax.rem(self.me[axis] - offset + self.size[axis], self.size[axis])

    def meet(self):
        barrier = pltpu.get_barrier_semaphore()
        total = 0
        for axis in range(3):
            for offset in range(1, self.size[axis]):
                pl.semaphore_signal(barrier, 1, device_id=self.peer(axis, offset), device_id_type=MESH)
                total += 1
        pl.semaphore_wait(barrier, total)

    def send(self, src, dst, target):
        copy = pltpu.make_async_remote_copy(
            src, dst, self.send_sem.at[self.count], self.recv_sem.at[self.count], device_id=target, device_id_type=MESH
        )
        copy.start()
        self.count += 1
        self.sent.append(copy)
        return copy

    def keep(self, src, dst):
        copy = pltpu.make_async_copy(src, dst, self.send_sem.at[self.count])
        copy.start()
        self.count += 1
        return copy

    def finish(self):
        for copy in self.sent:
            copy.wait_send()


DP, MP, HID = 0, 1, 2


def gather_kernel(
    n_sems, x_ref, c_ref, w1_ref, w2_ref, we_ref, wr_ref, cols_ref, rows_ref,
    xt_ref, ct_ref, w1f_ref, w2f_ref, wef_ref, wrf_ref, colsf_ref, rowsf_ref, send, recv,
):
    wire = Wire(send, recv)
    d, m, h = wire.me
    dp, mp, hid = wire.size
    rows = D // mp
    fcols = we_ref.shape[1]
    half = rows // dp
    offset = pl.multiple_of(d * half, half)
    own = (
        (w1_ref, lambda mm_, hh: w1f_ref.at[hh, mm_, d], w1f_ref.at[:, :, d]),
        (w2_ref, lambda mm_, hh: w2f_ref.at[mm_, hh, d], w2f_ref.at[:, :, d]),
        (we_ref.at[pl.ds(offset, half)], lambda mm_, hh: wef_ref.at[mm_, d, :, pl.ds(pl.multiple_of(hh * fcols, fcols), fcols)], wef_ref.at[:, d]),
        (wr_ref.at[pl.ds(offset, half)], lambda mm_, hh: wrf_ref.at[mm_, d, :, pl.ds(pl.multiple_of(hh * fcols, fcols), fcols)], wrf_ref.at[:, d]),
    )
    wire.meet()
    waits = []
    local = []

    def swap(src_ref, dst_ref):
        mine = pl.ds(pl.multiple_of(m * rows, rows), rows)
        for q in range(1, mp):
            to = wire.peer(MP, q)
            waits.append(wire.send(src_ref.at[:, pl.ds(pl.multiple_of(to[1] * SEQ, SEQ), SEQ)], dst_ref.at[mine], to))
        local.append(wire.keep(src_ref.at[:, pl.ds(pl.multiple_of(m * SEQ, SEQ), SEQ)], dst_ref.at[mine]))

    for q in range(1, mp):
        waits.append(wire.send(cols_ref, colsf_ref.at[pl.ds(pl.multiple_of(m * rows, rows), rows)], wire.peer(MP, q)))
    local.append(wire.keep(cols_ref, colsf_ref.at[pl.ds(pl.multiple_of(m * rows, rows), rows)]))
    for o in range(1, hid):
        waits.append(wire.send(rows_ref, rowsf_ref.at[h], wire.peer(HID, o)))
    local.append(wire.keep(rows_ref, rowsf_ref.at[h]))

    first = {}

    def stage_one(i, axis):
        src, dst, _ = own[i]
        first[i] = [wire.send(src, dst(m, h), wire.peer(axis, o)) for o in range(1, wire.size[axis])]
        first[i].insert(0, wire.keep(src, dst(m, h)))

    second = {}

    def stage_two(i, axis):
        _, dst, _ = own[i]
        other = MP if axis == HID else HID
        second[i] = []
        for o, copy in enumerate(first[i]):
            if o == 0:
                copy.wait()
            else:
                copy.wait_recv()
            at = wire.origin(axis, o)
            piece = dst(m, at) if axis == HID else dst(at, h)
            second[i] += [wire.send(piece, piece, wire.peer(other, q)) for q in range(1, wire.size[other])]

    def stage_three(i):
        slab = own[i][2]
        for copy in second[i]:
            copy.wait_recv()
        for r in range(1, dp):
            waits.append(wire.send(slab, slab, wire.peer(DP, r)))

    routes = (HID, HID, HID, MP)
    stage_one(0, routes[0])
    swap(x_ref, xt_ref)
    for i in (1, 2, 3):
        stage_one(i, routes[i])
    swap(c_ref, ct_ref)
    for i in range(4):
        stage_two(i, routes[i])
    for i in range(4):
        stage_three(i)
    for copy in local:
        copy.wait()
    for copy in waits:
        copy.wait_recv()
    wire.finish()


def gather(x, c, w1, w2, we, wr, cols, rows):
    dp, mp, hid = lax.axis_size("dp"), lax.axis_size("mp"), lax.axis_size("hidden")
    half = D // mp // dp
    fcols = we.shape[1]
    sds = jax.ShapeDtypeStruct
    out_shape = (
        sds((D, SEQ), BF16), sds((D, SEQ), BF16), sds((hid, mp, dp, half, w1.shape[1]), BF16),
        sds((mp, hid, dp) + w2.shape, BF16), sds((mp, dp, half, hid * fcols), BF16),
        sds((mp, dp, half, hid * fcols), BF16), sds((D, cols.shape[1]), F32), sds((hid,) + rows.shape, F32),
    )
    n = 3 * mp + hid + 4 * (hid + mp + hid * mp + dp) + 8
    hbm = pl.BlockSpec(memory_space=pl.ANY)
    return pl.pallas_call(
        functools.partial(gather_kernel, n),
        out_shape=out_shape,
        in_specs=[hbm] * 8,
        out_specs=(hbm,) * 8,
        scratch_shapes=[pltpu.SemaphoreType.DMA((n,)), pltpu.SemaphoreType.DMA((n,))],
        compiler_params=params(collective_id=0, has_side_effects=True),
        name="gather",
    )(x, c, w1, w2, we, wr, cols, rows)


def scatter_kernel(
    o_ref, x_ref, dw1_ref, dw2_ref, dwe_ref, dwr_ref, vec_ref,
    of_ref, xf_ref, g1_ref, g2_ref, ge_ref, gr_ref, vecf_ref,
    a1, a2, ae, ar, s1, s2, se, sr, b1, b2, be, br, t1, t2, te, tr, c1, c2, ce, cr, va, vb, vc, v1, v2, send, recv,
):
    wire = Wire(send, recv)
    v_in = (va, vb, vc)
    d, m, h = wire.me
    dp, mp, hid = wire.size
    rows = D // mp
    fcols = ge_ref.shape[1]
    waits, local = [], []
    wire.meet()
    hslice = lambda hh: pl.ds(pl.multiple_of(hh * fcols, fcols), fcols)
    items = (
        (lambda dd: dw1_ref.at[:, :, dd], a1, s1, b1, t1, c1, g1_ref, HID, MP),
        (lambda dd: dw2_ref.at[:, :, dd], a2, s2, b2, t2, c2, g2_ref, MP, HID),
        (lambda dd: dwe_ref.at[:, dd], ae, se, be, te, ce, ge_ref, None, MP),
        (lambda dd: dwr_ref.at[:, dd], ar, sr, br, tr, cr, gr_ref, None, HID),
    )
    core = {}
    loads = {}

    def stage_core(i):
        src, a, s = items[i][:3]
        core[i] = [wire.send(src(wire.peer(DP, r)[0]), a.at[r - 1], wire.peer(DP, r)) for r in range(1, dp)]
        loads[i] = wire.keep(src(d), s)

    def swap(src_ref, dst_ref):
        mine = pl.ds(pl.multiple_of(m * SEQ, SEQ), SEQ)
        for q in range(1, mp):
            to = wire.peer(MP, q)
            waits.append(wire.send(src_ref.at[pl.ds(pl.multiple_of(to[1] * rows, rows), rows)], dst_ref.at[:, mine], to))
        local.append(wire.keep(src_ref.at[pl.ds(pl.multiple_of(m * rows, rows), rows)], dst_ref.at[:, mine]))

    def add_all(dst, own, others, shape):
        lead = shape[:-2]
        total = math.prod(lead)

        def body(n, _):
            index = []
            for size in reversed(lead):
                index.insert(0, lax.rem(n, size))
                n = lax.div(n, size)
            index = tuple(index)
            value = own[index].astype(F32)
            for j in range(others.shape[0]):
                value = value + others[(j,) + index].astype(F32)
            dst[index] = value.astype(dst.dtype)
            return 0

        lax.fori_loop(0, total, body, 0)

    def part(i, ref, axis, at):
        if i < 2:
            lead = items[i][7] == axis
            return ref.at[at] if lead else ref.at[:, at]
        return ref.at[at] if axis == MP else ref.at[:, :, hslice(at)]

    plane = {}

    def stage_plane(i):
        _, a, s, b, t, c, g, _, axis = items[i]
        for copy in core[i]:
            copy.wait_recv()
        loads[i].wait()
        add_all(s, s, a, s.shape)
        plane[i] = [
            wire.send(part(i, s, axis, wire.peer(axis, q)[axis]), b.at[q - 1], wire.peer(axis, q))
            for q in range(1, wire.size[axis])
        ]

    last = {}

    def stage_last(i):
        _, a, s, b, t, c, g, _, axis = items[i]
        for copy in plane[i]:
            copy.wait_recv()
        add_all(t, part(i, s, axis, wire.me[axis]), b, t.shape)
        other = MP if axis == HID else HID
        last[i] = []
        for q in range(1, wire.size[other]):
            to = wire.peer(other, q)
            if i < 2 or other == MP:
                src = t.at[to[other]]
            else:
                src = t.at[:, hslice(to[other])]
            last[i].append(wire.send(src, c.at[q - 1], to))

    def stage_end(i):
        _, a, s, b, t, c, g, _, axis = items[i]
        other = MP if axis == HID else HID
        for copy in last[i]:
            copy.wait_recv()
        own = t[wire.me[other]] if (i < 2 or other == MP) else t[:, hslice(h)]
        value = own.astype(F32)
        for j in range(c.shape[0]):
            value = value + c[j].astype(F32)
        g[...] = value

    vec = {}

    def vec_send(axis, src):
        vec[axis] = [wire.send(src, v_in[axis].at[o - 1], wire.peer(axis, o)) for o in range(1, wire.size[axis])]

    def vec_sum(axis, src, dst):
        for copy in vec[axis]:
            copy.wait_recv()
        total = src[...]
        for j in range(wire.size[axis] - 1):
            total = total + v_in[axis][j]
        dst[...] = total

    vec_send(DP, vec_ref)
    for i in (3, 2, 1, 0):
        stage_core(i)
    swap(o_ref, of_ref)
    for i in (3, 2, 1, 0):
        stage_plane(i)
    swap(x_ref, xf_ref)
    vec_sum(DP, vec_ref, v1)
    vec_send(MP, v1)
    for i in (3, 2, 1, 0):
        stage_last(i)
    vec_sum(MP, v1, v2)
    vec_send(HID, v2)
    for i in (3, 2, 1, 0):
        stage_end(i)
    vec_sum(HID, v2, vecf_ref)
    for copy in local:
        copy.wait()
    for copy in waits:
        copy.wait_recv()
    wire.finish()


def scatter(o, x, dw1, dw2, dwe, dwr, vec):
    dp, mp, hid = lax.axis_size("dp"), lax.axis_size("mp"), lax.axis_size("hidden")
    sds = jax.ShapeDtypeStruct
    half, c1 = dw1.shape[3:]
    half2, c2 = dw2.shape[3:]
    ff = dwe.shape[3]
    fc = ff // hid
    out_shape = (
        sds((D // mp, mp * SEQ), BF16), sds((D // mp, mp * SEQ), BF16), sds((half, c1), F32), sds((half2, c2), F32),
        sds((half, fc), F32), sds((half, fc), F32), sds(vec.shape, F32),
    )
    vm = lambda *shape: pltpu.VMEM(shape, BF16)
    slabs = ((hid, mp, half, c1), (mp, hid, half2, c2), (mp, half, ff), (mp, half, ff))
    after = ((hid, half, c1), (mp, half2, c2), (half, ff), (mp, half, fc))
    ends = ((half, c1), (half2, c2), (half, fc), (half, fc))
    near = (mp, hid, mp, hid)
    far = (hid, mp, hid, mp)
    scratch = [vm(dp - 1, *s) for s in slabs] + [vm(*s) for s in slabs]
    scratch += [vm(n - 1, *s) for n, s in zip(near, after)] + [vm(*s) for s in after]
    scratch += [vm(n - 1, *s) for n, s in zip(far, ends)]
    scratch += [
        pltpu.VMEM((dp - 1,) + vec.shape, F32), pltpu.VMEM((mp - 1,) + vec.shape, F32),
        pltpu.VMEM((hid - 1,) + vec.shape, F32), pltpu.VMEM(vec.shape, F32), pltpu.VMEM(vec.shape, F32),
    ]
    n = dp + mp + hid + 2 * mp + 4 * (dp + mp + hid + 1) + 8
    scratch += [pltpu.SemaphoreType.DMA((n,)), pltpu.SemaphoreType.DMA((n,))]
    hbm = pl.BlockSpec(memory_space=pl.ANY)
    vmem = pl.BlockSpec(memory_space=pltpu.VMEM)
    return pl.pallas_call(
        scatter_kernel,
        out_shape=out_shape,
        in_specs=[hbm] * 6 + [vmem],
        out_specs=(hbm, hbm) + (vmem,) * 5,
        scratch_shapes=scratch,
        compiler_params=params(collective_id=1, has_side_effects=True),
        name="scatter",
    )(o, x, dw1, dw2, dwe, dwr, vec)


def local(
    stored, positions, segments, present, norm_gains, norm_biases, input_proj, input_bias, output_proj,
    output_bias, expand_weight, expand_bias, reduce_weight, reduce_bias, cotangent,
):
    mp, hid, dp = lax.axis_size("mp"), lax.axis_size("hidden"), lax.axis_size("dp")
    m, h, d = lax.axis_index("mp"), lax.axis_index("hidden"), lax.axis_index("dp")
    rows_mp, hcols, fcols = D // mp, D // hid, expand_weight.shape[1]
    half = rows_mp // dp
    cols = [norm_gains[0], norm_biases[0], norm_gains[1], norm_biases[1], output_bias.astype(F32), reduce_bias.astype(F32)]
    cols = jnp.pad(jnp.stack(cols, axis=1), ((0, 0), (0, 128 - len(cols))))
    rows = jnp.concatenate(
        [
            expand_bias.astype(F32)[None],
            jnp.pad(input_bias.astype(F32), ((0, 0), (0, fcols - hcols))),
            jnp.zeros((5, fcols), F32),
        ]
    )
    w1 = lax.dynamic_slice_in_dim(input_proj, d * half, half, 0).reshape(half, 3 * hcols)
    w2 = lax.dynamic_slice_in_dim(output_proj, d * (hcols // dp), hcols // dp, 0)
    xt, ct, w1n, w2n, we, wr, cols, rows = gather(
        stored, cotangent, w1, w2, expand_weight, reduce_weight, cols, rows
    )
    w1n = w1n.reshape(hid, D, 3 * hcols)
    w2n = w2n.reshape(mp, D, rows_mp)
    we, wr = we.reshape(D, hid * fcols), wr.reshape(D, hid * fcols)
    be = rows[:, 0].reshape(1, hid * fcols)
    b1 = rows[:, 1:3, :hcols].transpose(1, 0, 2).reshape(2, D)
    bias_row = jnp.concatenate([b1[0], jnp.zeros_like(b1[0]), b1[1]])[None]

    table = position_table(lax.dynamic_slice_in_dim(positions, m * SEQ, SEQ))
    key_col = jnp.where(present == 1, segments, -1)[:, None]
    seg_row = segments[None, :]

    et, ft, qkv, w1f = project(xt, table, cols, w1n, bias_row)
    at, lse = attend(qkv, key_col, seg_row)
    out_t, dmid, do, dwr, dwe, dbe, dw2, db_feed, dg_second = feed(at, et, ct, w2n, cols, we, be, wr)
    dqt, dk, dv = attend_back(qkv, do, lse, key_col, seg_row)
    dw1, dx, db_proj, dg_first = project_back(ft, dqt, dk, dv, w1f, et, dmid, cols, hid)

    dg = jnp.stack([jnp.sum(dg_first, axis=2), jnp.sum(dg_second, axis=2)])
    vectors = jnp.concatenate(
        [dg.reshape(-1), db_proj[:, 0].reshape(-1), db_feed[:, 0].reshape(-1), dbe.reshape(-1)]
    ).reshape(-1, 128)
    output, d_stored, d_input, d_output, d_expand, d_reduce, vectors = scatter(
        out_t,
        dx,
        dw1.reshape(hid, mp, dp, half, 3 * hcols),
        dw2.reshape(mp, hid, dp, hcols // dp, rows_mp),
        dwe.reshape(mp, dp, half, hid * fcols),
        dwr.reshape(mp, dp, half, hid * fcols),
        vectors,
    )
    vectors = vectors.reshape(-1)
    dg = vectors[: 4 * D].reshape(2, 2, D)
    piece = D // (hid * mp * dp)
    dg = lax.dynamic_slice_in_dim(dg, ((m * dp + d) * hid + h) * piece, piece, 2)
    db_proj = vectors[4 * D : 6 * D].reshape(2, D)
    db_proj = lax.dynamic_slice_in_dim(db_proj, (h * dp + d) * (hcols // dp), hcols // dp, 1)
    db_feed = lax.dynamic_slice_in_dim(vectors[6 * D : 8 * D].reshape(2, D), (m * dp + d) * half, half, 1)
    dbe = lax.dynamic_slice_in_dim(vectors[8 * D :], (h * dp + d) * (fcols // dp), fcols // dp)
    return (
        output, d_stored.astype(F32), dg[:, 0], dg[:, 1], d_input.reshape(half, 3, hcols), db_proj, d_output, db_feed[1],
        d_expand, dbe, d_reduce, db_feed[0],
    )


def solution(mesh):
    placed = (
        P("mp", ("dp", "hidden")),
        P(("dp", "hidden")),
        P(("dp", "hidden", "mp")),
        P(("dp", "hidden", "mp")),
        P(None, "mp"),
        P(None, "mp"),
        P("mp", None, "hidden"),
        P(None, "hidden"),
        P("hidden", "mp"),
        P("mp"),
        P("mp", "hidden"),
        P("hidden"),
        P("mp", "hidden"),
        P("mp"),
        P("mp", ("dp", "hidden")),
    )
    return jax.shard_map(
        local,
        mesh=mesh,
        in_specs=placed,
        out_specs=(
            P("mp", ("dp", "hidden")),
            P("mp", ("dp", "hidden")),
            P(None, ("mp", "dp", "hidden")),
            P(None, ("mp", "dp", "hidden")),
            P(("mp", "dp"), None, "hidden"),
            P(None, ("hidden", "dp")),
            P(("hidden", "dp"), "mp"),
            P(("mp", "dp")),
            P(("mp", "dp"), "hidden"),
            P(("hidden", "dp")),
            P(("mp", "dp"), "hidden"),
            P(("mp", "dp")),
        ),
        check_vma=False,
    )
```

```python
import functools
import math

import jax
import jax.numpy as jnp
from jax import lax
from jax.experimental import pallas as pl
from jax.experimental.pallas import tpu as pltpu
from jax.sharding import PartitionSpec as P

D = 768
HEADS = 12
HD = 64
SEQ = 1024
FB = 256
QB = 256
PAIR = 2 * HD
PAIRS = HEADS // 2
EPS = 1e-06
MASKED = -1e30
F32 = jnp.float32
BF16 = jnp.bfloat16
VMEM_LIMIT = 60 * 1024 * 1024
PI_2 = (1.5703125, 4.837512969970703125e-4, 7.549789948768648e-8)

NN = (((1,), (0,)), ((), ()))
NT = (((1,), (1,)), ((), ()))


def mm(a, b, dims=NN):
    return lax.dot_general(a, b, dims, preferred_element_type=F32)


def whole(shape):
    return pl.BlockSpec(shape, lambda *_: (0,) * len(shape), pipeline_mode=pl.Buffered(1))


def params(**kw):
    return pltpu.CompilerParams(vmem_limit_bytes=VMEM_LIMIT, **kw)


def lane_sums(x):
    total = x[:, 0:128]
    for j in range(1, x.shape[1] // 128):
        total = total + x[:, j * 128 : (j + 1) * 128]
    return total


def norm_stats(e):
    average = jnp.sum(e, axis=0, keepdims=True) * (1.0 / D)
    spread = jnp.sum(e * e, axis=0, keepdims=True) * (1.0 / D) - average * average
    return average, lax.rsqrt(spread + EPS)


def fill_bias(bias_ref, key_ref, seg_ref):
    def rows_of(i, _):
        rows = pl.ds(pl.multiple_of(i * 256, 256), 256)
        same = key_ref[rows, :] == seg_ref[...]
        row_id = lax.broadcasted_iota(jnp.int32, (256, SEQ), 0) + i * 256
        col_id = lax.broadcasted_iota(jnp.int32, (256, SEQ), 1)
        bias_ref[rows, :] = jnp.where(same | (row_id == col_id), 0.0, MASKED)
        return 0

    lax.fori_loop(0, SEQ // 256, rows_of, 0)


MESH = pl.DeviceIdType.MESH


class Wire:
    def __init__(self, send, recv):
        self.send_sem, self.recv_sem, self.count, self.sent = send, recv, 0, []
        self.me = (lax.axis_index("dp"), lax.axis_index("mp"), lax.axis_index("hidden"))
        self.size = (lax.axis_size("dp"), lax.axis_size("mp"), lax.axis_size("hidden"))

    def peer(self, axis, offset):
        where = list(self.me)
        where[axis] = lax.rem(where[axis] + offset, self.size[axis])
        return tuple(where)

    def origin(self, axis, offset):
        return lax.rem(self.me[axis] - offset + self.size[axis], self.size[axis])

    def meet(self):
        barrier = pltpu.get_barrier_semaphore()
        total = 0
        for axis in range(3):
            for offset in range(1, self.size[axis]):
                pl.semaphore_signal(barrier, 1, device_id=self.peer(axis, offset), device_id_type=MESH)
                total += 1
        pl.semaphore_wait(barrier, total)

    def send(self, src, dst, target):
        copy = pltpu.make_async_remote_copy(
            src, dst, self.send_sem.at[self.count], self.recv_sem.at[self.count], device_id=target, device_id_type=MESH
        )
        copy.start()
        self.count += 1
        self.sent.append(copy)
        return copy

    def keep(self, src, dst):
        copy = pltpu.make_async_copy(src, dst, self.send_sem.at[self.count])
        copy.start()
        self.count += 1
        return copy

    def finish(self):
        for copy in self.sent:
            copy.wait_send()


DP, MP, HID = 0, 1, 2


HALF = D // 2


def sin_cos(angles):
    turns = jnp.floor(angles * (2.0 / math.pi) + 0.5)
    r = ((angles - turns * PI_2[0]) - turns * PI_2[1]) - turns * PI_2[2]
    r2 = r * r
    s = r + r * r2 * (-1.6666654611e-1 + r2 * (8.3321608736e-3 + r2 * -1.9515295891e-4))
    c = 1.0 - 0.5 * r2 + r2 * r2 * (4.166664568298827e-2 + r2 * (-1.388731625493765e-3 + r2 * 2.443315711809948e-5))
    quarter = turns - 4.0 * jnp.floor(turns * 0.25)
    odd = (quarter == 1.0) | (quarter == 3.0)
    flip_s = quarter >= 2.0
    flip_c = (quarter == 1.0) | (quarter == 2.0)
    sine = jnp.where(odd, c, s)
    cosine = jnp.where(odd, s, c)
    return jnp.where(flip_s, -sine, sine), jnp.where(flip_c, -cosine, cosine)


def forward_kernel(
    x_ref, c_ref, w1a_ref, w1b_ref, w2_ref, we_ref, wr_ref, cols_ref, rows_ref, pos_ref, rate_ref, key_ref, seg_ref,
    et_out, ft_out, w1_out, qkv_out, at_ref, lse_ref, ct_ref, w2f_ref, wef_ref, wrf_ref, p_ref, rowsf_ref,
    xt, w1af, w1bf, tab, et, ft, f, w1, qkv, bias, vt, wb, send, recv,
):
    wire = Wire(send, recv)
    d, m, h = wire.me
    dp, mp, hid = wire.size
    rows = D // mp
    wide = D // hid
    fcols = we_ref.shape[1]
    half = rows // dp
    offset = pl.multiple_of(d * half, half)
    hs = lambda hh: pl.ds(pl.multiple_of(hh * fcols, fcols), fcols)
    own = (
        (w1a_ref, lambda mm_, hh: w1af.at[hh, mm_, d], lambda: w1af.at[:, :, d], HID),
        (w1b_ref, lambda mm_, hh: w1bf.at[hh, mm_, d], lambda: w1bf.at[:, :, d], MP),
        (w2_ref, lambda mm_, hh: w2f_ref.at[mm_, hh, d], lambda: w2f_ref.at[:, :, d], HID),
        (we_ref.at[pl.ds(offset, half)], lambda mm_, hh: wef_ref.at[mm_, d, :, hs(hh)], lambda: wef_ref.at[:, d], HID),
        (wr_ref.at[pl.ds(offset, half)], lambda mm_, hh: wrf_ref.at[mm_, d, :, hs(hh)], lambda: wrf_ref.at[:, d], MP),
    )
    wire.meet()
    waits, stored = [], []
    first, second, third = {}, {}, {}

    def swap(src_ref, dst_ref):
        mine = pl.ds(pl.multiple_of(m * rows, rows), rows)
        moved = []
        for q in range(1, mp):
            to = wire.peer(MP, q)
            moved.append(wire.send(src_ref.at[:, pl.ds(pl.multiple_of(to[1] * SEQ, SEQ), SEQ)], dst_ref.at[mine], to))
        return moved, wire.keep(src_ref.at[:, pl.ds(pl.multiple_of(m * SEQ, SEQ), SEQ)], dst_ref.at[mine])

    def landed(pair):
        for copy in pair[0]:
            copy.wait_recv()
        pair[1].wait()

    def stage_one(i):
        src, dst, _, axis = own[i]
        first[i] = [wire.keep(src, dst(m, h))]
        first[i] += [wire.send(src, dst(m, h), wire.peer(axis, o)) for o in range(1, wire.size[axis])]

    def stage_two(i):
        _, dst, _, axis = own[i]
        other = MP if axis == HID else HID
        second[i] = []
        for o, copy in enumerate(first[i]):
            if o == 0:
                copy.wait()
            else:
                copy.wait_recv()
            at = wire.origin(axis, o)
            piece = dst(m, at) if axis == HID else dst(at, h)
            second[i] += [wire.send(piece, piece, wire.peer(other, q)) for q in range(1, wire.size[other])]

    def stage_three(i):
        for copy in second[i]:
            copy.wait_recv()
        third[i] = [wire.send(own[i][2](), own[i][2](), wire.peer(DP, r)) for r in range(1, dp)]

    def done(i):
        for copy in third[i]:
            copy.wait_recv()

    mine = pl.ds(pl.multiple_of(m * rows, rows), rows)
    small = [wire.send(cols_ref, p_ref.at[mine], wire.peer(MP, q)) for q in range(1, mp)]
    small += [wire.send(rows_ref, rowsf_ref.at[h], wire.peer(HID, o)) for o in range(1, hid)]
    kept = [wire.keep(cols_ref, p_ref.at[mine]), wire.keep(rows_ref, rowsf_ref.at[h])]
    stage_one(0)
    stage_one(1)
    x_in = swap(x_ref, xt)

    def table_rows(j, _):
        at = pl.ds(pl.multiple_of(j * 64, 64), 64)
        sine, cosine = sin_cos(rate_ref[at, :] * pos_ref[...])
        tab[at, :] = sine
        tab[pl.ds(pl.multiple_of(j * 64 + HALF, 64), 64), :] = cosine
        return 0

    lax.fori_loop(0, 2, table_rows, 0)
    stage_two(0)
    stage_two(1)
    for i in (2, 3, 4):
        stage_one(i)
    lax.fori_loop(2, HALF // 64, table_rows, 0)
    fill_bias(bias, key_ref, seg_ref)
    c_in = swap(c_ref, ct_ref)
    for copy in small:
        copy.wait_recv()
    for copy in kept:
        copy.wait()
    wb[...] = jnp.zeros_like(wb)
    for hh in range(hid):
        wb[:, hh * wide : (hh + 1) * wide] = rowsf_ref[hh, 1:2, :wide]
        wb[:, 2 * D + hh * wide : 2 * D + (hh + 1) * wide] = rowsf_ref[hh, 2:3, :wide]
    landed(x_in)

    def norm_cols(j, _):
        cols = pl.ds(pl.multiple_of(j * 256, 256), 256)
        e = xt[:, cols].astype(F32) + tab[:, cols]
        et[:, cols] = e
        average, inv = norm_stats(e)
        low = ((e - average) * inv * p_ref[:, 0:1] + p_ref[:, 1:2]).astype(BF16)
        ft[:, cols] = low
        f[cols, :] = low.T
        return 0

    lax.fori_loop(0, SEQ // 256, norm_cols, 0)
    stored += [wire.keep(et, et_out), wire.keep(ft, ft_out)]
    stage_three(0)
    stage_three(1)
    stage_two(2)
    done(0)
    done(1)
    for hh in range(hid):
        for mm_ in range(mp):
            for dd in range(dp):
                at = slice(mm_ * rows + dd * half, mm_ * rows + (dd + 1) * half)
                for k in range(3):
                    if k < 2:
                        part = w1af[hh, mm_, dd, :, k * wide : (k + 1) * wide]
                    else:
                        part = w1bf[hh, mm_, dd]
                    w1[at, k * D + hh * wide : k * D + (hh + 1) * wide] = part
    stored.append(wire.keep(w1, w1_out))

    def cols_of(n, scale):
        cols = pl.ds(pl.multiple_of(n * 256, 256), 256)
        y = (mm(f[...], w1[:, cols]) + wb[:, cols]).astype(BF16)
        qkv[:, cols] = y * jnp.asarray(scale, BF16)
        return 0

    lax.fori_loop(0, D // 256, lambda n, c: cols_of(n, HD**-0.5), 0)
    stage_two(3)
    lax.fori_loop(D // 256, 3 * D // 256, lambda n, c: cols_of(n, 1.0), 0)
    stored.append(wire.keep(qkv, qkv_out))
    stage_two(4)

    low = lax.broadcasted_iota(jnp.int32, (QB, PAIR), 1) < HD
    lse_ref[...] = jnp.zeros_like(lse_ref)

    def pair_of(p, _):
        lanes = pl.ds(pl.multiple_of(p * PAIR, PAIR), PAIR)
        k_lanes = pl.ds(pl.multiple_of(p * PAIR + D, PAIR), PAIR)
        v_lanes = pl.ds(pl.multiple_of(p * PAIR + 2 * D, PAIR), PAIR)
        vt[...] = qkv[:, v_lanes].T

        def block(j, _):
            cols = pl.ds(pl.multiple_of(j * QB, QB), QB)
            q = qkv[cols, lanes]
            for hh in range(2):
                qm = jnp.where(low if hh == 0 else ~low, q, jnp.zeros_like(q))
                s = mm(qkv[:, k_lanes], qm, NT) + bias[:, cols]
                top = jnp.max(s, axis=0, keepdims=True)
                e = jnp.exp(s - top)
                total = jnp.sum(e, axis=0, keepdims=True)
                o = mm(vt[hh * HD : (hh + 1) * HD, :], e.astype(BF16)) / total
                at_ref[pl.ds(pl.multiple_of(p * PAIR + hh * HD, HD), HD), cols] = o.astype(BF16)
                lse_ref[p, hh : hh + 1, cols] = top + jnp.log(total)
            return 0

        lax.fori_loop(0, SEQ // QB, block, 0)
        return 0

    lax.fori_loop(0, 2, pair_of, 0)
    stage_three(2)
    lax.fori_loop(2, 4, pair_of, 0)
    stage_three(3)
    lax.fori_loop(4, PAIRS, pair_of, 0)
    stage_three(4)
    landed(c_in)
    for i in (2, 3, 4):
        done(i)
    for copy in stored:
        copy.wait()
    wire.finish()


def forward(x, c, w1a, w1b, w2, we, wr, cols, rows, pos, rate, key_col, seg_row):
    dp, mp, hid = lax.axis_size("dp"), lax.axis_size("mp"), lax.axis_size("hidden")
    half = D // mp // dp
    ff = hid * we.shape[1]
    sds = jax.ShapeDtypeStruct
    out_shape = (
        sds((D, SEQ), F32), sds((D, SEQ), BF16), sds((D, 3 * D), BF16), sds((SEQ, 3 * D), BF16),
        sds((D, SEQ), BF16), sds((PAIRS, 8, SEQ), F32),
        sds((D, SEQ), BF16), sds((mp, hid, dp) + w2.shape, BF16), sds((mp, dp, half, ff), BF16),
        sds((mp, dp, half, ff), BF16), sds((D, cols.shape[1]), F32), sds((hid,) + rows.shape, F32),
    )
    n = 3 * mp + hid + 5 * (hid + mp + hid * mp + dp) + 16
    hbm = pl.BlockSpec(memory_space=pl.ANY)
    vmem = pl.BlockSpec(memory_space=pltpu.VMEM)
    vm = lambda dtype, *shape: pltpu.VMEM(shape, dtype)
    return pl.pallas_call(
        forward_kernel,
        out_shape=out_shape,
        in_specs=[hbm] * 9 + [vmem] * 4,
        out_specs=(hbm,) * 4 + (vmem,) * 2 + (hbm,) * 4 + (vmem,) * 2,
        scratch_shapes=[
            vm(BF16, D, SEQ), vm(BF16, hid, mp, dp, half, w1a.shape[1]), vm(BF16, hid, mp, dp, half, w1b.shape[1]),
            vm(F32, D, SEQ), vm(F32, D, SEQ), vm(BF16, D, SEQ), vm(BF16, SEQ, D), vm(BF16, D, 3 * D),
            vm(BF16, SEQ, 3 * D), vm(F32, SEQ, SEQ), vm(BF16, PAIR, SEQ), vm(F32, 1, 3 * D),
            pltpu.SemaphoreType.DMA((n,)), pltpu.SemaphoreType.DMA((n,)),
        ],
        compiler_params=params(collective_id=0, has_side_effects=True),
        name="forward",
    )(x, c, w1a, w1b, w2, we, wr, cols, rows, pos, rate, key_col, seg_row)


def feed_kernel(
    at_ref, et_ref, ct_ref, w2n_ref, p_ref, we_ref, be_ref, wr_ref,
    out_ref, dmid_ref, do_ref, dwr_ref, dwe_ref, dbe_ref, dw2_ref, db_ref, dg_ref,
    s_ref, st_ref, c_ref, ot_ref, ds_ref, mid_ref, bt_ref, w2_ref,
):
    step = pl.program_id(0)

    @pl.when(step == 0)
    def _():
        mp = w2n_ref.shape[0]
        wide = D // mp
        for j in range(mp):
            w2_ref[:, j * wide : (j + 1) * wide] = w2n_ref[j]
        w2t = w2_ref[...].T

        def cols_of(j, _):
            cols = pl.ds(pl.multiple_of(j * 256, 256), 256)
            mid = et_ref[:, cols] + (mm(w2t, at_ref[:, cols]) + p_ref[:, 4:5])
            mid_ref[:, cols] = mid
            average, inv = norm_stats(mid)
            s = ((mid - average) * inv * p_ref[:, 2:3] + p_ref[:, 3:4]).astype(BF16)
            st_ref[:, cols] = s
            s_ref[cols, :] = s.T
            c_ref[cols, :] = ct_ref[:, cols].T
            return 0

        lax.fori_loop(0, SEQ // 256, cols_of, 0)

    pre = mm(s_ref[...], we_ref[...]) + be_ref[...]
    cdf = 0.5 * (1.0 + lax.erf(pre * (1.0 / math.sqrt(2.0))))
    act = (pre * cdf).astype(BF16)
    slope = cdf + pre * jnp.exp(-0.5 * pre * pre) * (1.0 / math.sqrt(2.0 * math.pi))
    grad = (mm(c_ref[...], wr_ref[...]) * slope).astype(BF16)
    dwr_ref[...] = mm(ct_ref[...], act).astype(BF16)
    dwe_ref[...] = mm(st_ref[...], grad).astype(BF16)
    dbe_ref[...] = jnp.sum(grad.astype(F32), axis=0, keepdims=True)
    o = mm(wr_ref[...], act, NT)
    ds = mm(we_ref[...], grad, NT)

    @pl.when(step == 0)
    def _():
        ot_ref[...] = o
        ds_ref[...] = ds

    @pl.when(step > 0)
    def _():
        ot_ref[...] += o
        ds_ref[...] += ds

    @pl.when(step == pl.num_programs(0) - 1)
    def _():
        dg_ref[...] = jnp.zeros_like(dg_ref)

        def cols_of(j, _):
            cols = pl.ds(pl.multiple_of(j * 256, 256), 256)
            mid = mid_ref[:, cols]
            out_ref[:, cols] = (mid + (ot_ref[:, cols] + p_ref[:, 5:6])).astype(BF16)
            average, inv = norm_stats(mid)
            normed = (mid - average) * inv
            ds = ds_ref[:, cols]
            scaled = ds * p_ref[:, 2:3]
            total = jnp.sum(scaled, axis=0, keepdims=True) * (1.0 / D)
            crossed = jnp.sum(scaled * normed, axis=0, keepdims=True) * (1.0 / D)
            dmid = ct_ref[:, cols].astype(F32) + inv * (scaled - total - normed * crossed)
            dmid_ref[:, cols] = dmid
            low = dmid.astype(BF16)
            bt_ref[:, cols] = low
            do_ref[cols, :] = mm(w2_ref[...], low).astype(BF16).T
            dg_ref[0] += lane_sums(ds * normed)
            dg_ref[1] += lane_sums(ds)
            return 0

        lax.fori_loop(0, SEQ // 256, cols_of, 0)
        ones = jnp.ones((8, SEQ), BF16)
        db_ref[0] = mm(ones, ct_ref[...], NT)
        db_ref[1] = mm(ones, bt_ref[...], NT)

        wide = D // dw2_ref.shape[0]
        for j in range(dw2_ref.shape[0]):
            dw2_ref[j] = mm(at_ref[...], bt_ref[j * wide : (j + 1) * wide, :], NT).astype(BF16)


def feed(at, et, ct, w2, small, we, be, wr):
    ff = we.shape[1]
    cols = pl.BlockSpec((D, FB), lambda f: (0, f))
    row = pl.BlockSpec((1, FB), lambda f: (0, f))
    sds = jax.ShapeDtypeStruct
    return pl.pallas_call(
        feed_kernel,
        grid=(ff // FB,),
        in_specs=[
            whole((D, SEQ)), whole((D, SEQ)), whole((D, SEQ)), whole(w2.shape), whole((D, 128)), cols, row, cols,
        ],
        out_specs=(
            whole((D, SEQ)), whole((D, SEQ)), whole((SEQ, D)), cols, cols, row, whole(w2.shape),
            whole((2, 8, D)), whole((2, D, 128)),
        ),
        out_shape=(
            sds((D, SEQ), BF16), sds((D, SEQ), F32), sds((SEQ, D), BF16), sds((D, ff), BF16), sds((D, ff), BF16),
            sds((1, ff), F32), sds(w2.shape, BF16), sds((2, 8, D), F32), sds((2, D, 128), F32),
        ),
        scratch_shapes=[
            pltpu.VMEM((SEQ, D), BF16), pltpu.VMEM((D, SEQ), BF16), pltpu.VMEM((SEQ, D), BF16),
            pltpu.VMEM((D, SEQ), F32), pltpu.VMEM((D, SEQ), F32), pltpu.VMEM((D, SEQ), F32),
            pltpu.VMEM((D, SEQ), BF16), pltpu.VMEM((D, D), BF16),
        ],
        compiler_params=params(),
        name="feed",
    )(at, et, ct, w2, small, we, be, wr)


def backward_kernel(
    o_ref, dw2_ref, dwe_ref, dwr_ref, qkv_in, do_in, lse_ref, key_ref, seg_ref, ft_in, w_in, et_in, dmid_in, p_ref,
    dbe_ref, dbf_ref, dgs_ref,
    of_ref, xf_ref, ga_ref, gb_ref, g2_ref, ge_ref, gr_ref, vecf_ref,
    qkv, do, bias, kt, dqt, dk, dv, dka, dva, ft, w1, et, dmid, dgp,
    a0, a1, a2, a3, a4, o0, o1, s2, s3, s4, b0, b1, b2, b3, b4, t0, t1, t2, t3, t4, c0, c1, c2, c3, c4,
    v0, va, vb, vc, v1, v2, loads, send, recv,
):
    wire = Wire(send, recv)
    d, m, h = wire.me
    dp, mp, hid = wire.size
    rows = D // mp
    wide = D // hid
    half = rows // dp
    fcols = ge_ref.shape[1]
    v_in = (va, vb, vc)
    hslice = lambda hh: pl.ds(pl.multiple_of(hh * fcols, fcols), fcols)

    def load(n, src, dst):
        copy = pltpu.make_async_copy(src, dst, loads.at[n])
        copy.start()
        return copy

    parts = []
    for p in range(PAIRS):
        got = []
        for k in range(3):
            lanes = slice(k * D + p * PAIR, k * D + (p + 1) * PAIR)
            got.append(load(4 * p + k, qkv_in.at[:, lanes], qkv.at[:, lanes]))
        lanes = slice(p * PAIR, (p + 1) * PAIR)
        got.append(load(4 * p + 3, do_in.at[:, lanes], do.at[:, lanes]))
        parts.append(got)
    others = [load(4 * PAIRS + i, a, b) for i, (a, b) in enumerate(((ft_in, ft), (w_in, w1), (et_in, et), (dmid_in, dmid)))]
    wire.meet()
    items = (
        (lambda dd: o0.at[dd], a0, o0.at[d], b0, t0, c0, ga_ref, MP, HID),
        (lambda dd: o1.at[dd], a1, o1.at[d], b1, t1, c1, gb_ref, HID, HID),
        (lambda dd: dw2_ref.at[:, :, dd], a2, s2, b2, t2, c2, g2_ref, MP, MP),
        (lambda dd: dwe_ref.at[:, dd], a3, s3, b3, t3, c3, ge_ref, MP, None),
        (lambda dd: dwr_ref.at[:, dd], a4, s4, b4, t4, c4, gr_ref, HID, None),
    )
    core, kept, near, far = {}, {}, {}, {}

    def stage_core(i):
        src, a, s = items[i][:3]
        core[i] = [wire.send(src(wire.peer(DP, r)[0]), a.at[r - 1], wire.peer(DP, r)) for r in range(1, dp)]
        if i > 1:
            kept[i] = wire.keep(src(d), s)

    def add_all(dst, own, others, shape):
        lead = shape[:-2]

        def body(n, _):
            index = []
            for size in reversed(lead):
                index.insert(0, lax.rem(n, size))
                n = lax.div(n, size)
            index = tuple(index)
            value = own[index].astype(F32)
            for j in range(others.shape[0]):
                value = value + others[(j,) + index].astype(F32)
            dst[index] = value.astype(dst.dtype)
            return 0

        lax.fori_loop(0, math.prod(lead), body, 0)

    def part(i, ref, axis, at, leads):
        if items[i][8] is None:
            return ref.at[(slice(None),) * len(leads) + (slice(None), hslice(at))] if axis == HID else ref.at[at]
        return ref.at[at] if leads[0] == axis else ref.at[:, at]

    def leads_of(i):
        lead = items[i][8]
        return (MP,) if lead is None else ((HID, MP) if lead == HID else (MP, HID))

    def stage_near(i):
        _, a, s, b, t, c, g, axis, _ = items[i]
        for copy in core[i]:
            copy.wait_recv()
        if i in kept:
            kept[i].wait()
        add_all(s, s, a, s.shape)
        near[i] = [
            wire.send(part(i, s, axis, wire.peer(axis, q)[axis], leads_of(i)), b.at[q - 1], wire.peer(axis, q))
            for q in range(1, wire.size[axis])
        ]

    def stage_far(i):
        _, a, s, b, t, c, g, axis, lead = items[i]
        for copy in near[i]:
            copy.wait_recv()
        add_all(t, part(i, s, axis, wire.me[axis], leads_of(i)), b, t.shape)
        other = MP if axis == HID else HID
        left = tuple(x for x in leads_of(i) if x != axis)
        far[i] = []
        for q in range(1, wire.size[other]):
            to = wire.peer(other, q)
            far[i].append(wire.send(part(i, t, other, to[other], left), c.at[q - 1], to))

    def stage_end(i):
        _, a, s, b, t, c, g, axis, lead = items[i]
        other = MP if axis == HID else HID
        left = tuple(x for x in leads_of(i) if x != axis)
        for copy in far[i]:
            copy.wait_recv()
        value = part(i, t, other, wire.me[other], left)[...].astype(F32)
        for j in range(c.shape[0]):
            value = value + c[j].astype(F32)
        g[...] = value

    moved, held = [], []

    def swap(src_ref, dst_ref):
        mine = pl.ds(pl.multiple_of(m * SEQ, SEQ), SEQ)
        for q in range(1, mp):
            to = wire.peer(MP, q)
            moved.append(wire.send(src_ref.at[pl.ds(pl.multiple_of(to[1] * rows, rows), rows)], dst_ref.at[:, mine], to))
        held.append(wire.keep(src_ref.at[pl.ds(pl.multiple_of(m * rows, rows), rows)], dst_ref.at[:, mine]))

    vec = {}

    def vec_send(axis, src):
        vec[axis] = [wire.send(src, v_in[axis].at[o - 1], wire.peer(axis, o)) for o in range(1, wire.size[axis])]

    def vec_sum(axis, src, dst):
        for copy in vec[axis]:
            copy.wait_recv()
        total = src[...]
        for j in range(wire.size[axis] - 1):
            total = total + v_in[axis][j]
        dst[...] = total

    for i in (4, 3, 2):
        stage_core(i)
    swap(o_ref, of_ref)
    fill_bias(bias, key_ref, seg_ref)
    low = lax.broadcasted_iota(jnp.int32, (QB, PAIR), 1) < HD

    def pair_of(p, _):
        off = pl.multiple_of(p * PAIR, PAIR)
        lanes = pl.ds(off, PAIR)
        k_lanes = pl.ds(pl.multiple_of(off + D, PAIR), PAIR)
        v_lanes = pl.ds(pl.multiple_of(off + 2 * D, PAIR), PAIR)
        kt[...] = qkv[:, k_lanes].T
        dka[...] = jnp.zeros_like(dka)
        dva[...] = jnp.zeros_like(dva)

        def block(j, _):
            cols = pl.ds(pl.multiple_of(j * QB, QB), QB)
            q = qkv[cols, lanes]
            g = do[cols, lanes]
            for hh in range(2):
                keep = low if hh == 0 else ~low
                qm = jnp.where(keep, q, jnp.zeros_like(q))
                gm = jnp.where(keep, g, jnp.zeros_like(g))
                e = jnp.exp(mm(qkv[:, k_lanes], qm, NT) + bias[:, cols] - lse_ref[p, hh : hh + 1, cols])
                t = e * mm(qkv[:, v_lanes], gm, NT)
                ds = (t - e * jnp.sum(t, axis=0, keepdims=True)).astype(BF16)
                dva[...] += mm(e.astype(BF16), gm)
                dka[...] += mm(ds, qm)
                dq = mm(kt[hh * HD : (hh + 1) * HD, :], ds) * HD**-0.5
                dqt[pl.ds(pl.multiple_of(off + hh * HD, HD), HD), cols] = dq.astype(BF16)
            return 0

        lax.fori_loop(0, SEQ // QB, block, 0)
        dk[:, lanes] = dka[...].astype(BF16)
        dv[:, lanes] = dva[...].astype(BF16)
        return 0

    def pairs(first, last):
        for p in range(first, last):
            for copy in parts[p]:
                copy.wait()
        lax.fori_loop(first, last, pair_of, 0)

    pairs(0, 1)
    stage_near(4)
    stage_near(3)
    stage_near(2)
    pairs(1, 5)
    stage_far(3)
    stage_far(2)
    pairs(5, PAIRS)
    stage_far(4)
    for copy in others:
        copy.wait()

    for hh in range(hid):
        for k in range(3):
            if k == 0:
                value = mm(ft[...], dqt[hh * wide : (hh + 1) * wide, :], NT).astype(BF16)
            else:
                value = mm(ft[...], (dk, dv)[k - 1][:, hh * wide : (hh + 1) * wide]).astype(BF16)
            for mm_ in range(mp):
                for dd in range(dp):
                    piece = value[mm_ * rows + dd * half : mm_ * rows + (dd + 1) * half, :]
                    if k < 2:
                        o0[dd, hh, mm_, :, k * wide : (k + 1) * wide] = piece
                    else:
                        o1[dd, hh, mm_] = piece
    stage_core(1)
    stage_core(0)
    df = bias.at[pl.ds(0, D)]
    dx = ft

    def feature_cols(j, _):
        cols = pl.ds(pl.multiple_of(j * 256, 256), 256)
        value = mm(w1[:, 0:D], dqt[:, cols])
        value += mm(w1[:, D : 2 * D], dk[cols, :], NT)
        value += mm(w1[:, 2 * D : 3 * D], dv[cols, :], NT)
        df[:, cols] = value
        return 0

    lax.fori_loop(0, SEQ // 256, feature_cols, 0)
    stage_near(1)
    stage_near(0)
    dgp[...] = jnp.zeros_like(dgp)

    def norm_cols(j, _):
        cols = pl.ds(pl.multiple_of(j * 256, 256), 256)
        e = et[:, cols]
        average, inv = norm_stats(e)
        normed = (e - average) * inv
        g = df[:, cols]
        scaled = g * p_ref[:, 0:1]
        total = jnp.sum(scaled, axis=0, keepdims=True) * (1.0 / D)
        crossed = jnp.sum(scaled * normed, axis=0, keepdims=True) * (1.0 / D)
        dx[:, cols] = (dmid[:, cols] + inv * (scaled - total - normed * crossed)).astype(BF16)
        dgp[0] += lane_sums(g * normed)
        dgp[1] += lane_sums(g)
        return 0

    lax.fori_loop(0, SEQ // 256, norm_cols, 0)
    swap(dx, xf_ref)
    ones = jnp.ones((8, SEQ), BF16)
    v0[...] = jnp.zeros_like(v0)
    for n in range(2):
        v0[n : n + 1, :] = jnp.sum(dgp[n].T, axis=0, keepdims=True)
        v0[2 + n : 3 + n, :] = jnp.sum(dgs_ref[n].T, axis=0, keepdims=True)
        v0[6 + n : 7 + n, :] = dbf_ref[n, 0:1, :]
    v0[4:5, :] = mm(ones, dqt[...], NT)[0:1]
    v0[5:6, :] = mm(ones, dv[...])[0:1]
    for n in range(dbe_ref.shape[1] // D):
        v0[8 + n : 9 + n, :] = dbe_ref[:, n * D : (n + 1) * D]
    vec_send(DP, v0)
    stage_end(3)
    stage_end(2)
    vec_sum(DP, v0, v1)
    vec_send(MP, v1)
    stage_far(1)
    stage_far(0)
    vec_sum(MP, v1, v2)
    vec_send(HID, v2)
    stage_end(4)
    stage_end(1)
    stage_end(0)
    vec_sum(HID, v2, vecf_ref)
    for copy in held:
        copy.wait()
    for copy in moved:
        copy.wait_recv()
    wire.finish()


def backward(o, dw2, dwe, dwr, qkv, do, lse, key_col, seg_row, ft, w1, et, dmid, cols, dbe, dbf, dgs):
    dp, mp, hid = lax.axis_size("dp"), lax.axis_size("mp"), lax.axis_size("hidden")
    sds = jax.ShapeDtypeStruct
    wide = D // hid
    half = D // mp // dp
    half2, c2 = dw2.shape[3:]
    ff = dwe.shape[3]
    fc = ff // hid
    out_shape = (
        sds((D // mp, mp * SEQ), BF16), sds((D // mp, mp * SEQ), BF16), sds((half, 2 * wide), F32),
        sds((half, wide), F32), sds((half2, c2), F32), sds((half, fc), F32), sds((half, fc), F32), sds((16, D), F32),
    )
    vm = lambda *shape: pltpu.VMEM(shape, BF16)
    vf = lambda *shape: pltpu.VMEM(shape, F32)
    slabs = (
        (hid, mp, half, 2 * wide), (hid, mp, half, wide), (mp, hid, half2, c2), (mp, half, ff), (mp, half, ff)
    )
    after = ((hid, half, 2 * wide), (mp, half, wide), (hid, half2, c2), (half, ff), (mp, half, fc))
    ends = ((half, 2 * wide), (half, wide), (half2, c2), (half, fc), (half, fc))
    near = (mp, hid, mp, mp, hid)
    far = (hid, mp, hid, hid, mp)
    scratch = [
        vm(SEQ, 3 * D), vm(SEQ, D), vf(SEQ, SEQ), vm(PAIR, SEQ), vm(D, SEQ), vm(SEQ, D), vm(SEQ, D),
        vf(SEQ, PAIR), vf(SEQ, PAIR), vm(D, SEQ), vm(D, 3 * D), vf(D, SEQ), vf(D, SEQ), vf(2, D, 128),
    ]
    scratch += [vm(dp - 1, *s) for s in slabs]
    scratch += [vm(dp, *s) for s in slabs[:2]] + [vm(*s) for s in slabs[2:]]
    scratch += [vm(n - 1, *s) for n, s in zip(near, after)] + [vm(*s) for s in after]
    scratch += [vm(n - 1, *s) for n, s in zip(far, ends)]
    scratch += [vf(16, D), vf(dp - 1, 16, D), vf(mp - 1, 16, D), vf(hid - 1, 16, D), vf(16, D), vf(16, D)]
    n = dp + mp + hid + 2 * mp + 5 * (dp + mp + hid + 1) + 8
    scratch += [pltpu.SemaphoreType.DMA((4 * PAIRS + 4,)), pltpu.SemaphoreType.DMA((n,)), pltpu.SemaphoreType.DMA((n,))]
    hbm = pl.BlockSpec(memory_space=pl.ANY)
    vmem = pl.BlockSpec(memory_space=pltpu.VMEM)
    return pl.pallas_call(
        backward_kernel,
        out_shape=out_shape,
        in_specs=[hbm] * 6 + [vmem] * 3 + [hbm] * 4 + [vmem] * 4,
        out_specs=(hbm, hbm) + (vmem,) * 6,
        scratch_shapes=scratch,
        compiler_params=params(collective_id=1, has_side_effects=True),
        name="backward",
    )(o, dw2, dwe, dwr, qkv, do, lse, key_col, seg_row, ft, w1, et, dmid, cols, dbe, dbf, dgs)


def local(
    stored, positions, segments, present, norm_gains, norm_biases, input_proj, input_bias, output_proj,
    output_bias, expand_weight, expand_bias, reduce_weight, reduce_bias, cotangent,
):
    mp, hid, dp = lax.axis_size("mp"), lax.axis_size("hidden"), lax.axis_size("dp")
    m, h, d = lax.axis_index("mp"), lax.axis_index("hidden"), lax.axis_index("dp")
    rows_mp, hcols, fcols = D // mp, D // hid, expand_weight.shape[1]
    half = rows_mp // dp
    cols = [norm_gains[0], norm_biases[0], norm_gains[1], norm_biases[1], output_bias.astype(F32), reduce_bias.astype(F32)]
    cols = jnp.pad(jnp.stack(cols, axis=1), ((0, 0), (0, 128 - len(cols))))
    rows = jnp.concatenate(
        [
            expand_bias.astype(F32)[None],
            jnp.pad(input_bias.astype(F32), ((0, 0), (0, fcols - hcols))),
            jnp.zeros((5, fcols), F32),
        ]
    )
    w1 = lax.dynamic_slice_in_dim(input_proj, d * half, half, 0)
    w2 = lax.dynamic_slice_in_dim(output_proj, d * (hcols // dp), hcols // dp, 0)
    pos = lax.dynamic_slice_in_dim(positions, m * SEQ, SEQ).astype(F32)[None]
    rate = jnp.exp(jnp.arange(D // 2, dtype=jnp.int32).astype(F32) * (-math.log(10000.0) / (D // 2)))[:, None]
    key_col = jnp.where(present == 1, segments, -1)[:, None]
    seg_row = segments[None, :]
    et, ft, w1f, qkv, at, lse, ct, w2n, we, wr, cols, rows = forward(
        stored, cotangent, w1[:, :2].reshape(half, 2 * hcols), w1[:, 2], w2, expand_weight, reduce_weight, cols, rows,
        pos, rate, key_col, seg_row,
    )
    w2n = w2n.reshape(mp, D, rows_mp)
    we, wr = we.reshape(D, hid * fcols), wr.reshape(D, hid * fcols)
    be = rows[:, 0].reshape(1, hid * fcols)
    out_t, dmid, do, dwr, dwe, dbe, dw2, dbf, dgs = feed(at, et, ct, w2n, cols, we, be, wr)
    output, d_stored, ga, gb, d_output, d_expand, d_reduce, vec = backward(
        out_t,
        dw2.reshape(mp, hid, dp, hcols // dp, rows_mp),
        dwe.reshape(mp, dp, half, hid * fcols),
        dwr.reshape(mp, dp, half, hid * fcols),
        qkv, do, lse, key_col, seg_row, ft, w1f, et, dmid, cols, dbe, dbf, dgs,
    )
    piece = D // (hid * mp * dp)
    cut = lambda x, at, size: lax.dynamic_slice_in_dim(x, at * size, size, x.ndim - 1)
    dg = cut(vec[:4].reshape(2, 2, D), (m * dp + d) * hid + h, piece)
    db_proj = cut(vec[4:6], h * dp + d, hcols // dp)
    db_feed = cut(vec[6:8], m * dp + d, half)
    dbe = cut(vec[8:].reshape(-1)[: hid * fcols], h * dp + d, fcols // dp)
    d_input = jnp.concatenate([ga.reshape(half, 2, hcols), gb[:, None]], axis=1)
    return (
        output, d_stored.astype(F32), dg[:, 0], dg[:, 1], d_input, db_proj, d_output, db_feed[1], d_expand, dbe, d_reduce,
        db_feed[0],
    )


def solution(mesh):
    placed = (
        P("mp", ("dp", "hidden")),
        P(("dp", "hidden")),
        P(("dp", "hidden", "mp")),
        P(("dp", "hidden", "mp")),
        P(None, "mp"),
        P(None, "mp"),
        P("mp", None, "hidden"),
        P(None, "hidden"),
        P("hidden", "mp"),
        P("mp"),
        P("mp", "hidden"),
        P("hidden"),
        P("mp", "hidden"),
        P("mp"),
        P("mp", ("dp", "hidden")),
    )
    return jax.shard_map(
        local,
        mesh=mesh,
        in_specs=placed,
        out_specs=(
            P("mp", ("dp", "hidden")),
            P("mp", ("dp", "hidden")),
            P(None, ("mp", "dp", "hidden")),
            P(None, ("mp", "dp", "hidden")),
            P(("mp", "dp"), None, "hidden"),
            P(None, ("hidden", "dp")),
            P(("hidden", "dp"), "mp"),
            P(("mp", "dp")),
            P(("mp", "dp"), "hidden"),
            P(("hidden", "dp")),
            P(("mp", "dp"), "hidden"),
            P(("mp", "dp")),
        ),
        check_vma=False,
    )
```

```python
import functools
import math

import jax
import jax.numpy as jnp
from jax import lax
from jax.experimental import pallas as pl
from jax.experimental.pallas import tpu as pltpu
from jax.sharding import PartitionSpec as P

D = 768
HEADS = 12
HD = 64
SEQ = 1024
QBB = 512
PAIR = 2 * HD
PAIRS = HEADS // 2
EPS = 1e-06
MASKED = -1e30
F32 = jnp.float32
BF16 = jnp.bfloat16
VMEM_LIMIT = 60 * 1024 * 1024
PI_2 = (1.5703125, 4.837512969970703125e-4, 7.549789948768648e-8)

NN = (((1,), (0,)), ((), ()))
NT = (((1,), (1,)), ((), ()))


def mm(a, b, dims=NN):
    return lax.dot_general(a, b, dims, preferred_element_type=F32)


def whole(shape):
    return pl.BlockSpec(shape, lambda *_: (0,) * len(shape), pipeline_mode=pl.Buffered(1))


def params(**kw):
    return pltpu.CompilerParams(vmem_limit_bytes=VMEM_LIMIT, **kw)


def lane_sums(x):
    total = x[:, 0:128]
    for j in range(1, x.shape[1] // 128):
        total = total + x[:, j * 128 : (j + 1) * 128]
    return total


def norm_stats(e):
    average = jnp.sum(e, axis=0, keepdims=True) * (1.0 / D)
    spread = jnp.sum(e * e, axis=0, keepdims=True) * (1.0 / D) - average * average
    return average, lax.rsqrt(spread + EPS)


def fill_bias(bias_ref, key_ref, seg_ref):
    def rows_of(i, _):
        rows = pl.ds(pl.multiple_of(i * 256, 256), 256)
        same = key_ref[rows, :] == seg_ref[...]
        row_id = lax.broadcasted_iota(jnp.int32, (256, SEQ), 0) + i * 256
        col_id = lax.broadcasted_iota(jnp.int32, (256, SEQ), 1)
        bias_ref[rows, :] = jnp.where(same | (row_id == col_id), 0.0, MASKED)
        return 0

    lax.fori_loop(0, SEQ // 256, rows_of, 0)


MESH = pl.DeviceIdType.MESH


class Wire:
    def __init__(self, send, recv):
        self.send_sem, self.recv_sem, self.count, self.sent = send, recv, 0, []
        self.me = (lax.axis_index("dp"), lax.axis_index("mp"), lax.axis_index("hidden"))
        self.size = (lax.axis_size("dp"), lax.axis_size("mp"), lax.axis_size("hidden"))

    def peer(self, axis, offset):
        where = list(self.me)
        where[axis] = lax.rem(where[axis] + offset, self.size[axis])
        return tuple(where)

    def origin(self, axis, offset):
        return lax.rem(self.me[axis] - offset + self.size[axis], self.size[axis])

    def meet(self):
        barrier = pltpu.get_barrier_semaphore()
        total = 0
        for axis in range(3):
            for offset in range(1, self.size[axis]):
                pl.semaphore_signal(barrier, 1, device_id=self.peer(axis, offset), device_id_type=MESH)
                total += 1
        pl.semaphore_wait(barrier, total)

    def send(self, src, dst, target):
        copy = pltpu.make_async_remote_copy(
            src, dst, self.send_sem.at[self.count], self.recv_sem.at[self.count], device_id=target, device_id_type=MESH
        )
        copy.start()
        self.count += 1
        self.sent.append(copy)
        return copy

    def keep(self, src, dst):
        copy = pltpu.make_async_copy(src, dst, self.send_sem.at[self.count])
        copy.start()
        self.count += 1
        return copy

    def finish(self):
        for copy in self.sent:
            copy.wait_send()


DP, MP, HID = 0, 1, 2


HALF = D // 2


def sin_cos(angles):
    turns = jnp.floor(angles * (2.0 / math.pi) + 0.5)
    r = ((angles - turns * PI_2[0]) - turns * PI_2[1]) - turns * PI_2[2]
    r2 = r * r
    s = r + r * r2 * (-1.6666654611e-1 + r2 * (8.3321608736e-3 + r2 * -1.9515295891e-4))
    c = 1.0 - 0.5 * r2 + r2 * r2 * (4.166664568298827e-2 + r2 * (-1.388731625493765e-3 + r2 * 2.443315711809948e-5))
    quarter = turns - 4.0 * jnp.floor(turns * 0.25)
    odd = (quarter == 1.0) | (quarter == 3.0)
    flip_s = quarter >= 2.0
    flip_c = (quarter == 1.0) | (quarter == 2.0)
    sine = jnp.where(odd, c, s)
    cosine = jnp.where(odd, s, c)
    return jnp.where(flip_s, -sine, sine), jnp.where(flip_c, -cosine, cosine)


def forward_kernel(
    x_ref, c_ref, w1a_ref, w1b_ref, w2_ref, we_ref, wr_ref, cols_ref, rows_ref, pos_ref, rate_ref, key_ref, seg_ref,
    et_out, ft_out, w1_out, qkv_out, out_out, dmid_out, do_out, dwr_out, dwe_out, wef_ref, wrf_ref,
    lse_ref, p_ref, dbe_ref, dw2_ref, dbf_ref, dgs_ref,
    xt, ct, w1af, w1bf, w2f, rowsf, tab, et, ft, f, w1, qkv, bias, vt, wb, at, out, wblk, dblk, w2c,
    send, recv, z_send, z_recv, p_send, p_recv, c_send, c_recv, local,
):
    wire = Wire(send, recv)
    d, m, h = wire.me
    dp, mp, hid = wire.size
    rows = D // mp
    wide = D // hid
    fcols = we_ref.shape[1]
    half = rows // dp
    offset = pl.multiple_of(d * half, half)
    own = (
        (w1a_ref, lambda mm_, hh: w1af.at[hh, mm_, d], lambda: w1af.at[:, :, d], HID),
        (w1b_ref, lambda mm_, hh: w1bf.at[hh, mm_, d], lambda: w1bf.at[:, :, d], MP),
        (w2_ref, lambda mm_, hh: w2f.at[mm_, hh, d], lambda: w2f.at[:, :, d], HID),
    )
    wire.meet()
    waits, stored = [], []
    first, second, third = {}, {}, {}

    def swap(src_ref, dst_ref):
        mine = pl.ds(pl.multiple_of(m * rows, rows), rows)
        moved = []
        for q in range(1, mp):
            to = wire.peer(MP, q)
            moved.append(wire.send(src_ref.at[:, pl.ds(pl.multiple_of(to[1] * SEQ, SEQ), SEQ)], dst_ref.at[mine], to))
        return moved, wire.keep(src_ref.at[:, pl.ds(pl.multiple_of(m * SEQ, SEQ), SEQ)], dst_ref.at[mine])

    def landed(pair):
        for copy in pair[0]:
            copy.wait_recv()
        pair[1].wait()

    def stage_one(i):
        src, dst, _, axis = own[i]
        first[i] = [wire.keep(src, dst(m, h))]
        first[i] += [wire.send(src, dst(m, h), wire.peer(axis, o)) for o in range(1, wire.size[axis])]

    def stage_two(i):
        _, dst, _, axis = own[i]
        other = MP if axis == HID else HID
        second[i] = []
        for o, copy in enumerate(first[i]):
            if o == 0:
                copy.wait()
            else:
                copy.wait_recv()
            at_ = wire.origin(axis, o)
            piece = dst(m, at_) if axis == HID else dst(at_, h)
            second[i] += [wire.send(piece, piece, wire.peer(other, q)) for q in range(1, wire.size[other])]

    def stage_three(i):
        for copy in second[i]:
            copy.wait_recv()
        third[i] = [wire.send(own[i][2](), own[i][2](), wire.peer(DP, r)) for r in range(1, dp)]

    def done(i):
        for copy in third[i]:
            copy.wait_recv()

    full = (wef_ref, wrf_ref)
    part = (we_ref.at[pl.ds(offset, half)], wr_ref.at[pl.ds(offset, half)])

    def plane_of(o):
        return lax.rem(h - o + hid, hid)

    def piece(j, mm_, dd, o):
        at_ = pl.ds(pl.multiple_of(mm_ * rows + dd * half, half), half)
        return full[j].at[at_, pl.ds(pl.multiple_of(plane_of(o) * fcols, fcols), fcols)]

    def remote(src, dst, sems, target):
        return pltpu.make_async_remote_copy(src, dst, sems[0], sems[1], device_id=target, device_id_type=MESH)

    def to_plane(j, o, q):
        src = part[j] if isinstance(o, int) and o == 0 else piece(j, m, d, o)
        return remote(src, piece(j, m, d, o), (p_send.at[j, o, q], p_recv.at[j, o, q]), wire.peer(MP, q))

    def to_depth(j, o, k):
        if j == 0:
            src, dst = part[0], piece(0, m, d, 0)
        else:
            src = dst = piece(1, k, d, 0)
        return remote(src, dst, (z_send.at[j, o, k], z_recv.at[j, o, k]), wire.peer(HID, o))

    def to_core(j, o, k, r):
        return remote(
            piece(j, k, d, o), piece(j, k, d, o), (c_send.at[j, o, k, r], c_recv.at[j, o, k, r]), wire.peer(DP, r)
        )

    depth_count = (1, mp)

    def keep_own(j):
        return pltpu.make_async_copy(part[j], piece(j, m, d, 0), local.at[j])

    def expand_plane(o):
        if not (isinstance(o, int) and o == 0):
            to_depth(0, o, 0).wait_recv()
        for q in range(1, mp):
            to_plane(0, o, q).start()

    def reduce_depth():
        for q in range(1, mp):
            to_plane(1, 0, q).wait_recv()
        keep_own(1).wait()
        for o in range(1, hid):
            for k in range(mp):
                to_depth(1, o, k).start()

    def cores(o):
        zero = isinstance(o, int) and o == 0
        if zero:
            keep_own(0).wait()
        else:
            for k in range(mp):
                to_depth(1, o, k).wait_recv()
        for q in range(1, mp):
            to_plane(0, o, q).wait_recv()
        for j in range(2):
            for k in range(mp):
                for r in range(1, dp):
                    to_core(j, o, k, r).start()

    def arrived(o):
        for j in range(2):
            for k in range(mp):
                for r in range(1, dp):
                    to_core(j, o, k, r).wait_recv()

    mine = pl.ds(pl.multiple_of(m * rows, rows), rows)
    small = [wire.send(cols_ref, p_ref.at[mine], wire.peer(MP, q)) for q in range(1, mp)]
    small += [wire.send(rows_ref, rowsf.at[h], wire.peer(HID, o)) for o in range(1, hid)]
    kept = [wire.keep(cols_ref, p_ref.at[mine]), wire.keep(rows_ref, rowsf.at[h])]
    stage_one(0)
    stage_one(1)
    x_in = swap(x_ref, xt)

    def table_rows(j, _):
        at_ = pl.ds(pl.multiple_of(j * 64, 64), 64)
        sine, cosine = sin_cos(rate_ref[at_, :] * pos_ref[...])
        tab[at_, :] = sine
        tab[pl.ds(pl.multiple_of(j * 64 + HALF, 64), 64), :] = cosine
        return 0

    lax.fori_loop(0, 2, table_rows, 0)
    stage_two(0)
    stage_two(1)
    stage_one(2)
    for j in range(2):
        keep_own(j).start()
    for o in range(1, hid):
        to_depth(0, o, 0).start()
    for q in range(1, mp):
        to_plane(1, 0, q).start()
    lax.fori_loop(2, HALF // 64, table_rows, 0)
    fill_bias(bias, key_ref, seg_ref)
    c_in = swap(c_ref, ct)
    expand_plane(0)
    for copy in small:
        copy.wait_recv()
    for copy in kept:
        copy.wait()
    wb[...] = jnp.zeros_like(wb)
    for hh in range(hid):
        wb[:, hh * wide : (hh + 1) * wide] = rowsf[hh, 1:2, :wide]
        wb[:, 2 * D + hh * wide : 2 * D + (hh + 1) * wide] = rowsf[hh, 2:3, :wide]
    landed(x_in)

    def norm_cols(j, _):
        cols = pl.ds(pl.multiple_of(j * 256, 256), 256)
        e = xt[:, cols].astype(F32) + tab[:, cols]
        et[:, cols] = e
        average, inv = norm_stats(e)
        low = ((e - average) * inv * p_ref[:, 0:1] + p_ref[:, 1:2]).astype(BF16)
        ft[:, cols] = low
        f[cols, :] = low.T
        return 0

    lax.fori_loop(0, SEQ // 256, norm_cols, 0)
    stored += [wire.keep(et, et_out), wire.keep(ft, ft_out)]
    stage_three(0)
    stage_three(1)
    stage_two(2)
    reduce_depth()
    done(0)
    done(1)
    for hh in range(hid):
        for mm_ in range(mp):
            for dd in range(dp):
                at_ = slice(mm_ * rows + dd * half, mm_ * rows + (dd + 1) * half)
                for k in range(3):
                    if k < 2:
                        value = w1af[hh, mm_, dd, :, k * wide : (k + 1) * wide]
                    else:
                        value = w1bf[hh, mm_, dd]
                    w1[at_, k * D + hh * wide : k * D + (hh + 1) * wide] = value
    stored.append(wire.keep(w1, w1_out))
    for o in range(1, hid):
        expand_plane(o)

    def cols_of(n, scale):
        cols = pl.ds(pl.multiple_of(n * 256, 256), 256)
        y = (mm(f[...], w1[:, cols]) + wb[:, cols]).astype(BF16)
        qkv[:, cols] = y * jnp.asarray(scale, BF16)
        return 0

    lax.fori_loop(0, D // 256, lambda n, c: cols_of(n, HD**-0.5), 0)
    lax.fori_loop(D // 256, 3 * D // 256, lambda n, c: cols_of(n, 1.0), 0)
    stored.append(wire.keep(qkv, qkv_out))

    low = lax.broadcasted_iota(jnp.int32, (SEQ, PAIR), 1) < HD
    lse_ref[...] = jnp.zeros_like(lse_ref)

    def pair_of(p, _):
        lanes = pl.ds(pl.multiple_of(p * PAIR, PAIR), PAIR)
        k_lanes = pl.ds(pl.multiple_of(p * PAIR + D, PAIR), PAIR)
        v_lanes = pl.ds(pl.multiple_of(p * PAIR + 2 * D, PAIR), PAIR)
        vt[...] = qkv[:, v_lanes].T
        q = qkv[:, lanes]
        for hh in range(2):
            qm = jnp.where(low if hh == 0 else ~low, q, jnp.zeros_like(q))
            s = mm(qkv[:, k_lanes], qm, NT) + bias[...]
            top = jnp.max(s, axis=0, keepdims=True)
            e = jnp.exp(s - top)
            total = jnp.sum(e, axis=0, keepdims=True)
            o = mm(vt[hh * HD : (hh + 1) * HD, :], e.astype(BF16)) / total
            at[pl.ds(pl.multiple_of(p * PAIR + hh * HD, HD), HD), :] = o.astype(BF16)
            lse_ref[p, hh : hh + 1, :] = top + jnp.log(total)
        return 0

    lax.fori_loop(0, PAIRS // 2, pair_of, 0)
    stage_three(2)
    cores(0)
    lax.fori_loop(PAIRS // 2, PAIRS, pair_of, 0)
    for copy in stored:
        copy.wait()
    landed(c_in)
    done(2)

    ot, ds_sum, st, bt, mid = bias.at[pl.ds(0, D)], tab, xt, ft, et
    tokens = [pl.ds(n * D, D) for n in range(3)]
    for mm_ in range(mp):
        for hh in range(hid):
            for dd in range(dp):
                at_ = hh * wide + dd * (wide // dp)
                w2c[at_ : at_ + wide // dp, mm_ * rows : (mm_ + 1) * rows] = w2f[mm_, hh, dd]
    w2t = w2c[...].T

    def middle_cols(j, _):
        cols = pl.ds(pl.multiple_of(j * 256, 256), 256)
        value = et[:, cols] + (mm(w2t, at[:, cols]) + p_ref[:, 4:5])
        mid[:, cols] = value
        ot[:, cols] = value + p_ref[:, 5:6]
        average, inv = norm_stats(value)
        s = ((value - average) * inv * p_ref[:, 2:3] + p_ref[:, 3:4]).astype(BF16)
        st[:, cols] = s
        qkv[cols, tokens[0]] = s.T
        qkv[cols, tokens[1]] = ct[:, cols].T
        return 0

    lax.fori_loop(0, SEQ // 256, middle_cols, 0)
    ds_sum[...] = jnp.zeros_like(ds_sum)

    def fetch(j, o):
        hcols = pl.ds(pl.multiple_of(plane_of(o) * fcols, fcols), fcols)
        return pltpu.make_async_copy(full[j].at[:, hcols], wblk.at[j], local.at[2 + j])

    def put(j, o):
        hcols = pl.ds(pl.multiple_of(plane_of(o) * fcols, fcols), fcols)
        return pltpu.make_async_copy(dblk.at[j], (dwr_out, dwe_out)[j].at[:, hcols], local.at[4 + j])

    def block(o, _):
        hh = plane_of(o)
        arrived(o)
        for j in range(2):
            fetch(j, o).start()
        for j in range(2):
            fetch(j, o).wait()

        @pl.when(o + 1 < hid)
        def _():
            cores(o + 1)

        pre = mm(qkv[:, tokens[0]], wblk[0]) + rowsf[hh, 0:1, :]
        cdf = 0.5 * (1.0 + lax.erf(pre * (1.0 / math.sqrt(2.0))))
        act = (pre * cdf).astype(BF16)
        slope = cdf + pre * jnp.exp(-0.5 * pre * pre) * (1.0 / math.sqrt(2.0 * math.pi))
        grad = (mm(qkv[:, tokens[1]], wblk[1]) * slope).astype(BF16)

        @pl.when(o > 0)
        def _():
            for j in range(2):
                put(j, o - 1).wait()

        dblk[0] = mm(ct[...], act).astype(BF16)
        dblk[1] = mm(st[...], grad).astype(BF16)
        for j in range(2):
            put(j, o).start()
        dbe_ref[hh, 0:1, :] = jnp.sum(grad.astype(F32), axis=0, keepdims=True)
        ot[...] += mm(wblk[1], act, NT)
        ds_sum[...] += mm(wblk[0], grad, NT)
        return 0

    lax.fori_loop(0, hid, block, 0)
    dgs_ref[...] = jnp.zeros_like(dgs_ref)

    def back_cols(j, _):
        cols = pl.ds(pl.multiple_of(j * 256, 256), 256)
        value = mid[:, cols]
        out[:, cols] = ot[:, cols].astype(BF16)
        average, inv = norm_stats(value)
        normed = (value - average) * inv
        ds = ds_sum[:, cols]
        scaled = ds * p_ref[:, 2:3]
        total = jnp.sum(scaled, axis=0, keepdims=True) * (1.0 / D)
        crossed = jnp.sum(scaled * normed, axis=0, keepdims=True) * (1.0 / D)
        dmid = ct[:, cols].astype(F32) + inv * (scaled - total - normed * crossed)
        mid[:, cols] = dmid
        low_ = dmid.astype(BF16)
        bt[:, cols] = low_
        qkv[cols, tokens[2]] = mm(w2c[...], low_).astype(BF16).T
        dgs_ref[0] += lane_sums(ds * normed)
        dgs_ref[1] += lane_sums(ds)
        return 0

    lax.fori_loop(0, SEQ // 256, back_cols, 0)
    last = [wire.keep(out, out_out), wire.keep(mid, dmid_out), wire.keep(qkv.at[:, tokens[2]], do_out)]
    ones = jnp.ones((8, SEQ), BF16)
    dbf_ref[0] = mm(ones, ct[...], NT)
    dbf_ref[1] = mm(ones, bt[...], NT)
    for j in range(mp):
        dw2_ref[j] = mm(at[...], bt[j * rows : (j + 1) * rows, :], NT).astype(BF16)
    for j in range(2):
        put(j, hid - 1).wait()
    for copy in last:
        copy.wait()
    wire.finish()
    for j in range(2):
        for o in range(hid):
            if o:
                for k in range(depth_count[j]):
                    to_depth(j, o, k).wait_send()
            if o == 0 or j == 0:
                for q in range(1, mp):
                    to_plane(j, o, q).wait_send()
            for k in range(mp):
                for r in range(1, dp):
                    to_core(j, o, k, r).wait_send()


def forward(x, c, w1a, w1b, w2, we, wr, cols, rows, pos, rate, key_col, seg_row):
    dp, mp, hid = lax.axis_size("dp"), lax.axis_size("mp"), lax.axis_size("hidden")
    half = D // mp // dp
    fc = we.shape[1]
    ff = hid * fc
    sds = jax.ShapeDtypeStruct
    out_shape = (
        sds((D, SEQ), F32), sds((D, SEQ), BF16), sds((D, 3 * D), BF16), sds((SEQ, 3 * D), BF16),
        sds((D, SEQ), BF16), sds((D, SEQ), F32), sds((SEQ, D), BF16), sds((D, ff), BF16), sds((D, ff), BF16),
        sds((D, ff), BF16), sds((D, ff), BF16),
        sds((PAIRS, 8, SEQ), F32), sds((D, cols.shape[1]), F32), sds((hid, 8, fc), F32), sds((mp, D, D // mp), BF16),
        sds((2, 8, D), F32), sds((2, D, 128), F32),
    )
    n = 4 * mp + hid + 3 * (hid + mp + hid * mp + dp) + 16
    hbm = pl.BlockSpec(memory_space=pl.ANY)
    vmem = pl.BlockSpec(memory_space=pltpu.VMEM)
    vm = lambda dtype, *shape: pltpu.VMEM(shape, dtype)
    sem = lambda *shape: pltpu.SemaphoreType.DMA(shape)
    return pl.pallas_call(
        forward_kernel,
        out_shape=out_shape,
        in_specs=[hbm] * 9 + [vmem] * 4,
        out_specs=(hbm,) * 11 + (vmem,) * 6,
        scratch_shapes=[
            vm(BF16, D, SEQ), vm(BF16, D, SEQ), vm(BF16, hid, mp, dp, half, w1a.shape[1]),
            vm(BF16, hid, mp, dp, half, w1b.shape[1]), vm(BF16, mp, hid, dp, *w2.shape), vm(F32, hid, *rows.shape),
            vm(F32, D, SEQ), vm(F32, D, SEQ), vm(BF16, D, SEQ), vm(BF16, SEQ, D), vm(BF16, D, 3 * D),
            vm(BF16, SEQ, 3 * D), vm(F32, SEQ, SEQ), vm(BF16, PAIR, SEQ), vm(F32, 1, 3 * D),
            vm(BF16, D, SEQ), vm(BF16, D, SEQ), vm(BF16, 2, D, fc), vm(BF16, 2, D, fc), vm(BF16, D, D),
            sem(n), sem(n), sem(2, hid, mp), sem(2, hid, mp), sem(2, hid, mp), sem(2, hid, mp),
            sem(2, hid, mp, dp), sem(2, hid, mp, dp), sem(6),
        ],
        compiler_params=params(collective_id=0, has_side_effects=True),
        name="forward",
    )(x, c, w1a, w1b, w2, we, wr, cols, rows, pos, rate, key_col, seg_row)


def backward_kernel(
    o_ref, dw2_ref, dwe_ref, dwr_ref, qkv_in, do_in, lse_ref, key_ref, seg_ref, ft_in, w_in, et_in, dmid_in, p_ref,
    dbe_ref, dbf_ref, dgs_ref,
    of_ref, xf_ref, ga_ref, gb_ref, g2_ref, ge_ref, gr_ref, vecf_ref,
    qkv, do, bias, kt, dqt, dk, dv, dka, dva, ft, et, dmid, dgp,
    a0, a1, a2, a3, a4, o0, o1, s2, s3, s4, b0, b1, b2, b3, b4, t0, t1, t2, t3, t4, c0, c1, c2, c3, c4,
    v0, va, vb, vc, v1, v2, loads, send, recv,
):
    wire = Wire(send, recv)
    d, m, h = wire.me
    dp, mp, hid = wire.size
    rows = D // mp
    wide = D // hid
    half = rows // dp
    fcols = ge_ref.shape[1]
    v_in = (va, vb, vc)
    hslice = lambda hh: pl.ds(pl.multiple_of(hh * fcols, fcols), fcols)

    def load(n, src, dst):
        copy = pltpu.make_async_copy(src, dst, loads.at[n])
        copy.start()
        return copy

    parts = []
    for p in range(PAIRS):
        got = []
        for k in range(3):
            lanes = slice(k * D + p * PAIR, k * D + (p + 1) * PAIR)
            got.append(load(4 * p + k, qkv_in.at[:, lanes], qkv.at[:, lanes]))
        lanes = slice(p * PAIR, (p + 1) * PAIR)
        got.append(load(4 * p + 3, do_in.at[:, lanes], do.at[:, lanes]))
        parts.append(got)
    others = [load(4 * PAIRS + i, a, b) for i, (a, b) in enumerate(((ft_in, ft), (et_in, et), (dmid_in, dmid)))]
    wire.meet()
    items = (
        (lambda dd: o0.at[dd], a0, o0.at[d], b0, t0, c0, ga_ref, MP, HID),
        (lambda dd: o1.at[dd], a1, o1.at[d], b1, t1, c1, gb_ref, HID, HID),
        (lambda dd: dw2_ref.at[:, :, dd], a2, s2, b2, t2, c2, g2_ref, MP, MP),
        (lambda dd: dwe_ref.at[:, dd], a3, s3, b3, t3, c3, ge_ref, MP, None),
        (lambda dd: dwr_ref.at[:, dd], a4, s4, b4, t4, c4, gr_ref, HID, None),
    )
    core, kept, near, far = {}, {}, {}, {}

    def stage_core(i):
        src, a, s = items[i][:3]
        core[i] = [wire.send(src(wire.peer(DP, r)[0]), a.at[r - 1], wire.peer(DP, r)) for r in range(1, dp)]
        if i > 1:
            kept[i] = wire.keep(src(d), s)

    def add_all(dst, own, others, shape):
        lead = shape[:-2]

        def body(n, _):
            index = []
            for size in reversed(lead):
                index.insert(0, lax.rem(n, size))
                n = lax.div(n, size)
            index = tuple(index)
            value = own[index].astype(F32)
            for j in range(others.shape[0]):
                value = value + others[(j,) + index].astype(F32)
            dst[index] = value.astype(dst.dtype)
            return 0

        lax.fori_loop(0, math.prod(lead), body, 0)

    def part(i, ref, axis, at, leads):
        if items[i][8] is None:
            return ref.at[(slice(None),) * len(leads) + (slice(None), hslice(at))] if axis == HID else ref.at[at]
        return ref.at[at] if leads[0] == axis else ref.at[:, at]

    def leads_of(i):
        lead = items[i][8]
        return (MP,) if lead is None else ((HID, MP) if lead == HID else (MP, HID))

    def stage_near(i):
        _, a, s, b, t, c, g, axis, _ = items[i]
        for copy in core[i]:
            copy.wait_recv()
        if i in kept:
            kept[i].wait()
        add_all(s, s, a, s.shape)
        near[i] = [
            wire.send(part(i, s, axis, wire.peer(axis, q)[axis], leads_of(i)), b.at[q - 1], wire.peer(axis, q))
            for q in range(1, wire.size[axis])
        ]

    def stage_far(i):
        _, a, s, b, t, c, g, axis, lead = items[i]
        for copy in near[i]:
            copy.wait_recv()
        add_all(t, part(i, s, axis, wire.me[axis], leads_of(i)), b, t.shape)
        other = MP if axis == HID else HID
        left = tuple(x for x in leads_of(i) if x != axis)
        far[i] = []
        for q in range(1, wire.size[other]):
            to = wire.peer(other, q)
            far[i].append(wire.send(part(i, t, other, to[other], left), c.at[q - 1], to))

    def stage_end(i):
        _, a, s, b, t, c, g, axis, lead = items[i]
        other = MP if axis == HID else HID
        left = tuple(x for x in leads_of(i) if x != axis)
        for copy in far[i]:
            copy.wait_recv()
        value = part(i, t, other, wire.me[other], left)[...].astype(F32)
        for j in range(c.shape[0]):
            value = value + c[j].astype(F32)
        g[...] = value

    moved, held = [], []

    def swap(src_ref, dst_ref):
        mine = pl.ds(pl.multiple_of(m * SEQ, SEQ), SEQ)
        for q in range(1, mp):
            to = wire.peer(MP, q)
            moved.append(wire.send(src_ref.at[pl.ds(pl.multiple_of(to[1] * rows, rows), rows)], dst_ref.at[:, mine], to))
        held.append(wire.keep(src_ref.at[pl.ds(pl.multiple_of(m * rows, rows), rows)], dst_ref.at[:, mine]))

    vec = {}

    def vec_send(axis, src):
        vec[axis] = [wire.send(src, v_in[axis].at[o - 1], wire.peer(axis, o)) for o in range(1, wire.size[axis])]

    def vec_sum(axis, src, dst):
        for copy in vec[axis]:
            copy.wait_recv()
        total = src[...]
        for j in range(wire.size[axis] - 1):
            total = total + v_in[axis][j]
        dst[...] = total

    for i in (4, 3, 2):
        stage_core(i)
    swap(o_ref, of_ref)
    fill_bias(bias, key_ref, seg_ref)
    low = lax.broadcasted_iota(jnp.int32, (QBB, PAIR), 1) < HD

    def pair_of(p, _):
        off = pl.multiple_of(p * PAIR, PAIR)
        lanes = pl.ds(off, PAIR)
        k_lanes = pl.ds(pl.multiple_of(off + D, PAIR), PAIR)
        v_lanes = pl.ds(pl.multiple_of(off + 2 * D, PAIR), PAIR)
        kt[...] = qkv[:, k_lanes].T
        dka[...] = jnp.zeros_like(dka)
        dva[...] = jnp.zeros_like(dva)

        def block(j, _):
            cols = pl.ds(pl.multiple_of(j * QBB, QBB), QBB)
            q = qkv[cols, lanes]
            g = do[cols, lanes]
            for hh in range(2):
                keep = low if hh == 0 else ~low
                qm = jnp.where(keep, q, jnp.zeros_like(q))
                gm = jnp.where(keep, g, jnp.zeros_like(g))
                e = jnp.exp(mm(qkv[:, k_lanes], qm, NT) + bias[:, cols] - lse_ref[p, hh : hh + 1, cols])
                t = e * mm(qkv[:, v_lanes], gm, NT)
                ds = (t - e * jnp.sum(t, axis=0, keepdims=True)).astype(BF16)
                dva[...] += mm(e.astype(BF16), gm)
                dka[...] += mm(ds, qm)
                dq = mm(kt[hh * HD : (hh + 1) * HD, :], ds) * HD**-0.5
                dqt[pl.ds(pl.multiple_of(off + hh * HD, HD), HD), cols] = dq.astype(BF16)
            return 0

        lax.fori_loop(0, SEQ // QBB, block, 0)
        dk[:, lanes] = dka[...].astype(BF16)
        dv[:, lanes] = dva[...].astype(BF16)
        return 0

    def pairs(first, last):
        for p in range(first, last):
            for copy in parts[p]:
                copy.wait()
        lax.fori_loop(first, last, pair_of, 0)

    pairs(0, 2)
    stage_near(4)
    stage_near(3)
    stage_near(2)
    pairs(2, PAIRS)
    w1 = qkv.at[pl.ds(0, D)]
    w_load = load(4 * PAIRS + 3, w_in, w1)
    for copy in others:
        copy.wait()

    for hh in range(hid):
        for k in range(3):
            if k == 0:
                value = mm(ft[...], dqt[hh * wide : (hh + 1) * wide, :], NT).astype(BF16)
            else:
                value = mm(ft[...], (dk, dv)[k - 1][:, hh * wide : (hh + 1) * wide]).astype(BF16)
            for mm_ in range(mp):
                for dd in range(dp):
                    piece = value[mm_ * rows + dd * half : mm_ * rows + (dd + 1) * half, :]
                    if k < 2:
                        o0[dd, hh, mm_, :, k * wide : (k + 1) * wide] = piece
                    else:
                        o1[dd, hh, mm_] = piece
    stage_core(1)
    stage_core(0)
    df = bias.at[pl.ds(0, D)]
    w_load.wait()
    dx = ft

    def feature_cols(j, _):
        cols = pl.ds(pl.multiple_of(j * 256, 256), 256)
        value = mm(w1[:, 0:D], dqt[:, cols])
        value += mm(w1[:, D : 2 * D], dk[cols, :], NT)
        value += mm(w1[:, 2 * D : 3 * D], dv[cols, :], NT)
        df[:, cols] = value
        return 0

    lax.fori_loop(0, SEQ // 256, feature_cols, 0)
    stage_near(1)
    stage_near(0)
    dgp[...] = jnp.zeros_like(dgp)

    def norm_cols(j, _):
        cols = pl.ds(pl.multiple_of(j * 256, 256), 256)
        e = et[:, cols]
        average, inv = norm_stats(e)
        normed = (e - average) * inv
        g = df[:, cols]
        scaled = g * p_ref[:, 0:1]
        total = jnp.sum(scaled, axis=0, keepdims=True) * (1.0 / D)
        crossed = jnp.sum(scaled * normed, axis=0, keepdims=True) * (1.0 / D)
        dx[:, cols] = (dmid[:, cols] + inv * (scaled - total - normed * crossed)).astype(BF16)
        dgp[0] += lane_sums(g * normed)
        dgp[1] += lane_sums(g)
        return 0

    lax.fori_loop(0, SEQ // 256, norm_cols, 0)
    swap(dx, xf_ref)
    for i in (3, 2, 4):
        stage_far(i)
    ones = jnp.ones((8, SEQ), BF16)
    v0[...] = jnp.zeros_like(v0)
    for n in range(2):
        v0[n : n + 1, :] = jnp.sum(dgp[n].T, axis=0, keepdims=True)
        v0[2 + n : 3 + n, :] = jnp.sum(dgs_ref[n].T, axis=0, keepdims=True)
        v0[6 + n : 7 + n, :] = dbf_ref[n, 0:1, :]
    v0[4:5, :] = mm(ones, dqt[...], NT)[0:1]
    v0[5:6, :] = mm(ones, dv[...])[0:1]
    for hh in range(hid):
        row, lane = divmod(hh * fcols, D)
        v0[8 + row : 9 + row, lane : lane + fcols] = dbe_ref[hh, 0:1, :]
    vec_send(DP, v0)
    vec_sum(DP, v0, v1)
    vec_send(MP, v1)
    stage_far(1)
    stage_far(0)
    vec_sum(MP, v1, v2)
    vec_send(HID, v2)
    stage_end(3)
    stage_end(2)
    stage_end(4)
    stage_end(1)
    stage_end(0)
    vec_sum(HID, v2, vecf_ref)
    for copy in held:
        copy.wait()
    for copy in moved:
        copy.wait_recv()
    wire.finish()


def backward(o, dw2, dwe, dwr, qkv, do, lse, key_col, seg_row, ft, w1, et, dmid, cols, dbe, dbf, dgs):
    dp, mp, hid = lax.axis_size("dp"), lax.axis_size("mp"), lax.axis_size("hidden")
    sds = jax.ShapeDtypeStruct
    wide = D // hid
    half = D // mp // dp
    half2, c2 = dw2.shape[3:]
    ff = dwe.shape[3]
    fc = ff // hid
    out_shape = (
        sds((D // mp, mp * SEQ), BF16), sds((D // mp, mp * SEQ), BF16), sds((half, 2 * wide), F32),
        sds((half, wide), F32), sds((half2, c2), F32), sds((half, fc), F32), sds((half, fc), F32), sds((16, D), F32),
    )
    vm = lambda *shape: pltpu.VMEM(shape, BF16)
    vf = lambda *shape: pltpu.VMEM(shape, F32)
    slabs = (
        (hid, mp, half, 2 * wide), (hid, mp, half, wide), (mp, hid, half2, c2), (mp, half, ff), (mp, half, ff)
    )
    after = ((hid, half, 2 * wide), (mp, half, wide), (hid, half2, c2), (half, ff), (mp, half, fc))
    ends = ((half, 2 * wide), (half, wide), (half2, c2), (half, fc), (half, fc))
    near = (mp, hid, mp, mp, hid)
    far = (hid, mp, hid, hid, mp)
    scratch = [
        vm(SEQ, 3 * D), vm(SEQ, D), vf(SEQ, SEQ), vm(PAIR, SEQ), vm(D, SEQ), vm(SEQ, D), vm(SEQ, D),
        vf(SEQ, PAIR), vf(SEQ, PAIR), vm(D, SEQ), vf(D, SEQ), vf(D, SEQ), vf(2, D, 128),
    ]
    scratch += [vm(dp - 1, *s) for s in slabs]
    scratch += [vm(dp, *s) for s in slabs[:2]] + [vm(*s) for s in slabs[2:]]
    scratch += [vm(n - 1, *s) for n, s in zip(near, after)] + [vm(*s) for s in after]
    scratch += [vm(n - 1, *s) for n, s in zip(far, ends)]
    scratch += [vf(16, D), vf(dp - 1, 16, D), vf(mp - 1, 16, D), vf(hid - 1, 16, D), vf(16, D), vf(16, D)]
    n = dp + mp + hid + 2 * mp + 5 * (dp + mp + hid + 1) + 8
    scratch += [pltpu.SemaphoreType.DMA((4 * PAIRS + 4,)), pltpu.SemaphoreType.DMA((n,)), pltpu.SemaphoreType.DMA((n,))]
    hbm = pl.BlockSpec(memory_space=pl.ANY)
    vmem = pl.BlockSpec(memory_space=pltpu.VMEM)
    return pl.pallas_call(
        backward_kernel,
        out_shape=out_shape,
        in_specs=[hbm] * 6 + [vmem] * 3 + [hbm] * 4 + [vmem] * 4,
        out_specs=(hbm, hbm) + (vmem,) * 6,
        scratch_shapes=scratch,
        compiler_params=params(collective_id=1, has_side_effects=True),
        name="backward",
    )(o, dw2, dwe, dwr, qkv, do, lse, key_col, seg_row, ft, w1, et, dmid, cols, dbe, dbf, dgs)


def local(
    stored, positions, segments, present, norm_gains, norm_biases, input_proj, input_bias, output_proj,
    output_bias, expand_weight, expand_bias, reduce_weight, reduce_bias, cotangent,
):
    mp, hid, dp = lax.axis_size("mp"), lax.axis_size("hidden"), lax.axis_size("dp")
    m, h, d = lax.axis_index("mp"), lax.axis_index("hidden"), lax.axis_index("dp")
    rows_mp, hcols, fcols = D // mp, D // hid, expand_weight.shape[1]
    half = rows_mp // dp
    cols = [norm_gains[0], norm_biases[0], norm_gains[1], norm_biases[1], output_bias.astype(F32), reduce_bias.astype(F32)]
    cols = jnp.pad(jnp.stack(cols, axis=1), ((0, 0), (0, 128 - len(cols))))
    rows = jnp.concatenate(
        [
            expand_bias.astype(F32)[None],
            jnp.pad(input_bias.astype(F32), ((0, 0), (0, fcols - hcols))),
            jnp.zeros((5, fcols), F32),
        ]
    )
    w1 = lax.dynamic_slice_in_dim(input_proj, d * half, half, 0)
    w2 = lax.dynamic_slice_in_dim(output_proj, d * (hcols // dp), hcols // dp, 0)
    pos = lax.dynamic_slice_in_dim(positions, m * SEQ, SEQ).astype(F32)[None]
    rate = jnp.exp(jnp.arange(D // 2, dtype=jnp.int32).astype(F32) * (-math.log(10000.0) / (D // 2)))[:, None]
    key_col = jnp.where(present == 1, segments, -1)[:, None]
    seg_row = segments[None, :]
    et, ft, w1f, qkv, out_t, dmid, do, dwr, dwe, _, _, lse, cols, dbe, dw2, dbf, dgs = forward(
        stored, cotangent, w1[:, :2].reshape(half, 2 * hcols), w1[:, 2], w2, expand_weight, reduce_weight, cols, rows,
        pos, rate, key_col, seg_row,
    )
    output, d_stored, ga, gb, d_output, d_expand, d_reduce, vec = backward(
        out_t,
        dw2.reshape(mp, hid, dp, hcols // dp, rows_mp),
        dwe.reshape(mp, dp, half, hid * fcols),
        dwr.reshape(mp, dp, half, hid * fcols),
        qkv, do, lse, key_col, seg_row, ft, w1f, et, dmid, cols, dbe, dbf, dgs,
    )
    piece = D // (hid * mp * dp)
    cut = lambda x, at, size: lax.dynamic_slice_in_dim(x, at * size, size, x.ndim - 1)
    dg = cut(vec[:4].reshape(2, 2, D), (m * dp + d) * hid + h, piece)
    db_proj = cut(vec[4:6], h * dp + d, hcols // dp)
    db_feed = cut(vec[6:8], m * dp + d, half)
    dbe = cut(vec[8:].reshape(-1)[: hid * fcols], h * dp + d, fcols // dp)
    d_input = jnp.concatenate([ga.reshape(half, 2, hcols), gb[:, None]], axis=1)
    return (
        output, d_stored.astype(F32), dg[:, 0], dg[:, 1], d_input, db_proj, d_output, db_feed[1], d_expand, dbe, d_reduce,
        db_feed[0],
    )


def solution(mesh):
    placed = (
        P("mp", ("dp", "hidden")),
        P(("dp", "hidden")),
        P(("dp", "hidden", "mp")),
        P(("dp", "hidden", "mp")),
        P(None, "mp"),
        P(None, "mp"),
        P("mp", None, "hidden"),
        P(None, "hidden"),
        P("hidden", "mp"),
        P("mp"),
        P("mp", "hidden"),
        P("hidden"),
        P("mp", "hidden"),
        P("mp"),
        P("mp", ("dp", "hidden")),
    )
    return jax.shard_map(
        local,
        mesh=mesh,
        in_specs=placed,
        out_specs=(
            P("mp", ("dp", "hidden")),
            P("mp", ("dp", "hidden")),
            P(None, ("mp", "dp", "hidden")),
            P(None, ("mp", "dp", "hidden")),
            P(("mp", "dp"), None, "hidden"),
            P(None, ("hidden", "dp")),
            P(("hidden", "dp"), "mp"),
            P(("mp", "dp")),
            P(("mp", "dp"), "hidden"),
            P(("hidden", "dp")),
            P(("mp", "dp"), "hidden"),
            P(("mp", "dp")),
        ),
        check_vma=False,
    )
```

```python
import functools
import math

import jax
import jax.numpy as jnp
from jax import lax
from jax.experimental import pallas as pl
from jax.experimental.pallas import tpu as pltpu
from jax.sharding import PartitionSpec as P

D = 768
HEADS = 12
HD = 64
SEQ = 1024
QBB = 1024
PAIR = 2 * HD
PAIRS = HEADS // 2
EPS = 1e-06
MASKED = -1e30
F32 = jnp.float32
BF16 = jnp.bfloat16
VMEM_LIMIT = 60 * 1024 * 1024
PI_2 = (1.5703125, 4.837512969970703125e-4, 7.549789948768648e-8)

NN = (((1,), (0,)), ((), ()))
NT = (((1,), (1,)), ((), ()))


def mm(a, b, dims=NN):
    return lax.dot_general(a, b, dims, preferred_element_type=F32)


def whole(shape):
    return pl.BlockSpec(shape, lambda *_: (0,) * len(shape), pipeline_mode=pl.Buffered(1))


def params(**kw):
    return pltpu.CompilerParams(vmem_limit_bytes=VMEM_LIMIT, **kw)


def lane_sums(x):
    total = x[:, 0:128]
    for j in range(1, x.shape[1] // 128):
        total = total + x[:, j * 128 : (j + 1) * 128]
    return total


def norm_stats(e):
    average = jnp.sum(e, axis=0, keepdims=True) * (1.0 / D)
    spread = jnp.sum(e * e, axis=0, keepdims=True) * (1.0 / D) - average * average
    return average, lax.rsqrt(spread + EPS)


def fill_bias(bias_ref, key_ref, seg_ref):
    def rows_of(i, _):
        rows = pl.ds(pl.multiple_of(i * 256, 256), 256)
        same = key_ref[rows, :] == seg_ref[...]
        row_id = lax.broadcasted_iota(jnp.int32, (256, SEQ), 0) + i * 256
        col_id = lax.broadcasted_iota(jnp.int32, (256, SEQ), 1)
        bias_ref[rows, :] = jnp.where(same | (row_id == col_id), 0.0, MASKED)
        return 0

    lax.fori_loop(0, SEQ // 256, rows_of, 0)


MESH = pl.DeviceIdType.MESH


class Wire:
    def __init__(self, send, recv):
        self.send_sem, self.recv_sem, self.count, self.sent = send, recv, 0, []
        self.me = (lax.axis_index("dp"), lax.axis_index("mp"), lax.axis_index("hidden"))
        self.size = (lax.axis_size("dp"), lax.axis_size("mp"), lax.axis_size("hidden"))

    def peer(self, axis, offset):
        where = list(self.me)
        where[axis] = lax.rem(where[axis] + offset, self.size[axis])
        return tuple(where)

    def origin(self, axis, offset):
        return lax.rem(self.me[axis] - offset + self.size[axis], self.size[axis])

    def meet(self):
        barrier = pltpu.get_barrier_semaphore()
        total = 0
        for axis in range(3):
            for offset in range(1, self.size[axis]):
                pl.semaphore_signal(barrier, 1, device_id=self.peer(axis, offset), device_id_type=MESH)
                total += 1
        pl.semaphore_wait(barrier, total)

    def send(self, src, dst, target):
        copy = pltpu.make_async_remote_copy(
            src, dst, self.send_sem.at[self.count], self.recv_sem.at[self.count], device_id=target, device_id_type=MESH
        )
        copy.start()
        self.count += 1
        self.sent.append(copy)
        return copy

    def keep(self, src, dst):
        copy = pltpu.make_async_copy(src, dst, self.send_sem.at[self.count])
        copy.start()
        self.count += 1
        return copy

    def finish(self):
        assert self.count <= self.send_sem.shape[0], self.count
        for copy in self.sent:
            copy.wait_send()


DP, MP, HID = 0, 1, 2


HALF = D // 2


def sin_cos(angles):
    turns = jnp.floor(angles * (2.0 / math.pi) + 0.5)
    r = ((angles - turns * PI_2[0]) - turns * PI_2[1]) - turns * PI_2[2]
    r2 = r * r
    s = r + r * r2 * (-1.6666654611e-1 + r2 * (8.3321608736e-3 + r2 * -1.9515295891e-4))
    c = 1.0 - 0.5 * r2 + r2 * r2 * (4.166664568298827e-2 + r2 * (-1.388731625493765e-3 + r2 * 2.443315711809948e-5))
    quarter = turns - 4.0 * jnp.floor(turns * 0.25)
    odd = (quarter == 1.0) | (quarter == 3.0)
    flip_s = quarter >= 2.0
    flip_c = (quarter == 1.0) | (quarter == 2.0)
    sine = jnp.where(odd, c, s)
    cosine = jnp.where(odd, s, c)
    return jnp.where(flip_s, -sine, sine), jnp.where(flip_c, -cosine, cosine)


def forward_kernel(
    x_ref, c_ref, w1a_ref, w1b_ref, w2_ref, we_ref, wr_ref, cols_ref, rows_ref, pos_ref, rate_ref, key_ref, seg_ref,
    et_out, ft_out, w1_out, qkv_out, out_out, dmid_out, do_out, near_r, near_e, last_sum, wef_ref, wrf_ref,
    lse_ref, p_ref, dbe_ref, dw2_ref, dbf_ref, dgs_ref,
    xt, ct, w1af, w1bf, w2f, rowsf, tab, et, ft, f, w1, qkv, bias, vt, wb, at, out, wblk, dblk, w2c, theirs, sums,
    send, recv, z_send, z_recv, p_send, p_recv, c_send, c_recv, x_send, x_recv, n_send, n_recv, o_sem, local,
):
    wire = Wire(send, recv)
    d, m, h = wire.me
    dp, mp, hid = wire.size
    rows = D // mp
    wide = D // hid
    fcols = we_ref.shape[1]
    half = rows // dp
    offset = pl.multiple_of(d * half, half)
    own = (
        (w1a_ref, lambda mm_, hh: w1af.at[hh, mm_, d], lambda: w1af.at[:, :, d], HID),
        (w1b_ref, lambda mm_, hh: w1bf.at[hh, mm_, d], lambda: w1bf.at[:, :, d], MP),
        (w2_ref, lambda mm_, hh: w2f.at[mm_, hh, d], lambda: w2f.at[:, :, d], HID),
    )
    wire.meet()
    waits, stored = [], []
    first, second, third = {}, {}, {}

    def swap(src_ref, dst_ref):
        mine = pl.ds(pl.multiple_of(m * rows, rows), rows)
        moved = []
        for q in range(1, mp):
            to = wire.peer(MP, q)
            moved.append(wire.send(src_ref.at[:, pl.ds(pl.multiple_of(to[1] * SEQ, SEQ), SEQ)], dst_ref.at[mine], to))
        return moved, wire.keep(src_ref.at[:, pl.ds(pl.multiple_of(m * SEQ, SEQ), SEQ)], dst_ref.at[mine])

    def landed(pair):
        for copy in pair[0]:
            copy.wait_recv()
        pair[1].wait()

    def stage_one(i):
        src, dst, _, axis = own[i]
        first[i] = [wire.keep(src, dst(m, h))]
        first[i] += [wire.send(src, dst(m, h), wire.peer(axis, o)) for o in range(1, wire.size[axis])]

    def stage_two(i):
        _, dst, _, axis = own[i]
        other = MP if axis == HID else HID
        second[i] = []
        for o, copy in enumerate(first[i]):
            if o == 0:
                copy.wait()
            else:
                copy.wait_recv()
            at_ = wire.origin(axis, o)
            piece = dst(m, at_) if axis == HID else dst(at_, h)
            second[i] += [wire.send(piece, piece, wire.peer(other, q)) for q in range(1, wire.size[other])]

    def stage_three(i):
        for copy in second[i]:
            copy.wait_recv()
        third[i] = [wire.send(own[i][2](), own[i][2](), wire.peer(DP, r)) for r in range(1, dp)]

    def done(i):
        for copy in third[i]:
            copy.wait_recv()

    full = (wef_ref, wrf_ref)
    part = (we_ref.at[pl.ds(offset, half)], wr_ref.at[pl.ds(offset, half)])
    whole_planes = ((1,), (1, hid - 1))
    order = [0, 1, hid - 1] + list(range(2, hid - 1))

    def plane_of(o):
        return lax.rem(h - o + hid, hid)

    def piece(j, mm_, dd, o):
        at_ = pl.ds(pl.multiple_of(mm_ * rows + dd * half, half), half)
        return full[j].at[at_, pl.ds(pl.multiple_of(plane_of(o) * fcols, fcols), fcols)]

    def remote(src, dst, sems, target):
        return pltpu.make_async_remote_copy(src, dst, sems[0], sems[1], device_id=target, device_id_type=MESH)

    def to_plane(j, o, q):
        src = part[j] if o == 0 else piece(j, m, d, o)
        return remote(src, piece(j, m, d, o), (p_send.at[j, o, q], p_recv.at[j, o, q]), wire.peer(MP, q))

    def to_depth(j, o, k):
        if o in whole_planes[j]:
            src = dst = piece(j, k, d, 0)
        else:
            src, dst = part[j], piece(j, m, d, 0)
        return remote(src, dst, (z_send.at[j, o, k], z_recv.at[j, o, k]), wire.peer(HID, o))

    def depth_count(j, o):
        return mp if o in whole_planes[j] else 1

    def to_core(j, o, k, r):
        return remote(
            piece(j, k, d, o), piece(j, k, d, o), (c_send.at[j, o, k, r - 1], c_recv.at[j, o, k, r - 1]), wire.peer(DP, r)
        )

    def keep_own(j):
        return pltpu.make_async_copy(part[j], piece(j, m, d, 0), local.at[j])

    def plane_start(j, o):
        if o:
            to_depth(j, o, 0).wait_recv()
        else:
            keep_own(j).start()
        for q in range(1, mp):
            to_plane(j, o, q).start()

    def plane_wait(j, o):
        if o == 0:
            keep_own(j).wait()
        for q in range(1, mp):
            to_plane(j, o, q).wait_recv()

    def depth_start(j, o):
        for k in range(depth_count(j, o)):
            to_depth(j, o, k).start()

    def apart(j):
        return [o for o in range(1, hid) if o not in whole_planes[j]]

    def core_start(j, o):
        if o in whole_planes[j]:
            for k in range(mp):
                to_depth(j, o, k).wait_recv()
        elif o:
            plane_wait(j, o)
        for k in range(mp):
            for r in range(1, dp):
                to_core(j, o, k, r).start()

    def arrived(j, o):
        for k in range(mp):
            for r in range(1, dp):
                to_core(j, o, k, r).wait_recv()

    mine = pl.ds(pl.multiple_of(m * rows, rows), rows)
    small = [wire.send(cols_ref, p_ref.at[mine], wire.peer(MP, q)) for q in range(1, mp)]
    small += [wire.send(rows_ref, rowsf.at[h], wire.peer(HID, o)) for o in range(1, hid)]
    kept = [wire.keep(cols_ref, p_ref.at[mine]), wire.keep(rows_ref, rowsf.at[h])]
    stage_one(0)
    stage_one(1)
    x_in = swap(x_ref, xt)

    def table_rows(j, _):
        at_ = pl.ds(pl.multiple_of(j * 64, 64), 64)
        sine, cosine = sin_cos(rate_ref[at_, :] * pos_ref[...])
        tab[at_, :] = sine
        tab[pl.ds(pl.multiple_of(j * 64 + HALF, 64), 64), :] = cosine
        return 0

    lax.fori_loop(0, 1, table_rows, 0)
    stage_two(0)
    stage_two(1)
    lax.fori_loop(1, HALF // 64, table_rows, 0)
    fill_bias(bias, key_ref, seg_ref)
    for copy in small:
        copy.wait_recv()
    for copy in kept:
        copy.wait()
    wb[...] = jnp.zeros_like(wb)
    for hh in range(hid):
        wb[:, hh * wide : (hh + 1) * wide] = rowsf[hh, 1:2, :wide]
        wb[:, 2 * D + hh * wide : 2 * D + (hh + 1) * wide] = rowsf[hh, 2:3, :wide]
    landed(x_in)

    def norm_cols(j, _):
        cols = pl.ds(pl.multiple_of(j * 256, 256), 256)
        e = xt[:, cols].astype(F32) + tab[:, cols]
        et[:, cols] = e
        average, inv = norm_stats(e)
        low = ((e - average) * inv * p_ref[:, 0:1] + p_ref[:, 1:2]).astype(BF16)
        ft[:, cols] = low
        f[cols, :] = low.T
        return 0

    lax.fori_loop(0, SEQ // 256, norm_cols, 0)
    stored += [wire.keep(et, et_out), wire.keep(ft, ft_out)]
    stage_three(0)
    stage_three(1)
    for j in (1, 0):
        for o in apart(j):
            depth_start(j, o)
    plane_start(1, 0)
    stage_one(2)
    done(0)
    done(1)
    plane_start(0, 0)
    c_in = swap(c_ref, ct)
    for hh in range(hid):
        for mm_ in range(mp):
            for dd in range(dp):
                at_ = slice(mm_ * rows + dd * half, mm_ * rows + (dd + 1) * half)
                for k in range(3):
                    if k < 2:
                        value = w1af[hh, mm_, dd, :, k * wide : (k + 1) * wide]
                    else:
                        value = w1bf[hh, mm_, dd]
                    w1[at_, k * D + hh * wide : k * D + (hh + 1) * wide] = value
    stored.append(wire.keep(w1, w1_out))

    def cols_of(n, scale):
        cols = pl.ds(pl.multiple_of(n * 256, 256), 256)
        y = (mm(f[...], w1[:, cols]) + wb[:, cols]).astype(BF16)
        qkv[:, cols] = y * jnp.asarray(scale, BF16)
        return 0

    lax.fori_loop(0, D // 256, lambda n, c: cols_of(n, HD**-0.5), 0)
    stage_two(2)
    plane_wait(1, 0)
    for o in whole_planes[1]:
        depth_start(1, o)
    lax.fori_loop(D // 256, 3 * D // 256, lambda n, c: cols_of(n, 1.0), 0)
    stored.append(wire.keep(qkv, qkv_out))

    low = lax.broadcasted_iota(jnp.int32, (SEQ, PAIR), 1) < HD
    lse_ref[...] = jnp.zeros_like(lse_ref)

    def pair_of(p, _):
        lanes = pl.ds(pl.multiple_of(p * PAIR, PAIR), PAIR)
        k_lanes = pl.ds(pl.multiple_of(p * PAIR + D, PAIR), PAIR)
        v_lanes = pl.ds(pl.multiple_of(p * PAIR + 2 * D, PAIR), PAIR)
        vt[...] = qkv[:, v_lanes].T
        q = qkv[:, lanes]
        for hh in range(2):
            qm = jnp.where(low if hh == 0 else ~low, q, jnp.zeros_like(q))
            s = mm(qkv[:, k_lanes], qm, NT) + bias[...]
            top = jnp.max(s, axis=0, keepdims=True)
            e = jnp.exp(s - top)
            total = jnp.sum(e, axis=0, keepdims=True)
            o = mm(vt[hh * HD : (hh + 1) * HD, :], e.astype(BF16)) / total
            at[pl.ds(pl.multiple_of(p * PAIR + hh * HD, HD), HD), :] = o.astype(BF16)
            lse_ref[p, hh : hh + 1, :] = top + jnp.log(total)
        return 0

    lax.fori_loop(0, PAIRS // 3, pair_of, 0)
    plane_wait(0, 0)
    for o in whole_planes[0]:
        depth_start(0, o)
    for j in (1, 0):
        for o in apart(j):
            plane_start(j, o)
    lax.fori_loop(PAIRS // 3, 2 * PAIRS // 3, pair_of, 0)
    stage_three(2)
    for j in range(2):
        core_start(j, 0)
    lax.fori_loop(2 * PAIRS // 3, PAIRS, pair_of, 0)
    for copy in stored:
        copy.wait()
    landed(c_in)
    done(2)

    ot, ds_sum, st, bt, mid = bias.at[pl.ds(0, D)], tab, xt, ft, et
    tokens = [pl.ds(n * D, D) for n in range(3)]
    for mm_ in range(mp):
        for hh in range(hid):
            for dd in range(dp):
                at_ = hh * wide + dd * (wide // dp)
                w2c[at_ : at_ + wide // dp, mm_ * rows : (mm_ + 1) * rows] = w2f[mm_, hh, dd]
    w2t = w2c[...].T

    def middle_cols(j, _):
        cols = pl.ds(pl.multiple_of(j * 256, 256), 256)
        value = et[:, cols] + (mm(w2t, at[:, cols]) + p_ref[:, 4:5])
        mid[:, cols] = value
        ot[:, cols] = value + p_ref[:, 5:6]
        average, inv = norm_stats(value)
        s = ((value - average) * inv * p_ref[:, 2:3] + p_ref[:, 3:4]).astype(BF16)
        st[:, cols] = s
        qkv[cols, tokens[0]] = s.T
        qkv[cols, tokens[1]] = ct[:, cols].T
        return 0

    lax.fori_loop(0, SEQ // 256, middle_cols, 0)
    ds_sum[...] = jnp.zeros_like(ds_sum)

    def fetch(j, o):
        hcols = pl.ds(pl.multiple_of(plane_of(o) * fcols, fcols), fcols)
        return pltpu.make_async_copy(full[j].at[:, hcols], wblk.at[j], local.at[2 + j])

    def place(n):
        o = 0
        for k in range(1, hid):
            o = jnp.where(n == k, order[k], o)
        return o

    def swap_core(j, n, k, r):
        to = wire.peer(DP, r)
        return remote(
            dblk.at[j, k, to[0]], theirs.at[lax.rem(n, 2), j, r - 1, k], (x_send.at[j, n, k, r - 1], x_recv.at[j, n, k, r - 1]), to
        )

    def each_core(n, do):
        for j in range(2):
            for k in range(mp):
                for r in range(1, dp):
                    do(swap_core(j, n, k, r))

    end = hid - 1

    def sum_depth(n):
        to = (d, m, plane_of(place(n)))
        return remote(sums.at[lax.rem(n, 2), 0], near_r.at[n], (n_send.at[n, 0], n_recv.at[n, 0]), to)

    def sum_plane(n, q):
        to = wire.peer(MP, q)
        return remote(sums.at[lax.rem(n, 2), 1, to[1]], near_e.at[n, q], (n_send.at[n, q], n_recv.at[n, q]), to)

    def save(j, n, last):
        slot = lax.rem(n, 2)
        if last:
            return pltpu.make_async_copy(sums.at[slot, j], last_sum.at[j], o_sem.at[j, n])
        if j == 0:
            return pltpu.make_async_copy(sums.at[0, 0], near_r.at[0], o_sem.at[0, 0])
        return pltpu.make_async_copy(sums.at[slot, 1, m], near_e.at[n, 0], o_sem.at[1, n])

    def add_cores(n, last=False):
        each_core(n, lambda copy: copy.wait_recv())
        slot = lax.rem(n, 2)
        for j in range(2):
            for k in range(mp):
                value = dblk[j, k, d].astype(F32)
                for r in range(1, dp):
                    value = value + theirs[slot, j, r - 1, k].astype(F32)
                sums[slot, j, k] = value.astype(BF16)
        if last:
            for j in range(2):
                save(j, n, True).start()
            return
        for q in range(1, mp):
            sum_plane(n, q).start()
        save(1, n, False).start()

    def gone(n):
        for q in range(1, mp):
            sum_plane(n, q).wait_send()
        save(1, n, False).wait()

    def block(n, _):
        o = place(n)
        hh = plane_of(o)
        for j in range(2):
            arrived(j, o)
        for j in range(2):
            fetch(j, o).start()
        for j in range(2):
            fetch(j, o).wait()

        pre = mm(qkv[:, tokens[0]], wblk[0]) + rowsf[hh, 0:1, :]
        cdf = 0.5 * (1.0 + lax.erf(pre * (1.0 / math.sqrt(2.0))))
        act = (pre * cdf).astype(BF16)
        slope = cdf + pre * jnp.exp(-0.5 * pre * pre) * (1.0 / math.sqrt(2.0 * math.pi))
        grad = (mm(qkv[:, tokens[1]], wblk[1]) * slope).astype(BF16)

        @pl.when(n == 3)
        def _():
            gone(0)
            save(0, 0, False).wait()

        @pl.when(n > 3)
        def _():
            gone(n - 3)
            sum_depth(n - 3).wait_send()

        @pl.when(n > 0)
        def _():
            add_cores(n - 1)
            each_core(n - 1, lambda copy: copy.wait_send())

        @pl.when(n == 1)
        def _():
            save(0, 0, False).start()

        @pl.when(n > 1)
        def _():
            sum_depth(n - 1).start()

        for j, value in enumerate((mm(ct[...], act), mm(st[...], grad))):
            for k in range(mp):
                for dd in range(dp):
                    at_ = k * rows + dd * half
                    dblk[j, k, dd] = value[at_ : at_ + half, :].astype(BF16)
        each_core(n, lambda copy: copy.start())
        dbe_ref[hh, 0:1, :] = jnp.sum(grad.astype(F32), axis=0, keepdims=True)
        ot[...] += mm(wblk[1], act, NT)
        ds_sum[...] += mm(wblk[0], grad, NT)

        for k in range(1, hid):

            @pl.when(n + 1 == k)
            def _():
                for j in range(2):
                    core_start(j, order[k])

        return 0

    lax.fori_loop(0, hid, block, 0)
    gone(end - 2)
    sum_depth(end - 2).wait_send()
    add_cores(end, True)
    dgs_ref[...] = jnp.zeros_like(dgs_ref)

    def back_cols(j, _):
        cols = pl.ds(pl.multiple_of(j * 256, 256), 256)
        value = mid[:, cols]
        out[:, cols] = ot[:, cols].astype(BF16)
        average, inv = norm_stats(value)
        normed = (value - average) * inv
        ds = ds_sum[:, cols]
        scaled = ds * p_ref[:, 2:3]
        total = jnp.sum(scaled, axis=0, keepdims=True) * (1.0 / D)
        crossed = jnp.sum(scaled * normed, axis=0, keepdims=True) * (1.0 / D)
        dmid = ct[:, cols].astype(F32) + inv * (scaled - total - normed * crossed)
        mid[:, cols] = dmid
        low_ = dmid.astype(BF16)
        bt[:, cols] = low_
        qkv[cols, tokens[2]] = mm(w2c[...], low_).astype(BF16).T
        dgs_ref[0] += lane_sums(ds * normed)
        dgs_ref[1] += lane_sums(ds)
        return 0

    lax.fori_loop(0, SEQ // 256, back_cols, 0)
    last = [wire.keep(out, out_out), wire.keep(mid, dmid_out), wire.keep(qkv.at[:, tokens[2]], do_out)]
    ones = jnp.ones((8, SEQ), BF16)
    dbf_ref[0] = mm(ones, ct[...], NT)
    dbf_ref[1] = mm(ones, bt[...], NT)
    for j in range(mp):
        dw2_ref[j] = mm(at[...], bt[j * rows : (j + 1) * rows, :], NT).astype(BF16)
    each_core(end, lambda copy: copy.wait_send())
    gone(end - 1)
    sum_depth(end - 1).wait_send()
    for j in range(2):
        save(j, end, True).wait()
    for n in range(end):
        if n:
            sum_depth(n).wait_recv()
        for q in range(1, mp):
            sum_plane(n, q).wait_recv()
    for copy in last:
        copy.wait()
    wire.finish()
    for j in range(2):
        for o in range(hid):
            if o:
                for k in range(depth_count(j, o)):
                    to_depth(j, o, k).wait_send()
            if o not in whole_planes[j]:
                for q in range(1, mp):
                    to_plane(j, o, q).wait_send()
            for k in range(mp):
                for r in range(1, dp):
                    to_core(j, o, k, r).wait_send()


def forward(x, c, w1a, w1b, w2, we, wr, cols, rows, pos, rate, key_col, seg_row):
    dp, mp, hid = lax.axis_size("dp"), lax.axis_size("mp"), lax.axis_size("hidden")
    half = D // mp // dp
    fc = we.shape[1]
    ff = hid * fc
    sds = jax.ShapeDtypeStruct
    out_shape = (
        sds((D, SEQ), F32), sds((D, SEQ), BF16), sds((D, 3 * D), BF16), sds((SEQ, 3 * D), BF16),
        sds((D, SEQ), BF16), sds((D, SEQ), F32), sds((SEQ, D), BF16), sds((hid - 1, mp, half, fc), BF16),
        sds((hid - 1, mp, half, fc), BF16), sds((2, mp, half, fc), BF16), sds((D, ff), BF16), sds((D, ff), BF16),
        sds((PAIRS, 8, SEQ), F32), sds((D, cols.shape[1]), F32), sds((hid, 8, fc), F32), sds((mp, D, D // mp), BF16),
        sds((2, 8, D), F32), sds((2, D, 128), F32),
    )
    n = (mp - 1) + (hid - 1) + 2 + 2 * hid + mp + 2 * hid * (mp - 1) + mp * (hid - 1) + 3 * (dp - 1) + 2 * mp + 7
    hbm = pl.BlockSpec(memory_space=pl.ANY)
    vmem = pl.BlockSpec(memory_space=pltpu.VMEM)
    vm = lambda dtype, *shape: pltpu.VMEM(shape, dtype)
    sem = lambda *shape: pltpu.SemaphoreType.DMA(shape)
    return pl.pallas_call(
        forward_kernel,
        out_shape=out_shape,
        in_specs=[hbm] * 9 + [vmem] * 4,
        out_specs=(hbm,) * 12 + (vmem,) * 6,
        scratch_shapes=[
            vm(BF16, D, SEQ), vm(BF16, D, SEQ), vm(BF16, hid, mp, dp, half, w1a.shape[1]),
            vm(BF16, hid, mp, dp, half, w1b.shape[1]), vm(BF16, mp, hid, dp, *w2.shape), vm(F32, hid, *rows.shape),
            vm(F32, D, SEQ), vm(F32, D, SEQ), vm(BF16, D, SEQ), vm(BF16, SEQ, D), vm(BF16, D, 3 * D),
            vm(BF16, SEQ, 3 * D), vm(F32, SEQ, SEQ), vm(BF16, PAIR, SEQ), vm(F32, 1, 3 * D),
            vm(BF16, D, SEQ), vm(BF16, D, SEQ), vm(BF16, 2, D, fc), vm(BF16, 2, mp, dp, half, fc), vm(BF16, D, D),
            vm(BF16, 2, 2, dp - 1, mp, half, fc), vm(BF16, 2, 2, mp, half, fc),
            sem(n), sem(n), sem(2, hid, mp), sem(2, hid, mp), sem(2, hid, mp), sem(2, hid, mp),
            sem(2, hid, mp, dp - 1), sem(2, hid, mp, dp - 1), sem(2, hid, mp, dp - 1), sem(2, hid, mp, dp - 1),
            sem(hid, mp), sem(hid, mp), sem(2, hid), sem(4),
        ],
        compiler_params=params(collective_id=0, has_side_effects=True),
        name="forward",
    )(x, c, w1a, w1b, w2, we, wr, cols, rows, pos, rate, key_col, seg_row)


def backward_kernel(
    o_ref, dw2_ref, near_r, near_e, last_sum, qkv_in, do_in, lse_ref, key_ref, seg_ref, ft_in, w_in, et_in, dmid_in, p_ref,
    dbe_ref, dbf_ref, dgs_ref,
    of_ref, xf_ref, ga_ref, gb_ref, g2_ref, ge_ref, gr_ref, vecf_ref,
    qkv, do, bias, kt, dqt, dk, dv, dka, dva, ft, et, dmid, dgp,
    a0, a1, a2, o0, o1, s2, b0, b1, b2, be, br, t0, t1, t2, t3, t4, c0, c1, c2, c3, c4,
    v0, va, vb, vc, v1, v2, loads, send, recv,
):
    wire = Wire(send, recv)
    d, m, h = wire.me
    dp, mp, hid = wire.size
    rows = D // mp
    wide = D // hid
    half = rows // dp
    fcols = ge_ref.shape[1]
    v_in = (va, vb, vc)
    hslice = lambda hh: pl.ds(pl.multiple_of(hh * fcols, fcols), fcols)

    def load(n, src, dst):
        copy = pltpu.make_async_copy(src, dst, loads.at[n])
        copy.start()
        return copy

    parts = []
    for p in range(PAIRS):
        got = []
        for k in range(3):
            lanes = slice(k * D + p * PAIR, k * D + (p + 1) * PAIR)
            got.append(load(4 * p + k, qkv_in.at[:, lanes], qkv.at[:, lanes]))
        lanes = slice(p * PAIR, (p + 1) * PAIR)
        got.append(load(4 * p + 3, do_in.at[:, lanes], do.at[:, lanes]))
        parts.append(got)
    others = [load(4 * PAIRS + i, a, b) for i, (a, b) in enumerate(((ft_in, ft), (et_in, et), (dmid_in, dmid)))]
    wire.meet()
    items = (
        (lambda dd: o0.at[dd], a0, o0.at[d], b0, t0, c0, ga_ref, MP, HID),
        (lambda dd: o1.at[dd], a1, o1.at[d], b1, t1, c1, gb_ref, HID, HID),
        (lambda dd: dw2_ref.at[:, :, dd], a2, s2, b2, t2, c2, g2_ref, MP, MP),
        (None, None, None, be, t3, c3, ge_ref, MP, None),
        (None, None, None, br, t4, c4, gr_ref, HID, None),
    )
    core, kept, near, far = {}, {}, {}, {}
    end = hid - 1
    plane = lambda o: lax.rem(h - o + hid, hid)
    order = [0, 1, hid - 1] + list(range(2, hid - 1))
    at = 4 * PAIRS + 4
    own = {
        4: [load(at, near_r, br.at[pl.ds(0, end)])],
        3: [load(at + 1 + n, near_e.at[n], be.at[:, :, hslice(plane(order[n]))]) for n in range(end)],
    }
    own[3].append(load(at + 1 + end, last_sum.at[1, m], be.at[0, :, hslice(plane(order[end]))]))

    def stage_core(i):
        src, a, s = items[i][:3]
        core[i] = [wire.send(src(wire.peer(DP, r)[0]), a.at[r - 1], wire.peer(DP, r)) for r in range(1, dp)]
        if i > 1:
            kept[i] = wire.keep(src(d), s)

    def add_all(dst, own, others, shape):
        lead = shape[:-2]

        def body(n, _):
            index = []
            for size in reversed(lead):
                index.insert(0, lax.rem(n, size))
                n = lax.div(n, size)
            index = tuple(index)
            value = own[index].astype(F32)
            for j in range(others.shape[0]):
                value = value + others[(j,) + index].astype(F32)
            dst[index] = value.astype(dst.dtype)
            return 0

        lax.fori_loop(0, math.prod(lead), body, 0)

    def part(i, ref, axis, at, leads):
        if items[i][8] is None:
            return ref.at[(slice(None),) * len(leads) + (slice(None), hslice(at))] if axis == HID else ref.at[at]
        return ref.at[at] if leads[0] == axis else ref.at[:, at]

    def leads_of(i):
        lead = items[i][8]
        return (MP,) if lead is None else ((HID, MP) if lead == HID else (MP, HID))

    def stage_near(i):
        if i == 4:
            near[4] = [wire.send(last_sum.at[0], br.at[end], wire.peer(HID, hid - order[end]))]
            return
        if i == 3:
            here = hslice(plane(order[end]))
            near[3] = []
            for q in range(1, mp):
                to = wire.peer(MP, q)
                near[3].append(wire.send(last_sum.at[1, to[1]], be.at[q, :, here], to))
            return
        _, a, s, b, t, c, g, axis, _ = items[i]
        for copy in core[i]:
            copy.wait_recv()
        if i in kept:
            kept[i].wait()
        add_all(s, s, a, s.shape)
        near[i] = [
            wire.send(part(i, s, axis, wire.peer(axis, q)[axis], leads_of(i)), b.at[q - 1], wire.peer(axis, q))
            for q in range(1, wire.size[axis])
        ]

    def stage_far(i):
        _, a, s, b, t, c, g, axis, lead = items[i]
        if i < 3:
            for copy in near[i]:
                copy.wait_recv()
            add_all(t, part(i, s, axis, wire.me[axis], leads_of(i)), b, t.shape)
        else:
            for copy in near[i]:
                copy.wait_recv()
            for copy in own[i]:
                copy.wait()
            add_all(t, b.at[0], b.at[pl.ds(1, b.shape[0] - 1)], t.shape)
        other = MP if axis == HID else HID
        left = tuple(x for x in leads_of(i) if x != axis)
        far[i] = []
        for q in range(1, wire.size[other]):
            to = wire.peer(other, q)
            far[i].append(wire.send(part(i, t, other, to[other], left), c.at[q - 1], to))

    def stage_end(i):
        _, a, s, b, t, c, g, axis, lead = items[i]
        other = MP if axis == HID else HID
        left = tuple(x for x in leads_of(i) if x != axis)
        for copy in far[i]:
            copy.wait_recv()
        value = part(i, t, other, wire.me[other], left)[...].astype(F32)
        for j in range(c.shape[0]):
            value = value + c[j].astype(F32)
        g[...] = value

    moved, held = [], []

    def swap(src_ref, dst_ref):
        mine = pl.ds(pl.multiple_of(m * SEQ, SEQ), SEQ)
        for q in range(1, mp):
            to = wire.peer(MP, q)
            moved.append(wire.send(src_ref.at[pl.ds(pl.multiple_of(to[1] * rows, rows), rows)], dst_ref.at[:, mine], to))
        held.append(wire.keep(src_ref.at[pl.ds(pl.multiple_of(m * rows, rows), rows)], dst_ref.at[:, mine]))

    vec = {}

    def vec_send(axis, src):
        vec[axis] = [wire.send(src, v_in[axis].at[o - 1], wire.peer(axis, o)) for o in range(1, wire.size[axis])]

    def vec_sum(axis, src, dst):
        for copy in vec[axis]:
            copy.wait_recv()
        total = src[...]
        for j in range(wire.size[axis] - 1):
            total = total + v_in[axis][j]
        dst[...] = total

    stage_near(4)
    stage_near(3)
    stage_core(2)
    swap(o_ref, of_ref)
    fill_bias(bias, key_ref, seg_ref)
    low = lax.broadcasted_iota(jnp.int32, (QBB, PAIR), 1) < HD

    def pair_of(p, _):
        off = pl.multiple_of(p * PAIR, PAIR)
        lanes = pl.ds(off, PAIR)
        k_lanes = pl.ds(pl.multiple_of(off + D, PAIR), PAIR)
        v_lanes = pl.ds(pl.multiple_of(off + 2 * D, PAIR), PAIR)
        kt[...] = qkv[:, k_lanes].T
        dka[...] = jnp.zeros_like(dka)
        dva[...] = jnp.zeros_like(dva)

        def block(j, _):
            cols = pl.ds(pl.multiple_of(j * QBB, QBB), QBB)
            q = qkv[cols, lanes]
            g = do[cols, lanes]
            for hh in range(2):
                keep = low if hh == 0 else ~low
                qm = jnp.where(keep, q, jnp.zeros_like(q))
                gm = jnp.where(keep, g, jnp.zeros_like(g))
                e = jnp.exp(mm(qkv[:, k_lanes], qm, NT) + bias[:, cols] - lse_ref[p, hh : hh + 1, cols])
                t = e * mm(qkv[:, v_lanes], gm, NT)
                ds = (t - e * jnp.sum(t, axis=0, keepdims=True)).astype(BF16)
                dva[...] += mm(e.astype(BF16), gm)
                dka[...] += mm(ds, qm)
                dq = mm(kt[hh * HD : (hh + 1) * HD, :], ds) * HD**-0.5
                dqt[pl.ds(pl.multiple_of(off + hh * HD, HD), HD), cols] = dq.astype(BF16)
            return 0

        lax.fori_loop(0, SEQ // QBB, block, 0)
        dk[:, lanes] = dka[...].astype(BF16)
        dv[:, lanes] = dva[...].astype(BF16)
        return 0

    def pairs(first, last):
        for p in range(first, last):
            for copy in parts[p]:
                copy.wait()
        lax.fori_loop(first, last, pair_of, 0)

    pairs(0, 2)
    stage_near(2)
    pairs(2, PAIRS)
    w1 = qkv.at[pl.ds(0, D)]
    w_load = load(4 * PAIRS + 3, w_in, w1)
    for copy in others:
        copy.wait()

    for hh in range(hid):
        for k in range(3):
            if k == 0:
                value = mm(ft[...], dqt[hh * wide : (hh + 1) * wide, :], NT).astype(BF16)
            else:
                value = mm(ft[...], (dk, dv)[k - 1][:, hh * wide : (hh + 1) * wide]).astype(BF16)
            for mm_ in range(mp):
                for dd in range(dp):
                    piece = value[mm_ * rows + dd * half : mm_ * rows + (dd + 1) * half, :]
                    if k < 2:
                        o0[dd, hh, mm_, :, k * wide : (k + 1) * wide] = piece
                    else:
                        o1[dd, hh, mm_] = piece
    stage_core(1)
    stage_core(0)
    df = bias.at[pl.ds(0, D)]
    w_load.wait()
    dx = ft

    def feature_cols(j, _):
        cols = pl.ds(pl.multiple_of(j * 256, 256), 256)
        value = mm(w1[:, 0:D], dqt[:, cols])
        value += mm(w1[:, D : 2 * D], dk[cols, :], NT)
        value += mm(w1[:, 2 * D : 3 * D], dv[cols, :], NT)
        df[:, cols] = value
        return 0

    lax.fori_loop(0, SEQ // 256, feature_cols, 0)
    stage_near(1)
    stage_near(0)
    dgp[...] = jnp.zeros_like(dgp)

    def norm_cols(j, _):
        cols = pl.ds(pl.multiple_of(j * 256, 256), 256)
        e = et[:, cols]
        average, inv = norm_stats(e)
        normed = (e - average) * inv
        g = df[:, cols]
        scaled = g * p_ref[:, 0:1]
        total = jnp.sum(scaled, axis=0, keepdims=True) * (1.0 / D)
        crossed = jnp.sum(scaled * normed, axis=0, keepdims=True) * (1.0 / D)
        dx[:, cols] = (dmid[:, cols] + inv * (scaled - total - normed * crossed)).astype(BF16)
        dgp[0] += lane_sums(g * normed)
        dgp[1] += lane_sums(g)
        return 0

    lax.fori_loop(0, SEQ // 256, norm_cols, 0)
    swap(dx, xf_ref)
    for i in (3, 2, 4):
        stage_far(i)
    ones = jnp.ones((8, SEQ), BF16)
    v0[...] = jnp.zeros_like(v0)
    for n in range(2):
        v0[n : n + 1, :] = jnp.sum(dgp[n].T, axis=0, keepdims=True)
        v0[2 + n : 3 + n, :] = jnp.sum(dgs_ref[n].T, axis=0, keepdims=True)
        v0[6 + n : 7 + n, :] = dbf_ref[n, 0:1, :]
    v0[4:5, :] = mm(ones, dqt[...], NT)[0:1]
    v0[5:6, :] = mm(ones, dv[...])[0:1]
    for hh in range(hid):
        row, lane = divmod(hh * fcols, D)
        v0[8 + row : 9 + row, lane : lane + fcols] = dbe_ref[hh, 0:1, :]
    vec_send(DP, v0)
    vec_sum(DP, v0, v1)
    vec_send(MP, v1)
    stage_far(1)
    stage_far(0)
    vec_sum(MP, v1, v2)
    vec_send(HID, v2)
    stage_end(3)
    stage_end(2)
    stage_end(4)
    stage_end(1)
    stage_end(0)
    vec_sum(HID, v2, vecf_ref)
    for copy in held:
        copy.wait()
    for copy in moved:
        copy.wait_recv()
    wire.finish()


def backward(o, dw2, near_r, near_e, last_sum, qkv, do, lse, key_col, seg_row, ft, w1, et, dmid, cols, dbe, dbf, dgs):
    dp, mp, hid = lax.axis_size("dp"), lax.axis_size("mp"), lax.axis_size("hidden")
    sds = jax.ShapeDtypeStruct
    wide = D // hid
    half = D // mp // dp
    half2, c2 = dw2.shape[3:]
    fc = near_e.shape[3]
    ff = hid * fc
    out_shape = (
        sds((D // mp, mp * SEQ), BF16), sds((D // mp, mp * SEQ), BF16), sds((half, 2 * wide), F32),
        sds((half, wide), F32), sds((half2, c2), F32), sds((half, fc), F32), sds((half, fc), F32), sds((16, D), F32),
    )
    vm = lambda *shape: pltpu.VMEM(shape, BF16)
    vf = lambda *shape: pltpu.VMEM(shape, F32)
    slabs = ((hid, mp, half, 2 * wide), (hid, mp, half, wide), (mp, hid, half2, c2))
    after = ((hid, half, 2 * wide), (mp, half, wide), (hid, half2, c2), (half, ff), (mp, half, fc))
    ends = ((half, 2 * wide), (half, wide), (half2, c2), (half, fc), (half, fc))
    near = (mp, hid, mp, mp, hid)
    far = (hid, mp, hid, hid, mp)
    scratch = [
        vm(SEQ, 3 * D), vm(SEQ, D), vf(SEQ, SEQ), vm(PAIR, SEQ), vm(D, SEQ), vm(SEQ, D), vm(SEQ, D),
        vf(SEQ, PAIR), vf(SEQ, PAIR), vm(D, SEQ), vf(D, SEQ), vf(D, SEQ), vf(2, D, 128),
    ]
    scratch += [vm(dp - 1, *s) for s in slabs]
    scratch += [vm(dp, *s) for s in slabs[:2]] + [vm(*s) for s in slabs[2:]]
    scratch += [vm(n - 1, *s) for n, s in zip(near[:3], after)] + [vm(n, *s) for n, s in zip(near[3:], after[3:])]
    scratch += [vm(*s) for s in after]
    scratch += [vm(n - 1, *s) for n, s in zip(far, ends)]
    scratch += [vf(16, D), vf(dp - 1, 16, D), vf(mp - 1, 16, D), vf(hid - 1, 16, D), vf(16, D), vf(16, D)]
    n = dp + mp + hid - 3 + 2 * mp + 3 * (dp - 1) + 1 + 5 * (mp + hid - 2)
    scratch += [pltpu.SemaphoreType.DMA((4 * PAIRS + 6 + hid,)), pltpu.SemaphoreType.DMA((n,)), pltpu.SemaphoreType.DMA((n,))]
    hbm = pl.BlockSpec(memory_space=pl.ANY)
    vmem = pl.BlockSpec(memory_space=pltpu.VMEM)
    return pl.pallas_call(
        backward_kernel,
        out_shape=out_shape,
        in_specs=[hbm] * 7 + [vmem] * 3 + [hbm] * 4 + [vmem] * 4,
        out_specs=(hbm, hbm) + (vmem,) * 6,
        scratch_shapes=scratch,
        compiler_params=params(collective_id=1, has_side_effects=True),
        name="backward",
    )(o, dw2, near_r, near_e, last_sum, qkv, do, lse, key_col, seg_row, ft, w1, et, dmid, cols, dbe, dbf, dgs)


def local(
    stored, positions, segments, present, norm_gains, norm_biases, input_proj, input_bias, output_proj,
    output_bias, expand_weight, expand_bias, reduce_weight, reduce_bias, cotangent,
):
    mp, hid, dp = lax.axis_size("mp"), lax.axis_size("hidden"), lax.axis_size("dp")
    m, h, d = lax.axis_index("mp"), lax.axis_index("hidden"), lax.axis_index("dp")
    rows_mp, hcols, fcols = D // mp, D // hid, expand_weight.shape[1]
    half = rows_mp // dp
    cols = [norm_gains[0], norm_biases[0], norm_gains[1], norm_biases[1], output_bias.astype(F32), reduce_bias.astype(F32)]
    cols = jnp.pad(jnp.stack(cols, axis=1), ((0, 0), (0, 128 - len(cols))))
    rows = jnp.concatenate(
        [
            expand_bias.astype(F32)[None],
            jnp.pad(input_bias.astype(F32), ((0, 0), (0, fcols - hcols))),
            jnp.zeros((5, fcols), F32),
        ]
    )
    w1 = lax.dynamic_slice_in_dim(input_proj, d * half, half, 0)
    w2 = lax.dynamic_slice_in_dim(output_proj, d * (hcols // dp), hcols // dp, 0)
    pos = lax.dynamic_slice_in_dim(positions, m * SEQ, SEQ).astype(F32)[None]
    rate = jnp.exp(jnp.arange(D // 2, dtype=jnp.int32).astype(F32) * (-math.log(10000.0) / (D // 2)))[:, None]
    key_col = jnp.where(present == 1, segments, -1)[:, None]
    seg_row = segments[None, :]
    et, ft, w1f, qkv, out_t, dmid, do, near_r, near_e, last_sum, _, _, lse, cols, dbe, dw2, dbf, dgs = forward(
        stored, cotangent, w1[:, :2].reshape(half, 2 * hcols), w1[:, 2], w2, expand_weight, reduce_weight, cols, rows,
        pos, rate, key_col, seg_row,
    )
    output, d_stored, ga, gb, d_output, d_expand, d_reduce, vec = backward(
        out_t,
        dw2.reshape(mp, hid, dp, hcols // dp, rows_mp),
        near_r,
        near_e,
        last_sum,
        qkv, do, lse, key_col, seg_row, ft, w1f, et, dmid, cols, dbe, dbf, dgs,
    )
    piece = D // (hid * mp * dp)
    cut = lambda x, at, size: lax.dynamic_slice_in_dim(x, at * size, size, x.ndim - 1)
    dg = cut(vec[:4].reshape(2, 2, D), (m * dp + d) * hid + h, piece)
    db_proj = cut(vec[4:6], h * dp + d, hcols // dp)
    db_feed = cut(vec[6:8], m * dp + d, half)
    dbe = cut(vec[8:].reshape(-1)[: hid * fcols], h * dp + d, fcols // dp)
    d_input = jnp.concatenate([ga.reshape(half, 2, hcols), gb[:, None]], axis=1)
    return (
        output, d_stored.astype(F32), dg[:, 0], dg[:, 1], d_input, db_proj, d_output, db_feed[1], d_expand, dbe, d_reduce,
        db_feed[0],
    )


def solution(mesh):
    placed = (
        P("mp", ("dp", "hidden")),
        P(("dp", "hidden")),
        P(("dp", "hidden", "mp")),
        P(("dp", "hidden", "mp")),
        P(None, "mp"),
        P(None, "mp"),
        P("mp", None, "hidden"),
        P(None, "hidden"),
        P("hidden", "mp"),
        P("mp"),
        P("mp", "hidden"),
        P("hidden"),
        P("mp", "hidden"),
        P("mp"),
        P("mp", ("dp", "hidden")),
    )
    return jax.shard_map(
        local,
        mesh=mesh,
        in_specs=placed,
        out_specs=(
            P("mp", ("dp", "hidden")),
            P("mp", ("dp", "hidden")),
            P(None, ("mp", "dp", "hidden")),
            P(None, ("mp", "dp", "hidden")),
            P(("mp", "dp"), None, "hidden"),
            P(None, ("hidden", "dp")),
            P(("hidden", "dp"), "mp"),
            P(("mp", "dp")),
            P(("mp", "dp"), "hidden"),
            P(("hidden", "dp")),
            P(("mp", "dp"), "hidden"),
            P(("mp", "dp")),
        ),
        check_vma=False,
    )
```

```python
import functools
import math

import jax
import jax.numpy as jnp
import numpy as np
from jax import lax
from jax.experimental import pallas as pl
from jax.experimental.pallas import tpu as pltpu
from jax.sharding import PartitionSpec as P

D = 768
HEADS = 12
HD = 64
SEQ = 1024
QBB = 1024
PAIR = 2 * HD
PAIRS = HEADS // 2
EPS = 1e-06
MASKED = -1e30
F32 = jnp.float32
BF16 = jnp.bfloat16
VMEM_LIMIT = 60 * 1024 * 1024
PI_2 = (1.5703125, 4.837512969970703125e-4, 7.549789948768648e-8)

NN = (((1,), (0,)), ((), ()))
NT = (((1,), (1,)), ((), ()))


def mm(a, b, dims=NN):
    return lax.dot_general(a, b, dims, preferred_element_type=F32)


def whole(shape):
    return pl.BlockSpec(shape, lambda *_: (0,) * len(shape), pipeline_mode=pl.Buffered(1))


def params(**kw):
    return pltpu.CompilerParams(vmem_limit_bytes=VMEM_LIMIT, **kw)


def lane_sums(x):
    total = x[:, 0:128]
    for j in range(1, x.shape[1] // 128):
        total = total + x[:, j * 128 : (j + 1) * 128]
    return total


def norm_stats(e):
    average = jnp.sum(e, axis=0, keepdims=True) * (1.0 / D)
    spread = jnp.sum(e * e, axis=0, keepdims=True) * (1.0 / D) - average * average
    return average, lax.rsqrt(spread + EPS)


def fill_bias(bias_ref, seg_ref, present_ref):
    seg = seg_ref[...].astype(F32)
    key = jnp.where(present_ref[...] == 1, seg, -1.0)
    key_cols = jnp.broadcast_to(key, (8, SEQ)).T
    for i in range(SEQ // 256):
        same = key_cols[i * 256 : (i + 1) * 256, 0:1] == seg
        row_id = lax.broadcasted_iota(jnp.int32, (256, SEQ), 0) + i * 256
        col_id = lax.broadcasted_iota(jnp.int32, (256, SEQ), 1)
        bias_ref[i * 256 : (i + 1) * 256, :] = jnp.where(same | (row_id == col_id), 0.0, MASKED)


MESH = pl.DeviceIdType.MESH


class Wire:
    def __init__(self, send, recv):
        self.send_sem, self.recv_sem, self.count, self.sent = send, recv, 0, []
        self.me = (lax.axis_index("dp"), lax.axis_index("mp"), lax.axis_index("hidden"))
        self.size = (lax.axis_size("dp"), lax.axis_size("mp"), lax.axis_size("hidden"))

    def peer(self, axis, offset):
        where = list(self.me)
        where[axis] = lax.rem(where[axis] + offset, self.size[axis])
        return tuple(where)

    def origin(self, axis, offset):
        return lax.rem(self.me[axis] - offset + self.size[axis], self.size[axis])

    def meet(self):
        barrier = pltpu.get_barrier_semaphore()
        total = 0
        for axis in range(3):
            for offset in range(1, self.size[axis]):
                pl.semaphore_signal(barrier, 1, device_id=self.peer(axis, offset), device_id_type=MESH)
                total += 1
        pl.semaphore_wait(barrier, total)

    def send(self, src, dst, target):
        copy = pltpu.make_async_remote_copy(
            src, dst, self.send_sem.at[self.count], self.recv_sem.at[self.count], device_id=target, device_id_type=MESH
        )
        copy.start()
        self.count += 1
        self.sent.append(copy)
        return copy

    def keep(self, src, dst):
        copy = pltpu.make_async_copy(src, dst, self.send_sem.at[self.count])
        copy.start()
        self.count += 1
        return copy

    def finish(self):
        assert self.count <= self.send_sem.shape[0], self.count
        for copy in self.sent:
            copy.wait_send()


DP, MP, HID = 0, 1, 2


HALF = D // 2


def sin_cos(angles):
    turns = jnp.floor(angles * (2.0 / math.pi) + 0.5)
    r = ((angles - turns * PI_2[0]) - turns * PI_2[1]) - turns * PI_2[2]
    r2 = r * r
    s = r + r * r2 * (-1.6666654611e-1 + r2 * (8.3321608736e-3 + r2 * -1.9515295891e-4))
    c = 1.0 - 0.5 * r2 + r2 * r2 * (4.166664568298827e-2 + r2 * (-1.388731625493765e-3 + r2 * 2.443315711809948e-5))
    quarter = turns - 4.0 * jnp.floor(turns * 0.25)
    odd = (quarter == 1.0) | (quarter == 3.0)
    flip_s = quarter >= 2.0
    flip_c = (quarter == 1.0) | (quarter == 2.0)
    sine = jnp.where(odd, c, s)
    cosine = jnp.where(odd, s, c)
    return jnp.where(flip_s, -sine, sine), jnp.where(flip_c, -cosine, cosine)


def forward_kernel(
    x_ref, c_ref, w1a_ref, w1b_ref, w2_ref, we_ref, wr_ref, cols_ref, rows_ref, pos_ref, rate_ref, seg_ref, present_ref,
    et_out, ft_out, w1_out, qkv_out, out_out, dmid_out, do_out, near_r, near_e, last_sum, wef_ref, wrf_ref,
    lse_ref, p_ref, dbe_ref, dw2_ref, dbf_ref, dgs_ref,
    xt, ct, w1af, w1bf, w2f, rowsf, colsf, rates, tab, et, ft, f, w1, qkv, bias, vt, wb, at, out, wblk, dblk, w2c, theirs, sums,
    send, recv, z_send, z_recv, p_send, p_recv, c_send, c_recv, x_send, x_recv, n_send, n_recv, o_sem, local,
):
    wire = Wire(send, recv)
    d, m, h = wire.me
    dp, mp, hid = wire.size
    rows = D // mp
    wide = D // hid
    fcols = we_ref.shape[1]
    half = rows // dp
    offset = pl.multiple_of(d * half, half)
    half2 = wide // dp
    w2_part = w2_ref
    if w2_ref.shape[0] > half2:
        w2_part = w2_ref.at[pl.ds(pl.multiple_of(d * half2, half2), half2)]
    own = (
        (w1a_ref, lambda mm_, hh: w1af.at[hh, mm_, d], lambda: w1af.at[:, :, d], HID),
        (w1b_ref, lambda mm_, hh: w1bf.at[hh, mm_, d], lambda: w1bf.at[:, :, d], MP),
        (w2_part, lambda mm_, hh: w2f.at[mm_, hh, d], lambda: w2f.at[:, :, d], HID),
    )
    wire.meet()
    waits, stored = [], []
    first, second, third = {}, {}, {}

    def swap(src_ref, dst_ref):
        mine = pl.ds(pl.multiple_of(m * rows, rows), rows)
        moved = []
        for q in range(1, mp):
            to = wire.peer(MP, q)
            moved.append(wire.send(src_ref.at[:, pl.ds(pl.multiple_of(to[1] * SEQ, SEQ), SEQ)], dst_ref.at[mine], to))
        return moved, wire.keep(src_ref.at[:, pl.ds(pl.multiple_of(m * SEQ, SEQ), SEQ)], dst_ref.at[mine])

    def landed(pair):
        for copy in pair[0]:
            copy.wait_recv()
        pair[1].wait()

    def stage_one(i):
        src, dst, _, axis = own[i]
        first[i] = [wire.keep(src, dst(m, h))]
        first[i] += [wire.send(src, dst(m, h), wire.peer(axis, o)) for o in range(1, wire.size[axis])]

    def stage_two(i):
        _, dst, _, axis = own[i]
        other = MP if axis == HID else HID
        second[i] = []
        for o, copy in enumerate(first[i]):
            if o == 0:
                copy.wait()
            else:
                copy.wait_recv()
            at_ = wire.origin(axis, o)
            piece = dst(m, at_) if axis == HID else dst(at_, h)
            second[i] += [wire.send(piece, piece, wire.peer(other, q)) for q in range(1, wire.size[other])]

    def stage_three(i):
        for copy in second[i]:
            copy.wait_recv()
        third[i] = [wire.send(own[i][2](), own[i][2](), wire.peer(DP, r)) for r in range(1, dp)]

    def done(i):
        for copy in third[i]:
            copy.wait_recv()

    full = (wef_ref, wrf_ref)
    part = (we_ref.at[pl.ds(offset, half)], wr_ref.at[pl.ds(offset, half)])
    whole_planes = ((1,), (1, hid - 1))
    order = [0, 1, hid - 1] + list(range(2, hid - 1))

    def plane_of(o):
        return lax.rem(h - o + hid, hid)

    def piece(j, mm_, dd, o):
        at_ = pl.ds(pl.multiple_of(mm_ * rows + dd * half, half), half)
        return full[j].at[at_, pl.ds(pl.multiple_of(plane_of(o) * fcols, fcols), fcols)]

    def remote(src, dst, sems, target):
        return pltpu.make_async_remote_copy(src, dst, sems[0], sems[1], device_id=target, device_id_type=MESH)

    def to_plane(j, o, q):
        src = part[j] if o == 0 else piece(j, m, d, o)
        return remote(src, piece(j, m, d, o), (p_send.at[j, o, q], p_recv.at[j, o, q]), wire.peer(MP, q))

    def to_depth(j, o, k):
        if o in whole_planes[j]:
            src = dst = piece(j, k, d, 0)
        else:
            src, dst = part[j], piece(j, m, d, 0)
        return remote(src, dst, (z_send.at[j, o, k], z_recv.at[j, o, k]), wire.peer(HID, o))

    def depth_count(j, o):
        return mp if o in whole_planes[j] else 1

    def to_core(j, o, k, r):
        return remote(
            piece(j, k, d, o), piece(j, k, d, o), (c_send.at[j, o, k, r - 1], c_recv.at[j, o, k, r - 1]), wire.peer(DP, r)
        )

    def keep_own(j):
        return pltpu.make_async_copy(part[j], piece(j, m, d, 0), local.at[j])

    def plane_start(j, o):
        if o:
            to_depth(j, o, 0).wait_recv()
        else:
            keep_own(j).start()
        for q in range(1, mp):
            to_plane(j, o, q).start()

    def plane_wait(j, o):
        if o == 0:
            keep_own(j).wait()
        for q in range(1, mp):
            to_plane(j, o, q).wait_recv()

    def depth_start(j, o):
        for k in range(depth_count(j, o)):
            to_depth(j, o, k).start()

    def apart(j):
        return [o for o in range(1, hid) if o not in whole_planes[j]]

    def core_start(j, o):
        if o in whole_planes[j]:
            for k in range(mp):
                to_depth(j, o, k).wait_recv()
        elif o:
            plane_wait(j, o)
        for k in range(mp):
            for r in range(1, dp):
                to_core(j, o, k, r).start()

    def arrived(j, o):
        for k in range(mp):
            for r in range(1, dp):
                to_core(j, o, k, r).wait_recv()

    small = [wire.send(cols_ref, colsf.at[m], wire.peer(MP, q)) for q in range(1, mp)]
    small += [wire.send(rows_ref, rowsf.at[h], wire.peer(HID, o)) for o in range(1, hid)]
    kept = [wire.keep(cols_ref, colsf.at[m]), wire.keep(rows_ref, rowsf.at[h])]
    stage_one(0)
    stage_one(1)
    x_in = swap(x_ref, xt)

    rates[...] = jnp.broadcast_to(rate_ref[...], (8, HALF)).T
    places = pos_ref[:, pl.ds(pl.multiple_of(m * SEQ, SEQ), SEQ)].astype(F32)

    def table_rows(j, _):
        at_ = pl.ds(pl.multiple_of(j * 64, 64), 64)
        sine, cosine = sin_cos(rates[at_, 0:1] * places)
        tab[at_, :] = sine
        tab[pl.ds(pl.multiple_of(j * 64 + HALF, 64), 64), :] = cosine
        return 0

    lax.fori_loop(0, 1, table_rows, 0)
    stage_two(0)
    stage_two(1)
    lax.fori_loop(1, HALF // 64, table_rows, 0)
    fill_bias(bias, seg_ref, present_ref)
    for copy in small:
        copy.wait_recv()
    for copy in kept:
        copy.wait()
    for mm_ in range(mp):
        p_ref[mm_ * rows : (mm_ + 1) * rows, 0:8] = colsf[mm_].T[:rows, :]
    wb[...] = jnp.zeros_like(wb)
    for hh in range(hid):
        wb[:, hh * wide : (hh + 1) * wide] = rowsf[hh, 1:2, :wide]
        wb[:, 2 * D + hh * wide : 2 * D + (hh + 1) * wide] = rowsf[hh, 2:3, :wide]
    landed(x_in)

    def norm_cols(j, _):
        cols = pl.ds(pl.multiple_of(j * 256, 256), 256)
        e = xt[:, cols].astype(F32) + tab[:, cols]
        et[:, cols] = e
        average, inv = norm_stats(e)
        low = ((e - average) * inv * p_ref[:, 0:1] + p_ref[:, 1:2]).astype(BF16)
        ft[:, cols] = low
        f[cols, :] = low.T
        return 0

    lax.fori_loop(0, SEQ // 256, norm_cols, 0)
    stored += [wire.keep(et, et_out), wire.keep(ft, ft_out)]
    stage_three(0)
    stage_three(1)
    for j in (1, 0):
        for o in apart(j):
            depth_start(j, o)
    plane_start(1, 0)
    stage_one(2)
    plane_start(0, 0)
    c_in = swap(c_ref, ct)
    def unpack(dd):
        for hh in range(hid):
            for mm_ in range(mp):
                at_ = slice(mm_ * rows + dd * half, mm_ * rows + (dd + 1) * half)
                for k in range(3):
                    if k < 2:
                        value = w1af[hh, mm_, dd, :, k * wide : (k + 1) * wide]
                    else:
                        value = w1bf[hh, mm_, dd]
                    w1[at_, k * D + hh * wide : k * D + (hh + 1) * wide] = value

    if dp == 2:
        for dd in range(dp):

            @pl.when(d == dd)
            def _():
                unpack(dd)

        done(0)
        done(1)
        for dd in range(dp):

            @pl.when(d == 1 - dd)
            def _():
                unpack(dd)

    else:
        done(0)
        done(1)
        for dd in range(dp):
            unpack(dd)
    stored.append(wire.keep(w1, w1_out))

    def cols_of(n, scale):
        cols = pl.ds(pl.multiple_of(n * 256, 256), 256)
        y = (mm(f[...], w1[:, cols]) + wb[:, cols]).astype(BF16)
        qkv[:, cols] = y * jnp.asarray(scale, BF16)
        return 0

    lax.fori_loop(0, D // 256, lambda n, c: cols_of(n, HD**-0.5), 0)
    stage_two(2)
    plane_wait(1, 0)
    for o in whole_planes[1]:
        depth_start(1, o)
    lax.fori_loop(D // 256, 3 * D // 256, lambda n, c: cols_of(n, 1.0), 0)
    stored.append(wire.keep(qkv, qkv_out))

    low = lax.broadcasted_iota(jnp.int32, (SEQ, PAIR), 1) < HD
    lse_ref[...] = jnp.zeros_like(lse_ref)

    def pair_of(p, _):
        lanes = pl.ds(pl.multiple_of(p * PAIR, PAIR), PAIR)
        k_lanes = pl.ds(pl.multiple_of(p * PAIR + D, PAIR), PAIR)
        v_lanes = pl.ds(pl.multiple_of(p * PAIR + 2 * D, PAIR), PAIR)
        vt[...] = qkv[:, v_lanes].T
        q = qkv[:, lanes]
        for hh in range(2):
            qm = jnp.where(low if hh == 0 else ~low, q, jnp.zeros_like(q))
            s = mm(qkv[:, k_lanes], qm, NT) + bias[...]
            top = jnp.max(s, axis=0, keepdims=True)
            e = jnp.exp(s - top)
            total = jnp.sum(e, axis=0, keepdims=True)
            o = mm(vt[hh * HD : (hh + 1) * HD, :], e.astype(BF16)) / total
            at[pl.ds(pl.multiple_of(p * PAIR + hh * HD, HD), HD), :] = o.astype(BF16)
            lse_ref[p, hh : hh + 1, :] = top + jnp.log(total)
        return 0

    lax.fori_loop(0, PAIRS // 3, pair_of, 0)
    plane_wait(0, 0)
    for o in whole_planes[0]:
        depth_start(0, o)
    for j in (1, 0):
        for o in apart(j):
            plane_start(j, o)
    lax.fori_loop(PAIRS // 3, 2 * PAIRS // 3, pair_of, 0)
    stage_three(2)
    for j in range(2):
        core_start(j, 0)
    lax.fori_loop(2 * PAIRS // 3, PAIRS, pair_of, 0)
    for copy in stored:
        copy.wait()
    landed(c_in)
    done(2)

    ot, ds_sum, st, bt, mid = bias.at[pl.ds(0, D)], tab, xt, ft, et
    tokens = [pl.ds(n * D, D) for n in range(3)]
    for mm_ in range(mp):
        for hh in range(hid):
            for dd in range(dp):
                at_ = hh * wide + dd * (wide // dp)
                w2c[at_ : at_ + wide // dp, mm_ * rows : (mm_ + 1) * rows] = w2f[mm_, hh, dd]
    w2t = w2c[...].T

    def middle_cols(j, _):
        cols = pl.ds(pl.multiple_of(j * 256, 256), 256)
        value = et[:, cols] + (mm(w2t, at[:, cols]) + p_ref[:, 4:5])
        mid[:, cols] = value
        ot[:, cols] = value + p_ref[:, 5:6]
        average, inv = norm_stats(value)
        s = ((value - average) * inv * p_ref[:, 2:3] + p_ref[:, 3:4]).astype(BF16)
        st[:, cols] = s
        qkv[cols, tokens[0]] = s.T
        qkv[cols, tokens[1]] = ct[:, cols].T
        return 0

    lax.fori_loop(0, SEQ // 256, middle_cols, 0)
    ds_sum[...] = jnp.zeros_like(ds_sum)

    def fetch(j, o):
        hcols = pl.ds(pl.multiple_of(plane_of(o) * fcols, fcols), fcols)
        return pltpu.make_async_copy(full[j].at[:, hcols], wblk.at[j], local.at[2 + j])

    def place(n):
        o = 0
        for k in range(1, hid):
            o = jnp.where(n == k, order[k], o)
        return o

    def swap_core(j, n, k, r):
        to = wire.peer(DP, r)
        return remote(
            dblk.at[j, k, to[0]], theirs.at[lax.rem(n, 2), j, r - 1, k], (x_send.at[j, n, k, r - 1], x_recv.at[j, n, k, r - 1]), to
        )

    def each_core(n, do):
        for j in range(2):
            for k in range(mp):
                for r in range(1, dp):
                    do(swap_core(j, n, k, r))

    end = hid - 1

    def sum_depth(n):
        to = (d, m, plane_of(place(n)))
        return remote(sums.at[lax.rem(n, 2), 0], near_r.at[n], (n_send.at[n, 0], n_recv.at[n, 0]), to)

    def sum_plane(n, q):
        to = wire.peer(MP, q)
        return remote(sums.at[lax.rem(n, 2), 1, to[1]], near_e.at[n, q], (n_send.at[n, q], n_recv.at[n, q]), to)

    def save(j, n, last):
        slot = lax.rem(n, 2)
        if last:
            return pltpu.make_async_copy(sums.at[slot, j], last_sum.at[j], o_sem.at[j, n])
        if j == 0:
            return pltpu.make_async_copy(sums.at[0, 0], near_r.at[0], o_sem.at[0, 0])
        return pltpu.make_async_copy(sums.at[slot, 1, m], near_e.at[n, 0], o_sem.at[1, n])

    def add_cores(n, last=False):
        each_core(n, lambda copy: copy.wait_recv())
        slot = lax.rem(n, 2)
        for j in range(2):
            for k in range(mp):
                value = dblk[j, k, d].astype(F32)
                for r in range(1, dp):
                    value = value + theirs[slot, j, r - 1, k].astype(F32)
                sums[slot, j, k] = value.astype(BF16)
        if last:
            for j in range(2):
                save(j, n, True).start()
            return
        for q in range(1, mp):
            sum_plane(n, q).start()
        save(1, n, False).start()

    def gone(n):
        for q in range(1, mp):
            sum_plane(n, q).wait_send()
        save(1, n, False).wait()

    def block(n, _):
        o = place(n)
        hh = plane_of(o)
        for j in range(2):
            arrived(j, o)
        for j in range(2):
            fetch(j, o).start()
        for j in range(2):
            fetch(j, o).wait()

        pre = mm(qkv[:, tokens[0]], wblk[0]) + rowsf[hh, 0:1, :]
        cdf = 0.5 * (1.0 + lax.erf(pre * (1.0 / math.sqrt(2.0))))
        act = (pre * cdf).astype(BF16)
        slope = cdf + pre * jnp.exp(-0.5 * pre * pre) * (1.0 / math.sqrt(2.0 * math.pi))
        grad = (mm(qkv[:, tokens[1]], wblk[1]) * slope).astype(BF16)

        @pl.when(n == 3)
        def _():
            gone(0)
            save(0, 0, False).wait()

        @pl.when(n > 3)
        def _():
            gone(n - 3)
            sum_depth(n - 3).wait_send()

        @pl.when(n > 0)
        def _():
            add_cores(n - 1)
            each_core(n - 1, lambda copy: copy.wait_send())

        @pl.when(n == 1)
        def _():
            save(0, 0, False).start()

        @pl.when(n > 1)
        def _():
            sum_depth(n - 1).start()

        for j, value in enumerate((mm(ct[...], act), mm(st[...], grad))):
            for k in range(mp):
                for dd in range(dp):
                    at_ = k * rows + dd * half
                    dblk[j, k, dd] = value[at_ : at_ + half, :].astype(BF16)
        each_core(n, lambda copy: copy.start())
        dbe_ref[hh, 0:1, :] = jnp.sum(grad.astype(F32), axis=0, keepdims=True)
        ot[...] += mm(wblk[1], act, NT)
        ds_sum[...] += mm(wblk[0], grad, NT)

        for k in range(1, hid):

            @pl.when(n + 1 == k)
            def _():
                for j in range(2):
                    core_start(j, order[k])

        return 0

    lax.fori_loop(0, hid, block, 0)
    gone(end - 2)
    sum_depth(end - 2).wait_send()
    add_cores(end, True)
    dgs_ref[...] = jnp.zeros_like(dgs_ref)

    def back_cols(j, _):
        cols = pl.ds(pl.multiple_of(j * 256, 256), 256)
        value = mid[:, cols]
        out[:, cols] = ot[:, cols].astype(BF16)
        average, inv = norm_stats(value)
        normed = (value - average) * inv
        ds = ds_sum[:, cols]
        scaled = ds * p_ref[:, 2:3]
        total = jnp.sum(scaled, axis=0, keepdims=True) * (1.0 / D)
        crossed = jnp.sum(scaled * normed, axis=0, keepdims=True) * (1.0 / D)
        dmid = ct[:, cols].astype(F32) + inv * (scaled - total - normed * crossed)
        mid[:, cols] = dmid
        low_ = dmid.astype(BF16)
        bt[:, cols] = low_
        qkv[cols, tokens[2]] = mm(w2c[...], low_).astype(BF16).T
        dgs_ref[0] += lane_sums(ds * normed)
        dgs_ref[1] += lane_sums(ds)
        return 0

    lax.fori_loop(0, SEQ // 256, back_cols, 0)
    last = [wire.keep(out, out_out), wire.keep(mid, dmid_out), wire.keep(qkv.at[:, tokens[2]], do_out)]
    ones = jnp.ones((8, SEQ), BF16)
    dbf_ref[0] = mm(ones, ct[...], NT)
    dbf_ref[1] = mm(ones, bt[...], NT)
    for j in range(mp):
        dw2_ref[j] = mm(at[...], bt[j * rows : (j + 1) * rows, :], NT).astype(BF16)
    each_core(end, lambda copy: copy.wait_send())
    gone(end - 1)
    sum_depth(end - 1).wait_send()
    for j in range(2):
        save(j, end, True).wait()
    for n in range(end):
        if n:
            sum_depth(n).wait_recv()
        for q in range(1, mp):
            sum_plane(n, q).wait_recv()
    for copy in last:
        copy.wait()
    wire.finish()
    for j in range(2):
        for o in range(hid):
            if o:
                for k in range(depth_count(j, o)):
                    to_depth(j, o, k).wait_send()
            if o not in whole_planes[j]:
                for q in range(1, mp):
                    to_plane(j, o, q).wait_send()
            for k in range(mp):
                for r in range(1, dp):
                    to_core(j, o, k, r).wait_send()


def forward(x, c, w1a, w1b, w2, we, wr, cols, rows, pos, rate, seg, present):
    dp, mp, hid = lax.axis_size("dp"), lax.axis_size("mp"), lax.axis_size("hidden")
    half = D // mp // dp
    fc = we.shape[1]
    ff = hid * fc
    sds = jax.ShapeDtypeStruct
    out_shape = (
        sds((D, SEQ), F32), sds((D, SEQ), BF16), sds((D, 3 * D), BF16), sds((SEQ, 3 * D), BF16),
        sds((D, SEQ), BF16), sds((D, SEQ), F32), sds((SEQ, D), BF16), sds((hid - 1, mp, half, fc), BF16),
        sds((hid - 1, mp, half, fc), BF16), sds((2, mp, half, fc), BF16), sds((D, ff), BF16), sds((D, ff), BF16),
        sds((PAIRS, 8, SEQ), F32), sds((D, 128), F32), sds((hid, 8, fc), F32), sds((mp, D, D // mp), BF16),
        sds((2, 8, D), F32), sds((2, D, 128), F32),
    )
    n = (mp - 1) + (hid - 1) + 2 + 2 * hid + mp + 2 * hid * (mp - 1) + mp * (hid - 1) + 3 * (dp - 1) + 2 * mp + 7
    hbm = pl.BlockSpec(memory_space=pl.ANY)
    vmem = pl.BlockSpec(memory_space=pltpu.VMEM)
    vm = lambda dtype, *shape: pltpu.VMEM(shape, dtype)
    sem = lambda *shape: pltpu.SemaphoreType.DMA(shape)
    return pl.pallas_call(
        forward_kernel,
        out_shape=out_shape,
        in_specs=[hbm] * 9 + [vmem] * 4,
        out_specs=(hbm,) * 12 + (vmem,) * 6,
        scratch_shapes=[
            vm(BF16, D, SEQ), vm(BF16, D, SEQ), vm(BF16, hid, mp, dp, half, w1a.shape[1]),
            vm(BF16, hid, mp, dp, half, w1b.shape[1]), vm(BF16, mp, hid, dp, D // hid // dp, w2.shape[1]), vm(F32, hid, *rows.shape),
            vm(F32, mp, *cols.shape), vm(F32, HALF, 8),
            vm(F32, D, SEQ), vm(F32, D, SEQ), vm(BF16, D, SEQ), vm(BF16, SEQ, D), vm(BF16, D, 3 * D),
            vm(BF16, SEQ, 3 * D), vm(F32, SEQ, SEQ), vm(BF16, PAIR, SEQ), vm(F32, 1, 3 * D),
            vm(BF16, D, SEQ), vm(BF16, D, SEQ), vm(BF16, 2, D, fc), vm(BF16, 2, mp, dp, half, fc), vm(BF16, D, D),
            vm(BF16, 2, 2, dp - 1, mp, half, fc), vm(BF16, 2, 2, mp, half, fc),
            sem(n), sem(n), sem(2, hid, mp), sem(2, hid, mp), sem(2, hid, mp), sem(2, hid, mp),
            sem(2, hid, mp, dp - 1), sem(2, hid, mp, dp - 1), sem(2, hid, mp, dp - 1), sem(2, hid, mp, dp - 1),
            sem(hid, mp), sem(hid, mp), sem(2, hid), sem(4),
        ],
        compiler_params=params(collective_id=0, has_side_effects=True),
        name="forward",
    )(x, c, w1a, w1b, w2, we, wr, cols, rows, pos, rate, seg, present)


def backward_kernel(
    o_ref, dw2_ref, near_r, near_e, last_sum, qkv_in, do_in, lse_ref, seg_ref, present_ref, ft_in, w_in, et_in, dmid_in, p_ref,
    dbe_ref, dbf_ref, dgs_ref,
    of_ref, xf_ref, g1_ref, g2_ref, ge_ref, gr_ref, vecf_ref,
    qkv, do, bias, kt, dqt, dk, dv, dka, dva, ft, et, dmid, dgp,
    a0, a1, a2, o0, o1, s2, b0, b1, b2, be, br, t0, t1, t2, t3, t4, c0, c1, c2, c3, c4,
    v0, va, vb, vc, v1, v2, loads, send, recv,
):
    wire = Wire(send, recv)
    d, m, h = wire.me
    dp, mp, hid = wire.size
    rows = D // mp
    wide = D // hid
    half = rows // dp
    fcols = ge_ref.shape[1]
    v_in = (va, vb, vc)
    slab0 = o0.shape[1:]
    hslice = lambda hh: pl.ds(pl.multiple_of(hh * fcols, fcols), fcols)

    def load(n, src, dst):
        copy = pltpu.make_async_copy(src, dst, loads.at[n])
        copy.start()
        return copy

    parts = []
    for p in range(PAIRS):
        got = []
        for k in range(3):
            lanes = slice(k * D + p * PAIR, k * D + (p + 1) * PAIR)
            got.append(load(4 * p + k, qkv_in.at[:, lanes], qkv.at[:, lanes]))
        lanes = slice(p * PAIR, (p + 1) * PAIR)
        got.append(load(4 * p + 3, do_in.at[:, lanes], do.at[:, lanes]))
        parts.append(got)
    others = [load(4 * PAIRS + i, a, b) for i, (a, b) in enumerate(((ft_in, ft), (et_in, et), (dmid_in, dmid)))]
    wire.meet()
    items = (
        (lambda dd: o0.at[dd], a0, o0.at[d], b0, t0, c0, None, MP, HID),
        (lambda dd: o1.at[dd], a1, o1.at[d], b1, t1, c1, None, HID, HID),
        (lambda dd: dw2_ref.at[:, :, dd], a2, s2, b2, t2, c2, g2_ref, MP, MP),
        (None, None, None, be, t3, c3, ge_ref, MP, None),
        (None, None, None, br, t4, c4, gr_ref, HID, None),
    )
    core, kept, near, far = {}, {}, {}, {}
    end = hid - 1
    plane = lambda o: lax.rem(h - o + hid, hid)
    order = [0, 1, hid - 1] + list(range(2, hid - 1))
    at = 4 * PAIRS + 4
    own = {
        4: [load(at, near_r, br.at[pl.ds(0, end)])],
        3: [load(at + 1 + n, near_e.at[n], be.at[:, :, hslice(plane(order[n]))]) for n in range(end)],
    }
    own[3].append(load(at + 1 + end, last_sum.at[1, m], be.at[0, :, hslice(plane(order[end]))]))

    def stage_core(i):
        src, a, s = items[i][:3]
        core[i] = [wire.send(src(wire.peer(DP, r)[0]), a.at[r - 1], wire.peer(DP, r)) for r in range(1, dp)]
        if i > 1:
            kept[i] = wire.keep(src(d), s)

    def add_all(dst, own, others, shape):
        lead = shape[:-2]

        def body(n, _):
            index = []
            for size in reversed(lead):
                index.insert(0, lax.rem(n, size))
                n = lax.div(n, size)
            index = tuple(index)
            value = own[index].astype(F32)
            for j in range(others.shape[0]):
                value = value + others[(j,) + index].astype(F32)
            dst[index] = value.astype(dst.dtype)
            return 0

        lax.fori_loop(0, math.prod(lead), body, 0)

    def part(i, ref, axis, at, leads):
        if items[i][8] is None:
            return ref.at[(slice(None),) * len(leads) + (slice(None), hslice(at))] if axis == HID else ref.at[at]
        return ref.at[at] if leads[0] == axis else ref.at[:, at]

    def leads_of(i):
        lead = items[i][8]
        return (MP,) if lead is None else ((HID, MP) if lead == HID else (MP, HID))

    def stage_near(i):
        if i == 4:
            near[4] = [wire.send(last_sum.at[0], br.at[end], wire.peer(HID, hid - order[end]))]
            return
        if i == 3:
            here = hslice(plane(order[end]))
            near[3] = []
            for q in range(1, mp):
                to = wire.peer(MP, q)
                near[3].append(wire.send(last_sum.at[1, to[1]], be.at[q, :, here], to))
            return
        _, a, s, b, t, c, g, axis, _ = items[i]
        for copy in core[i]:
            copy.wait_recv()
        if i in kept:
            kept[i].wait()
        add_all(s, s, a, s.shape)
        near[i] = [
            wire.send(part(i, s, axis, wire.peer(axis, q)[axis], leads_of(i)), b.at[q - 1], wire.peer(axis, q))
            for q in range(1, wire.size[axis])
        ]

    def stage_far(i):
        _, a, s, b, t, c, g, axis, lead = items[i]
        if i < 3:
            for copy in near[i] if i else nears_half[0] + nears_half[1]:
                copy.wait_recv()
            add_all(t, part(i, s, axis, wire.me[axis], leads_of(i)), b, t.shape)
        else:
            for copy in near[i]:
                copy.wait_recv()
            for copy in own[i]:
                copy.wait()
            add_all(t, b.at[0], b.at[pl.ds(1, b.shape[0] - 1)], t.shape)
        other = MP if axis == HID else HID
        left = tuple(x for x in leads_of(i) if x != axis)
        far[i] = []
        for q in range(1, wire.size[other]):
            to = wire.peer(other, q)
            far[i].append(wire.send(part(i, t, other, to[other], left), c.at[q - 1], to))

    def stage_end(i):
        _, a, s, b, t, c, g, axis, lead = items[i]
        other = MP if axis == HID else HID
        left = tuple(x for x in leads_of(i) if x != axis)
        for copy in far[i]:
            copy.wait_recv()
        value = part(i, t, other, wire.me[other], left)[...].astype(F32)
        for j in range(c.shape[0]):
            value = value + c[j].astype(F32)
        if i == 0:
            g1_ref[0] = value[:, :wide]
            g1_ref[1] = value[:, wide:]
        elif i == 1:
            g1_ref[2] = value
        else:
            g[...] = value

    moved, held = [], []

    def swap(src_ref, dst_ref):
        mine = pl.ds(pl.multiple_of(m * SEQ, SEQ), SEQ)
        for q in range(1, mp):
            to = wire.peer(MP, q)
            moved.append(wire.send(src_ref.at[pl.ds(pl.multiple_of(to[1] * rows, rows), rows)], dst_ref.at[:, mine], to))
        held.append(wire.keep(src_ref.at[pl.ds(pl.multiple_of(m * rows, rows), rows)], dst_ref.at[:, mine]))

    vec = {}

    def vec_send(axis, src):
        vec[axis] = [wire.send(src, v_in[axis].at[o - 1], wire.peer(axis, o)) for o in range(1, wire.size[axis])]

    def vec_sum(axis, src, dst):
        for copy in vec[axis]:
            copy.wait_recv()
        total = src[...]
        for j in range(wire.size[axis] - 1):
            total = total + v_in[axis][j]
        dst[...] = total

    stage_near(4)
    stage_near(3)
    stage_core(2)
    swap(o_ref, of_ref)
    fill_bias(bias, seg_ref, present_ref)
    low = lax.broadcasted_iota(jnp.int32, (QBB, PAIR), 1) < HD

    def pair_of(p, _):
        off = pl.multiple_of(p * PAIR, PAIR)
        lanes = pl.ds(off, PAIR)
        k_lanes = pl.ds(pl.multiple_of(off + D, PAIR), PAIR)
        v_lanes = pl.ds(pl.multiple_of(off + 2 * D, PAIR), PAIR)
        kt[...] = qkv[:, k_lanes].T
        dka[...] = jnp.zeros_like(dka)
        dva[...] = jnp.zeros_like(dva)

        def block(j, _):
            cols = pl.ds(pl.multiple_of(j * QBB, QBB), QBB)
            q = qkv[cols, lanes]
            g = do[cols, lanes]
            for hh in range(2):
                keep = low if hh == 0 else ~low
                qm = jnp.where(keep, q, jnp.zeros_like(q))
                gm = jnp.where(keep, g, jnp.zeros_like(g))
                e = jnp.exp(mm(qkv[:, k_lanes], qm, NT) + bias[:, cols] - lse_ref[p, hh : hh + 1, cols])
                t = e * mm(qkv[:, v_lanes], gm, NT)
                ds = (t - e * jnp.sum(t, axis=0, keepdims=True)).astype(BF16)
                dva[...] += mm(e.astype(BF16), gm)
                dka[...] += mm(ds, qm)
                dq = mm(kt[hh * HD : (hh + 1) * HD, :], ds) * HD**-0.5
                dqt[pl.ds(pl.multiple_of(off + hh * HD, HD), HD), cols] = dq.astype(BF16)
            return 0

        lax.fori_loop(0, SEQ // QBB, block, 0)
        dk[:, lanes] = dka[...].astype(BF16)
        dv[:, lanes] = dva[...].astype(BF16)
        return 0

    def pairs(first, last):
        for p in range(first, last):
            for copy in parts[p]:
                copy.wait()
        lax.fori_loop(first, last, pair_of, 0)

    span = D // 2
    each = hid // 2

    def weight_half(g):
        wide_k = mm(ft[...], dk[:, g * span : (g + 1) * span]).astype(BF16)
        wide_v = mm(ft[...], dv[:, g * span : (g + 1) * span]).astype(BF16)
        for hh in range(g * each, (g + 1) * each):
            lanes = slice((hh - g * each) * wide, (hh - g * each + 1) * wide)
            value_q = mm(ft[...], dqt[hh * wide : (hh + 1) * wide, :], NT).astype(BF16)
            for mm_ in range(mp):
                for dd in range(dp):
                    at_ = slice(mm_ * rows + dd * half, mm_ * rows + (dd + 1) * half)
                    o0[dd, hh, mm_, :, 0:wide] = value_q[at_, :]
                    o0[dd, hh, mm_, :, wide : 2 * wide] = wide_k[at_, lanes]
                    o1[dd, hh, mm_] = wide_v[at_, lanes]

    cores_half, nears_half = {}, {}

    def core_half(g):
        hs = pl.ds(g * each, each)
        cores_half[g] = [
            wire.send(o0.at[wire.peer(DP, r)[0], hs], a0.at[r - 1, hs], wire.peer(DP, r)) for r in range(1, dp)
        ]

    def near_half(g):
        hs = pl.ds(g * each, each)
        for copy in cores_half[g]:
            copy.wait_recv()
        add_all(o0.at[d, hs], o0.at[d, hs], a0.at[:, hs], (each,) + slab0[1:])
        nears_half[g] = []
        for q in range(1, mp):
            to = wire.peer(MP, q)
            nears_half[g].append(wire.send(o0.at[d, hs, to[1]], b0.at[q - 1, hs], to))

    pairs(0, PAIRS // 2)
    stage_near(2)
    for copy in others:
        copy.wait()
    weight_half(0)
    core_half(0)
    pairs(PAIRS // 2, PAIRS // 2 + 1)
    near_half(0)
    pairs(PAIRS // 2 + 1, PAIRS)
    w1 = qkv.at[pl.ds(0, D)]
    w_load = load(4 * PAIRS + 3, w_in, w1)
    weight_half(1)
    stage_core(1)
    core_half(1)
    df = bias.at[pl.ds(0, D)]
    w_load.wait()
    dx = ft

    def feature_cols(j, _):
        cols = pl.ds(pl.multiple_of(j * 256, 256), 256)
        value = mm(w1[:, 0:D], dqt[:, cols])
        value += mm(w1[:, D : 2 * D], dk[cols, :], NT)
        value += mm(w1[:, 2 * D : 3 * D], dv[cols, :], NT)
        df[:, cols] = value
        return 0

    lax.fori_loop(0, SEQ // 256, feature_cols, 0)
    stage_near(1)
    near_half(1)
    dgp[...] = jnp.zeros_like(dgp)

    def norm_cols(j, _):
        cols = pl.ds(pl.multiple_of(j * 256, 256), 256)
        e = et[:, cols]
        average, inv = norm_stats(e)
        normed = (e - average) * inv
        g = df[:, cols]
        scaled = g * p_ref[:, 0:1]
        total = jnp.sum(scaled, axis=0, keepdims=True) * (1.0 / D)
        crossed = jnp.sum(scaled * normed, axis=0, keepdims=True) * (1.0 / D)
        dx[:, cols] = (dmid[:, cols] + inv * (scaled - total - normed * crossed)).astype(BF16)
        dgp[0] += lane_sums(g * normed)
        dgp[1] += lane_sums(g)
        return 0

    lax.fori_loop(0, SEQ // 256, norm_cols, 0)
    swap(dx, xf_ref)
    for i in (3, 2, 4):
        stage_far(i)
    ones = jnp.ones((8, SEQ), BF16)
    v0[...] = jnp.zeros_like(v0)
    for n in range(2):
        v0[n : n + 1, :] = jnp.sum(dgp[n].T, axis=0, keepdims=True)
        v0[2 + n : 3 + n, :] = jnp.sum(dgs_ref[n].T, axis=0, keepdims=True)
        v0[6 + n : 7 + n, :] = dbf_ref[n, 0:1, :]
    v0[4:5, :] = mm(ones, dqt[...], NT)[0:1]
    v0[5:6, :] = mm(ones, dv[...])[0:1]
    for hh in range(hid):
        row, lane = divmod(hh * fcols, D)
        v0[8 + row : 9 + row, lane : lane + fcols] = dbe_ref[hh, 0:1, :]
    vec_send(DP, v0)
    vec_sum(DP, v0, v1)
    vec_send(MP, v1)
    stage_far(1)
    stage_far(0)
    vec_sum(MP, v1, v2)
    vec_send(HID, v2)
    stage_end(3)
    stage_end(2)
    stage_end(4)
    stage_end(1)
    stage_end(0)
    vec_sum(HID, v2, vecf_ref)
    for copy in held:
        copy.wait()
    for copy in moved:
        copy.wait_recv()
    wire.finish()


def backward(o, dw2, near_r, near_e, last_sum, qkv, do, lse, seg, present, ft, w1, et, dmid, cols, dbe, dbf, dgs):
    dp, mp, hid = lax.axis_size("dp"), lax.axis_size("mp"), lax.axis_size("hidden")
    sds = jax.ShapeDtypeStruct
    wide = D // hid
    half = D // mp // dp
    half2, c2 = dw2.shape[3:]
    fc = near_e.shape[3]
    ff = hid * fc
    out_shape = (
        sds((D // mp, mp * SEQ), BF16), sds((D // mp, mp * SEQ), BF16), sds((3, half, wide), F32),
        sds((half2, c2), F32), sds((half, fc), F32), sds((half, fc), F32), sds((16, D), F32),
    )
    vm = lambda *shape: pltpu.VMEM(shape, BF16)
    vf = lambda *shape: pltpu.VMEM(shape, F32)
    slabs = ((hid, mp, half, 2 * wide), (hid, mp, half, wide), (mp, hid, half2, c2))
    after = ((hid, half, 2 * wide), (mp, half, wide), (hid, half2, c2), (half, ff), (mp, half, fc))
    ends = ((half, 2 * wide), (half, wide), (half2, c2), (half, fc), (half, fc))
    near = (mp, hid, mp, mp, hid)
    far = (hid, mp, hid, hid, mp)
    scratch = [
        vm(SEQ, 3 * D), vm(SEQ, D), vf(SEQ, SEQ), vm(PAIR, SEQ), vm(D, SEQ), vm(SEQ, D), vm(SEQ, D),
        vf(SEQ, PAIR), vf(SEQ, PAIR), vm(D, SEQ), vf(D, SEQ), vf(D, SEQ), vf(2, D, 128),
    ]
    scratch += [vm(dp - 1, *s) for s in slabs]
    scratch += [vm(dp, *s) for s in slabs[:2]] + [vm(*s) for s in slabs[2:]]
    scratch += [vm(n - 1, *s) for n, s in zip(near[:3], after)] + [vm(n, *s) for n, s in zip(near[3:], after[3:])]
    scratch += [vm(*s) for s in after]
    scratch += [vm(n - 1, *s) for n, s in zip(far, ends)]
    scratch += [vf(16, D), vf(dp - 1, 16, D), vf(mp - 1, 16, D), vf(hid - 1, 16, D), vf(16, D), vf(16, D)]
    n = dp + mp + hid - 3 + 2 * mp + 4 * (dp - 1) + 1 + 6 * (mp + hid - 2)
    scratch += [pltpu.SemaphoreType.DMA((4 * PAIRS + 6 + hid,)), pltpu.SemaphoreType.DMA((n,)), pltpu.SemaphoreType.DMA((n,))]
    hbm = pl.BlockSpec(memory_space=pl.ANY)
    vmem = pl.BlockSpec(memory_space=pltpu.VMEM)
    return pl.pallas_call(
        backward_kernel,
        out_shape=out_shape,
        in_specs=[hbm] * 7 + [vmem] * 3 + [hbm] * 4 + [vmem] * 4,
        out_specs=(hbm, hbm) + (vmem,) * 5,
        scratch_shapes=scratch,
        compiler_params=params(collective_id=1, has_side_effects=True),
        name="backward",
    )(o, dw2, near_r, near_e, last_sum, qkv, do, lse, seg, present, ft, w1, et, dmid, cols, dbe, dbf, dgs)


def local(
    stored, positions, segments, present, norm_gains, norm_biases, input_proj, input_bias, output_proj,
    output_bias, expand_weight, expand_bias, reduce_weight, reduce_bias, cotangent,
):
    mp, hid, dp = lax.axis_size("mp"), lax.axis_size("hidden"), lax.axis_size("dp")
    m, h, d = lax.axis_index("mp"), lax.axis_index("hidden"), lax.axis_index("dp")
    rows_mp, hcols, fcols = D // mp, D // hid, expand_weight.shape[1]
    half = rows_mp // dp
    cols = [norm_gains[:1], norm_biases[:1], norm_gains[1:], norm_biases[1:], output_bias[None], reduce_bias[None]]
    cols = jnp.concatenate([c.astype(F32) for c in cols] + [jnp.zeros((2, rows_mp), F32)])
    cols = jnp.pad(cols, ((0, 0), (0, -rows_mp % 128)))
    rows = jnp.concatenate(
        [
            expand_bias.astype(F32)[None],
            jnp.pad(input_bias.astype(F32), ((0, 0), (0, fcols - hcols))),
            jnp.zeros((5, fcols), F32),
        ]
    )
    w1 = lax.dynamic_slice_in_dim(input_proj, d * half, half, 0)
    w2 = output_proj
    if hcols // dp % 16:
        w2 = lax.dynamic_slice_in_dim(output_proj, d * (hcols // dp), hcols // dp, 0)
    pos = positions[None]
    rate = np.exp(np.arange(D // 2, dtype=np.float32) * np.float32(-math.log(10000.0) / (D // 2)))[None]
    seg, present = segments[None], present[None]
    et, ft, w1f, qkv, out_t, dmid, do, near_r, near_e, last_sum, _, _, lse, cols, dbe, dw2, dbf, dgs = forward(
        stored, cotangent, w1[:, :2].reshape(half, 2 * hcols), w1[:, 2], w2, expand_weight, reduce_weight, cols, rows,
        pos, jnp.asarray(rate), seg, present,
    )
    output, d_stored, g1, d_output, d_expand, d_reduce, vec = backward(
        out_t,
        dw2.reshape(mp, hid, dp, hcols // dp, rows_mp),
        near_r,
        near_e,
        last_sum,
        qkv, do, lse, seg, present, ft, w1f, et, dmid, cols, dbe, dbf, dgs,
    )
    piece = D // (hid * mp * dp)
    cut = lambda x, at, size: lax.dynamic_slice_in_dim(x, at * size, size, x.ndim - 1)
    dg = cut(vec[:4].reshape(2, 2, D), (m * dp + d) * hid + h, piece)
    db_proj = cut(vec[4:6], h * dp + d, hcols // dp)
    db_feed = cut(vec[6:8], m * dp + d, half)
    dbe = cut(vec[8:].reshape(-1)[: hid * fcols], h * dp + d, fcols // dp)
    d_input = g1.transpose(1, 0, 2)
    return (
        output, d_stored.astype(F32), dg[:, 0], dg[:, 1], d_input, db_proj, d_output, db_feed[1], d_expand, dbe, d_reduce,
        db_feed[0],
    )


def solution(mesh):
    placed = (
        P("mp", ("dp", "hidden")),
        P(("dp", "hidden")),
        P(("dp", "hidden", "mp")),
        P(("dp", "hidden", "mp")),
        P(None, "mp"),
        P(None, "mp"),
        P("mp", None, "hidden"),
        P(None, "hidden"),
        P("hidden", "mp"),
        P("mp"),
        P("mp", "hidden"),
        P("hidden"),
        P("mp", "hidden"),
        P("mp"),
        P("mp", ("dp", "hidden")),
    )
    return jax.shard_map(
        local,
        mesh=mesh,
        in_specs=placed,
        out_specs=(
            P("mp", ("dp", "hidden")),
            P("mp", ("dp", "hidden")),
            P(None, ("mp", "dp", "hidden")),
            P(None, ("mp", "dp", "hidden")),
            P(("mp", "dp"), None, "hidden"),
            P(None, ("hidden", "dp")),
            P(("hidden", "dp"), "mp"),
            P(("mp", "dp")),
            P(("mp", "dp"), "hidden"),
            P(("hidden", "dp")),
            P(("mp", "dp"), "hidden"),
            P(("mp", "dp")),
        ),
        check_vma=False,
    )
```

```python
import functools
import math

import jax
import jax.numpy as jnp
import numpy as np
from jax import lax
from jax.experimental import pallas as pl
from jax.experimental.pallas import tpu as pltpu
from jax.sharding import PartitionSpec as P

D = 768
HEADS = 12
HD = 64
SEQ = 1024
QBB = 1024
PAIR = 2 * HD
PAIRS = HEADS // 2
EPS = 1e-06
MASKED = -1e30
F32 = jnp.float32
BF16 = jnp.bfloat16
VMEM_LIMIT = 60 * 1024 * 1024
PI_2 = (1.5703125, 4.837512969970703125e-4, 7.549789948768648e-8)

NN = (((1,), (0,)), ((), ()))
NT = (((1,), (1,)), ((), ()))


def mm(a, b, dims=NN):
    return lax.dot_general(a, b, dims, preferred_element_type=F32)


def whole(shape):
    return pl.BlockSpec(shape, lambda *_: (0,) * len(shape), pipeline_mode=pl.Buffered(1))


def params(**kw):
    return pltpu.CompilerParams(vmem_limit_bytes=VMEM_LIMIT, **kw)


def lane_sums(x):
    total = x[:, 0:128]
    for j in range(1, x.shape[1] // 128):
        total = total + x[:, j * 128 : (j + 1) * 128]
    return total


def norm_stats(e):
    average = jnp.sum(e, axis=0, keepdims=True) * (1.0 / D)
    spread = jnp.sum(e * e, axis=0, keepdims=True) * (1.0 / D) - average * average
    return average, lax.rsqrt(spread + EPS)


def fill_bias(bias_ref, seg_ref, present_ref):
    seg = seg_ref[...].astype(F32)
    key = jnp.where(present_ref[...] == 1, seg, -1.0)
    key_cols = jnp.broadcast_to(key, (8, SEQ)).T
    for i in range(SEQ // 256):
        same = key_cols[i * 256 : (i + 1) * 256, 0:1] == seg
        row_id = lax.broadcasted_iota(jnp.int32, (256, SEQ), 0) + i * 256
        col_id = lax.broadcasted_iota(jnp.int32, (256, SEQ), 1)
        bias_ref[i * 256 : (i + 1) * 256, :] = jnp.where(same | (row_id == col_id), 0.0, MASKED)


MESH = pl.DeviceIdType.MESH


class Wire:
    def __init__(self, send, recv):
        self.send_sem, self.recv_sem, self.count, self.sent = send, recv, 0, []
        self.me = (lax.axis_index("dp"), lax.axis_index("mp"), lax.axis_index("hidden"))
        self.size = (lax.axis_size("dp"), lax.axis_size("mp"), lax.axis_size("hidden"))

    def peer(self, axis, offset):
        where = list(self.me)
        where[axis] = lax.rem(where[axis] + offset, self.size[axis])
        return tuple(where)

    def origin(self, axis, offset):
        return lax.rem(self.me[axis] - offset + self.size[axis], self.size[axis])

    def meet(self):
        barrier = pltpu.get_barrier_semaphore()
        total = 0
        for axis in range(3):
            for offset in range(1, self.size[axis]):
                pl.semaphore_signal(barrier, 1, device_id=self.peer(axis, offset), device_id_type=MESH)
                total += 1
        pl.semaphore_wait(barrier, total)

    def send(self, src, dst, target):
        copy = pltpu.make_async_remote_copy(
            src, dst, self.send_sem.at[self.count], self.recv_sem.at[self.count], device_id=target, device_id_type=MESH
        )
        copy.start()
        self.count += 1
        self.sent.append(copy)
        return copy

    def keep(self, src, dst):
        copy = pltpu.make_async_copy(src, dst, self.send_sem.at[self.count])
        copy.start()
        self.count += 1
        return copy

    def finish(self):
        assert self.count <= self.send_sem.shape[0], self.count
        for copy in self.sent:
            copy.wait_send()


DP, MP, HID = 0, 1, 2


HALF = D // 2


def sin_cos(angles):
    turns = jnp.floor(angles * (2.0 / math.pi) + 0.5)
    r = ((angles - turns * PI_2[0]) - turns * PI_2[1]) - turns * PI_2[2]
    r2 = r * r
    s = r + r * r2 * (-1.6666654611e-1 + r2 * (8.3321608736e-3 + r2 * -1.9515295891e-4))
    c = 1.0 - 0.5 * r2 + r2 * r2 * (4.166664568298827e-2 + r2 * (-1.388731625493765e-3 + r2 * 2.443315711809948e-5))
    quarter = turns - 4.0 * jnp.floor(turns * 0.25)
    odd = (quarter == 1.0) | (quarter == 3.0)
    flip_s = quarter >= 2.0
    flip_c = (quarter == 1.0) | (quarter == 2.0)
    sine = jnp.where(odd, c, s)
    cosine = jnp.where(odd, s, c)
    return jnp.where(flip_s, -sine, sine), jnp.where(flip_c, -cosine, cosine)


def forward_kernel(
    x_ref, c_ref, w1a_ref, w1b_ref, w2_ref, we_ref, wr_ref, cols_ref, rows_ref, pos_ref, rate_ref, seg_ref, present_ref,
    et_out, ft_out, w1_out, qkv_out, out_out, dmid_out, do_out, near_r, near_e, last_sum, wef_ref, wrf_ref,
    lse_ref, p_ref, dbe_ref, dw2_ref, dbf_ref, dgs_ref,
    xt, ct, w1af, w1bf, w2f, rowsf, colsf, rates, tab, et, ft, f, w1, qkv, bias, vt, wb, at, out, wblk, dblk, w2c, theirs, sums,
    send, recv, z_send, z_recv, p_send, p_recv, c_send, c_recv, x_send, x_recv, n_send, n_recv, o_sem, local,
):
    wire = Wire(send, recv)
    d, m, h = wire.me
    dp, mp, hid = wire.size
    rows = D // mp
    wide = D // hid
    fcols = we_ref.shape[1]
    half = rows // dp
    offset = pl.multiple_of(d * half, half)
    half2 = wide // dp
    w2_part = w2_ref
    if w2_ref.shape[0] > half2:
        w2_part = w2_ref.at[pl.ds(pl.multiple_of(d * half2, half2), half2)]
    own = (
        (w1a_ref, lambda mm_, hh: w1af.at[hh, mm_, d], lambda: w1af.at[:, :, d], HID),
        (w1b_ref, lambda mm_, hh: w1bf.at[hh, mm_, d], lambda: w1bf.at[:, :, d], MP),
        (w2_part, lambda mm_, hh: w2f.at[mm_, hh, d], lambda: w2f.at[:, :, d], HID),
    )
    wire.meet()
    waits, stored = [], []
    first, second, third = {}, {}, {}

    def swap(src_ref, dst_ref):
        mine = pl.ds(pl.multiple_of(m * rows, rows), rows)
        moved = []
        for q in range(1, mp):
            to = wire.peer(MP, q)
            moved.append(wire.send(src_ref.at[:, pl.ds(pl.multiple_of(to[1] * SEQ, SEQ), SEQ)], dst_ref.at[mine], to))
        return moved, wire.keep(src_ref.at[:, pl.ds(pl.multiple_of(m * SEQ, SEQ), SEQ)], dst_ref.at[mine])

    def landed(pair):
        for copy in pair[0]:
            copy.wait_recv()
        pair[1].wait()

    def stage_one(i):
        src, dst, _, axis = own[i]
        first[i] = [wire.keep(src, dst(m, h))]
        first[i] += [wire.send(src, dst(m, h), wire.peer(axis, o)) for o in range(1, wire.size[axis])]

    def stage_two(i):
        _, dst, _, axis = own[i]
        other = MP if axis == HID else HID
        second[i] = []
        for o, copy in enumerate(first[i]):
            if o == 0:
                copy.wait()
            else:
                copy.wait_recv()
            at_ = wire.origin(axis, o)
            piece = dst(m, at_) if axis == HID else dst(at_, h)
            second[i] += [wire.send(piece, piece, wire.peer(other, q)) for q in range(1, wire.size[other])]

    def stage_three(i):
        for copy in second[i]:
            copy.wait_recv()
        third[i] = [wire.send(own[i][2](), own[i][2](), wire.peer(DP, r)) for r in range(1, dp)]

    def done(i):
        for copy in third[i]:
            copy.wait_recv()

    full = (wef_ref, wrf_ref)
    cut = tuple(ref.reshape(mp, dp, half, hid * fcols) for ref in full)
    part = (we_ref.at[pl.ds(offset, half)], wr_ref.at[pl.ds(offset, half)])
    whole_planes = ((1,), (1, hid - 1))
    order = [0, 1, hid - 1] + list(range(2, hid - 1))

    def plane_of(o):
        return lax.rem(h - o + hid, hid)

    def piece(j, mm_, dd, o):
        at_ = pl.ds(pl.multiple_of(mm_ * rows + dd * half, half), half)
        return full[j].at[at_, pl.ds(pl.multiple_of(plane_of(o) * fcols, fcols), fcols)]

    def remote(src, dst, sems, target):
        return pltpu.make_async_remote_copy(src, dst, sems[0], sems[1], device_id=target, device_id_type=MESH)

    def to_plane(j, o, q):
        src = part[j] if o == 0 else piece(j, m, d, o)
        return remote(src, piece(j, m, d, o), (p_send.at[j, o, q], p_recv.at[j, o, q]), wire.peer(MP, q))

    def slab(j, o):
        return cut[j].at[:, d, :, pl.ds(pl.multiple_of(plane_of(o) * fcols, fcols), fcols)]

    def to_depth(j, o):
        if o in whole_planes[j]:
            src = dst = slab(j, 0)
        else:
            src, dst = part[j], piece(j, m, d, 0)
        return remote(src, dst, (z_send.at[j, o], z_recv.at[j, o]), wire.peer(HID, o))

    def to_core(j, o, r):
        return remote(slab(j, o), slab(j, o), (c_send.at[j, o, r - 1], c_recv.at[j, o, r - 1]), wire.peer(DP, r))

    def keep_own(j):
        return pltpu.make_async_copy(part[j], piece(j, m, d, 0), local.at[j])

    def plane_start(j, o):
        if o:
            to_depth(j, o).wait_recv()
        else:
            keep_own(j).start()
        for q in range(1, mp):
            to_plane(j, o, q).start()

    def plane_wait(j, o):
        if o == 0:
            keep_own(j).wait()
        for q in range(1, mp):
            to_plane(j, o, q).wait_recv()

    def depth_start(j, o):
        to_depth(j, o).start()

    def apart(j):
        return [o for o in range(1, hid) if o not in whole_planes[j]]

    def core_start(j, o):
        if o in whole_planes[j]:
            to_depth(j, o).wait_recv()
        elif o:
            plane_wait(j, o)
        for r in range(1, dp):
            to_core(j, o, r).start()

    def arrived(j, o):
        for r in range(1, dp):
            to_core(j, o, r).wait_recv()

    small = [wire.send(cols_ref, colsf.at[m], wire.peer(MP, q)) for q in range(1, mp)]
    small += [wire.send(rows_ref, rowsf.at[h], wire.peer(HID, o)) for o in range(1, hid)]
    kept = [wire.keep(cols_ref, colsf.at[m]), wire.keep(rows_ref, rowsf.at[h])]
    stage_one(0)
    stage_one(1)
    x_in = swap(x_ref, xt)

    rates[...] = jnp.broadcast_to(rate_ref[...], (8, HALF)).T
    places = pos_ref[:, pl.ds(pl.multiple_of(m * SEQ, SEQ), SEQ)].astype(F32)

    def table_rows(j, _):
        at_ = pl.ds(pl.multiple_of(j * 64, 64), 64)
        sine, cosine = sin_cos(rates[at_, 0:1] * places)
        tab[at_, :] = sine
        tab[pl.ds(pl.multiple_of(j * 64 + HALF, 64), 64), :] = cosine
        return 0

    lax.fori_loop(0, 1, table_rows, 0)
    stage_two(0)
    stage_two(1)
    lax.fori_loop(1, HALF // 64, table_rows, 0)
    fill_bias(bias, seg_ref, present_ref)
    for copy in small:
        copy.wait_recv()
    for copy in kept:
        copy.wait()
    for mm_ in range(mp):
        p_ref[mm_ * rows : (mm_ + 1) * rows, 0:8] = colsf[mm_].T[:rows, :]
    wb[...] = jnp.zeros_like(wb)
    for hh in range(hid):
        wb[:, hh * wide : (hh + 1) * wide] = rowsf[hh, 1:2, :wide]
        wb[:, 2 * D + hh * wide : 2 * D + (hh + 1) * wide] = rowsf[hh, 2:3, :wide]
    landed(x_in)
    plane_start(1, 0)
    for j in (1, 0):
        for o in apart(j):
            depth_start(j, o)
    stage_one(2)

    def norm_cols(j, _):
        cols = pl.ds(pl.multiple_of(j * 256, 256), 256)
        e = xt[:, cols].astype(F32) + tab[:, cols]
        et[:, cols] = e
        average, inv = norm_stats(e)
        low = ((e - average) * inv * p_ref[:, 0:1] + p_ref[:, 1:2]).astype(BF16)
        ft[:, cols] = low
        f[cols, :] = low.T
        return 0

    lax.fori_loop(0, SEQ // 256, norm_cols, 0)
    stored += [wire.keep(et, et_out), wire.keep(ft, ft_out)]
    stage_three(0)
    stage_three(1)
    plane_start(0, 0)
    c_in = swap(c_ref, ct)
    def unpack(dd):
        for hh in range(hid):
            for mm_ in range(mp):
                at_ = slice(mm_ * rows + dd * half, mm_ * rows + (dd + 1) * half)
                for k in range(3):
                    if k < 2:
                        value = w1af[hh, mm_, dd, :, k * wide : (k + 1) * wide]
                    else:
                        value = w1bf[hh, mm_, dd]
                    w1[at_, k * D + hh * wide : k * D + (hh + 1) * wide] = value

    if dp == 2:
        for dd in range(dp):

            @pl.when(d == dd)
            def _():
                unpack(dd)

        done(0)
        done(1)
        for dd in range(dp):

            @pl.when(d == 1 - dd)
            def _():
                unpack(dd)

    else:
        done(0)
        done(1)
        for dd in range(dp):
            unpack(dd)
    stored.append(wire.keep(w1, w1_out))

    def cols_of(n, scale):
        cols = pl.ds(pl.multiple_of(n * 256, 256), 256)
        y = (mm(f[...], w1[:, cols]) + wb[:, cols]).astype(BF16)
        qkv[:, cols] = y * jnp.asarray(scale, BF16)
        return 0

    lax.fori_loop(0, D // 256, lambda n, c: cols_of(n, HD**-0.5), 0)
    stage_two(2)
    plane_wait(1, 0)
    for o in whole_planes[1]:
        depth_start(1, o)
    lax.fori_loop(D // 256, 3 * D // 256, lambda n, c: cols_of(n, 1.0), 0)
    stored.append(wire.keep(qkv, qkv_out))

    low = lax.broadcasted_iota(jnp.int32, (SEQ, PAIR), 1) < HD
    lse_ref[...] = jnp.zeros_like(lse_ref)

    def pair_of(p, _):
        lanes = pl.ds(pl.multiple_of(p * PAIR, PAIR), PAIR)
        k_lanes = pl.ds(pl.multiple_of(p * PAIR + D, PAIR), PAIR)
        v_lanes = pl.ds(pl.multiple_of(p * PAIR + 2 * D, PAIR), PAIR)
        vt[...] = qkv[:, v_lanes].T
        q = qkv[:, lanes]
        for hh in range(2):
            qm = jnp.where(low if hh == 0 else ~low, q, jnp.zeros_like(q))
            s = mm(qkv[:, k_lanes], qm, NT) + bias[...]
            top = jnp.max(s, axis=0, keepdims=True)
            e = jnp.exp(s - top)
            total = jnp.sum(e, axis=0, keepdims=True)
            o = mm(vt[hh * HD : (hh + 1) * HD, :], e.astype(BF16)) / total
            at[pl.ds(pl.multiple_of(p * PAIR + hh * HD, HD), HD), :] = o.astype(BF16)
            lse_ref[p, hh : hh + 1, :] = top + jnp.log(total)
        return 0

    lax.fori_loop(0, PAIRS // 3, pair_of, 0)
    plane_wait(0, 0)
    for o in whole_planes[0]:
        depth_start(0, o)
    for j in (1, 0):
        for o in apart(j):
            plane_start(j, o)
    lax.fori_loop(PAIRS // 3, 2 * PAIRS // 3, pair_of, 0)
    stage_three(2)
    for j in range(2):
        core_start(j, 0)
    lax.fori_loop(2 * PAIRS // 3, PAIRS, pair_of, 0)
    for copy in stored:
        copy.wait()
    landed(c_in)
    done(2)

    ot, ds_sum, st, bt, mid = bias.at[pl.ds(0, D)], tab, xt, ft, et
    tokens = [pl.ds(n * D, D) for n in range(3)]
    for mm_ in range(mp):
        for hh in range(hid):
            for dd in range(dp):
                at_ = hh * wide + dd * (wide // dp)
                w2c[at_ : at_ + wide // dp, mm_ * rows : (mm_ + 1) * rows] = w2f[mm_, hh, dd]
    w2t = w2c[...].T

    def middle_cols(j, _):
        cols = pl.ds(pl.multiple_of(j * 256, 256), 256)
        value = et[:, cols] + (mm(w2t, at[:, cols]) + p_ref[:, 4:5])
        mid[:, cols] = value
        ot[:, cols] = value + p_ref[:, 5:6]
        average, inv = norm_stats(value)
        s = ((value - average) * inv * p_ref[:, 2:3] + p_ref[:, 3:4]).astype(BF16)
        st[:, cols] = s
        qkv[cols, tokens[0]] = s.T
        qkv[cols, tokens[1]] = ct[:, cols].T
        return 0

    lax.fori_loop(0, SEQ // 256, middle_cols, 0)
    ds_sum[...] = jnp.zeros_like(ds_sum)

    def fetch(j, o):
        hcols = pl.ds(pl.multiple_of(plane_of(o) * fcols, fcols), fcols)
        return pltpu.make_async_copy(full[j].at[:, hcols], wblk.at[j], local.at[2 + j])

    def place(n):
        o = 0
        for k in range(1, hid):
            o = jnp.where(n == k, order[k], o)
        return o

    def swap_core(j, n, r):
        to = wire.peer(DP, r)
        return remote(
            dblk.at[j, :, to[0]], theirs.at[lax.rem(n, 2), j, r - 1], (x_send.at[j, n, r - 1], x_recv.at[j, n, r - 1]), to
        )

    def each_core(n, do):
        for j in range(2):
            for r in range(1, dp):
                do(swap_core(j, n, r))

    end = hid - 1

    def sum_depth(n):
        to = (d, m, plane_of(place(n)))
        return remote(sums.at[lax.rem(n, 2), 0], near_r.at[n], (n_send.at[n, 0], n_recv.at[n, 0]), to)

    def sum_plane(n, q):
        to = wire.peer(MP, q)
        return remote(sums.at[lax.rem(n, 2), 1, to[1]], near_e.at[n, q], (n_send.at[n, q], n_recv.at[n, q]), to)

    def save(j, n, last):
        slot = lax.rem(n, 2)
        if last:
            return pltpu.make_async_copy(sums.at[slot, j], last_sum.at[j], o_sem.at[j, n])
        if j == 0:
            return pltpu.make_async_copy(sums.at[0, 0], near_r.at[0], o_sem.at[0, 0])
        return pltpu.make_async_copy(sums.at[slot, 1, m], near_e.at[n, 0], o_sem.at[1, n])

    def add_cores(n, last=False):
        each_core(n, lambda copy: copy.wait_recv())
        slot = lax.rem(n, 2)
        for j in range(2):
            for k in range(mp):
                value = dblk[j, k, d].astype(F32)
                for r in range(1, dp):
                    value = value + theirs[slot, j, r - 1, k].astype(F32)
                sums[slot, j, k] = value.astype(BF16)
        if last:
            for j in range(2):
                save(j, n, True).start()
            return
        for q in range(1, mp):
            sum_plane(n, q).start()
        save(1, n, False).start()

    def gone(n):
        for q in range(1, mp):
            sum_plane(n, q).wait_send()
        save(1, n, False).wait()

    def block(n, _):
        o = place(n)
        hh = plane_of(o)
        for j in range(2):
            arrived(j, o)
        for j in range(2):
            fetch(j, o).start()
        for j in range(2):
            fetch(j, o).wait()

        pre = mm(qkv[:, tokens[0]], wblk[0]) + rowsf[hh, 0:1, :]
        cdf = 0.5 * (1.0 + lax.erf(pre * (1.0 / math.sqrt(2.0))))
        act = (pre * cdf).astype(BF16)
        slope = cdf + pre * jnp.exp(-0.5 * pre * pre) * (1.0 / math.sqrt(2.0 * math.pi))
        grad = (mm(qkv[:, tokens[1]], wblk[1]) * slope).astype(BF16)

        @pl.when(n == 3)
        def _():
            gone(0)
            save(0, 0, False).wait()

        @pl.when(n > 3)
        def _():
            gone(n - 3)
            sum_depth(n - 3).wait_send()

        @pl.when(n > 0)
        def _():
            add_cores(n - 1)
            each_core(n - 1, lambda copy: copy.wait_send())

        @pl.when(n == 1)
        def _():
            save(0, 0, False).start()

        @pl.when(n > 1)
        def _():
            sum_depth(n - 1).start()

        for j, value in enumerate((mm(ct[...], act), mm(st[...], grad))):
            for k in range(mp):
                for dd in range(dp):
                    at_ = k * rows + dd * half
                    dblk[j, k, dd] = value[at_ : at_ + half, :].astype(BF16)
        each_core(n, lambda copy: copy.start())
        dbe_ref[hh, 0:1, :] = jnp.sum(grad.astype(F32), axis=0, keepdims=True)
        ot[...] += mm(wblk[1], act, NT)
        ds_sum[...] += mm(wblk[0], grad, NT)

        for k in range(1, hid):

            @pl.when(n + 1 == k)
            def _():
                for j in range(2):
                    core_start(j, order[k])

        return 0

    lax.fori_loop(0, hid, block, 0)
    gone(end - 2)
    sum_depth(end - 2).wait_send()
    add_cores(end, True)
    dgs_ref[...] = jnp.zeros_like(dgs_ref)

    def back_cols(j, _):
        cols = pl.ds(pl.multiple_of(j * 256, 256), 256)
        value = mid[:, cols]
        out[:, cols] = ot[:, cols].astype(BF16)
        average, inv = norm_stats(value)
        normed = (value - average) * inv
        ds = ds_sum[:, cols]
        scaled = ds * p_ref[:, 2:3]
        total = jnp.sum(scaled, axis=0, keepdims=True) * (1.0 / D)
        crossed = jnp.sum(scaled * normed, axis=0, keepdims=True) * (1.0 / D)
        dmid = ct[:, cols].astype(F32) + inv * (scaled - total - normed * crossed)
        mid[:, cols] = dmid
        low_ = dmid.astype(BF16)
        bt[:, cols] = low_
        qkv[cols, tokens[2]] = mm(w2c[...], low_).astype(BF16).T
        dgs_ref[0] += lane_sums(ds * normed)
        dgs_ref[1] += lane_sums(ds)
        return 0

    lax.fori_loop(0, SEQ // 256, back_cols, 0)
    last = [wire.keep(out, out_out), wire.keep(mid, dmid_out), wire.keep(qkv.at[:, tokens[2]], do_out)]
    ones = jnp.ones((8, SEQ), BF16)
    dbf_ref[0] = mm(ones, ct[...], NT)
    dbf_ref[1] = mm(ones, bt[...], NT)
    for j in range(mp):
        dw2_ref[j] = mm(at[...], bt[j * rows : (j + 1) * rows, :], NT).astype(BF16)
    each_core(end, lambda copy: copy.wait_send())
    gone(end - 1)
    sum_depth(end - 1).wait_send()
    for j in range(2):
        save(j, end, True).wait()
    for n in range(end):
        if n:
            sum_depth(n).wait_recv()
        for q in range(1, mp):
            sum_plane(n, q).wait_recv()
    for copy in last:
        copy.wait()
    wire.finish()
    for j in range(2):
        for o in range(hid):
            if o:
                to_depth(j, o).wait_send()
            if o not in whole_planes[j]:
                for q in range(1, mp):
                    to_plane(j, o, q).wait_send()
            for r in range(1, dp):
                to_core(j, o, r).wait_send()


def forward(x, c, w1a, w1b, w2, we, wr, cols, rows, pos, rate, seg, present):
    dp, mp, hid = lax.axis_size("dp"), lax.axis_size("mp"), lax.axis_size("hidden")
    half = D // mp // dp
    fc = we.shape[1]
    ff = hid * fc
    sds = jax.ShapeDtypeStruct
    out_shape = (
        sds((D, SEQ), F32), sds((D, SEQ), BF16), sds((D, 3 * D), BF16), sds((SEQ, 3 * D), BF16),
        sds((D, SEQ), BF16), sds((D, SEQ), F32), sds((SEQ, D), BF16), sds((hid - 1, mp, half, fc), BF16),
        sds((hid - 1, mp, half, fc), BF16), sds((2, mp, half, fc), BF16), sds((D, ff), BF16), sds((D, ff), BF16),
        sds((PAIRS, 8, SEQ), F32), sds((D, 128), F32), sds((hid, 8, fc), F32), sds((mp, D, D // mp), BF16),
        sds((2, 8, D), F32), sds((2, D, 128), F32),
    )
    n = (mp - 1) + (hid - 1) + 2 + 2 * hid + mp + 2 * hid * (mp - 1) + mp * (hid - 1) + 3 * (dp - 1) + 2 * mp + 7
    hbm = pl.BlockSpec(memory_space=pl.ANY)
    vmem = pl.BlockSpec(memory_space=pltpu.VMEM)
    vm = lambda dtype, *shape: pltpu.VMEM(shape, dtype)
    sem = lambda *shape: pltpu.SemaphoreType.DMA(shape)
    return pl.pallas_call(
        forward_kernel,
        out_shape=out_shape,
        in_specs=[hbm] * 9 + [vmem] * 4,
        out_specs=(hbm,) * 12 + (vmem,) * 6,
        scratch_shapes=[
            vm(BF16, D, SEQ), vm(BF16, D, SEQ), vm(BF16, hid, mp, dp, half, w1a.shape[1]),
            vm(BF16, hid, mp, dp, half, w1b.shape[1]), vm(BF16, mp, hid, dp, D // hid // dp, w2.shape[1]), vm(F32, hid, *rows.shape),
            vm(F32, mp, *cols.shape), vm(F32, HALF, 8),
            vm(F32, D, SEQ), vm(F32, D, SEQ), vm(BF16, D, SEQ), vm(BF16, SEQ, D), vm(BF16, D, 3 * D),
            vm(BF16, SEQ, 3 * D), vm(F32, SEQ, SEQ), vm(BF16, PAIR, SEQ), vm(F32, 1, 3 * D),
            vm(BF16, D, SEQ), vm(BF16, D, SEQ), vm(BF16, 2, D, fc), vm(BF16, 2, mp, dp, half, fc), vm(BF16, D, D),
            vm(BF16, 2, 2, dp - 1, mp, half, fc), vm(BF16, 2, 2, mp, half, fc),
            sem(n), sem(n), sem(2, hid), sem(2, hid), sem(2, hid, mp), sem(2, hid, mp),
            sem(2, hid, dp - 1), sem(2, hid, dp - 1), sem(2, hid, dp - 1), sem(2, hid, dp - 1),
            sem(hid, mp), sem(hid, mp), sem(2, hid), sem(4),
        ],
        compiler_params=params(collective_id=0, has_side_effects=True),
        name="forward",
    )(x, c, w1a, w1b, w2, we, wr, cols, rows, pos, rate, seg, present)


def backward_kernel(
    o_ref, dw2_ref, near_r, near_e, last_sum, qkv_in, do_in, lse_ref, seg_ref, present_ref, ft_in, w_in, et_in, dmid_in, p_ref,
    dbe_ref, dbf_ref, dgs_ref,
    of_ref, xf_ref, g1_ref, g2_ref, ge_ref, gr_ref, vecf_ref,
    qkv, do, bias, kt, dqt, dk, dv, dka, dva, ft, et, dmid, dgp,
    a0, a1, a2, o0, o1, s2, b0, b1, b2, be, br, t0, t1, t2, t3, t4, c0, c1, c2, c3, c4,
    v0, va, vb, vc, v1, v2, loads, send, recv,
):
    wire = Wire(send, recv)
    d, m, h = wire.me
    dp, mp, hid = wire.size
    rows = D // mp
    wide = D // hid
    half = rows // dp
    fcols = ge_ref.shape[1]
    v_in = (va, vb, vc)
    slab0 = o0.shape[1:]
    hslice = lambda hh: pl.ds(pl.multiple_of(hh * fcols, fcols), fcols)

    def load(n, src, dst):
        copy = pltpu.make_async_copy(src, dst, loads.at[n])
        copy.start()
        return copy

    parts = []
    for p in range(PAIRS):
        got = []
        for k in range(3):
            lanes = slice(k * D + p * PAIR, k * D + (p + 1) * PAIR)
            got.append(load(4 * p + k, qkv_in.at[:, lanes], qkv.at[:, lanes]))
        lanes = slice(p * PAIR, (p + 1) * PAIR)
        got.append(load(4 * p + 3, do_in.at[:, lanes], do.at[:, lanes]))
        parts.append(got)
    others = [load(4 * PAIRS + i, a, b) for i, (a, b) in enumerate(((ft_in, ft), (et_in, et), (dmid_in, dmid)))]
    wire.meet()
    items = (
        (lambda dd: o0.at[dd], a0, o0.at[d], b0, t0, c0, None, MP, HID),
        (lambda dd: o1.at[dd], a1, o1.at[d], b1, t1, c1, None, HID, HID),
        (lambda dd: dw2_ref.at[:, :, dd], a2, s2, b2, t2, c2, g2_ref, MP, MP),
        (None, None, None, be, t3, c3, ge_ref, MP, None),
        (None, None, None, br, t4, c4, gr_ref, HID, None),
    )
    core, kept, near, far = {}, {}, {}, {}
    end = hid - 1
    plane = lambda o: lax.rem(h - o + hid, hid)
    order = [0, 1, hid - 1] + list(range(2, hid - 1))
    at = 4 * PAIRS + 4
    own = {
        4: [load(at, near_r, br.at[pl.ds(0, end)])],
        3: [load(at + 1 + n, near_e.at[n], be.at[:, :, hslice(plane(order[n]))]) for n in range(end)],
    }
    own[3].append(load(at + 1 + end, last_sum.at[1, m], be.at[0, :, hslice(plane(order[end]))]))

    def stage_core(i):
        src, a, s = items[i][:3]
        core[i] = [wire.send(src(wire.peer(DP, r)[0]), a.at[r - 1], wire.peer(DP, r)) for r in range(1, dp)]
        if i > 1:
            kept[i] = wire.keep(src(d), s)

    def add_all(dst, own, others, shape):
        lead = shape[:-2]

        def body(n, _):
            index = []
            for size in reversed(lead):
                index.insert(0, lax.rem(n, size))
                n = lax.div(n, size)
            index = tuple(index)
            value = own[index].astype(F32)
            for j in range(others.shape[0]):
                value = value + others[(j,) + index].astype(F32)
            dst[index] = value.astype(dst.dtype)
            return 0

        lax.fori_loop(0, math.prod(lead), body, 0)

    def part(i, ref, axis, at, leads):
        if items[i][8] is None:
            return ref.at[(slice(None),) * len(leads) + (slice(None), hslice(at))] if axis == HID else ref.at[at]
        return ref.at[at] if leads[0] == axis else ref.at[:, at]

    def leads_of(i):
        lead = items[i][8]
        return (MP,) if lead is None else ((HID, MP) if lead == HID else (MP, HID))

    def stage_near(i):
        if i == 4:
            near[4] = [wire.send(last_sum.at[0], br.at[end], wire.peer(HID, hid - order[end]))]
            return
        if i == 3:
            here = hslice(plane(order[end]))
            near[3] = []
            for q in range(1, mp):
                to = wire.peer(MP, q)
                near[3].append(wire.send(last_sum.at[1, to[1]], be.at[q, :, here], to))
            return
        _, a, s, b, t, c, g, axis, _ = items[i]
        for copy in core[i]:
            copy.wait_recv()
        if i in kept:
            kept[i].wait()
        add_all(s, s, a, s.shape)
        near[i] = [
            wire.send(part(i, s, axis, wire.peer(axis, q)[axis], leads_of(i)), b.at[q - 1], wire.peer(axis, q))
            for q in range(1, wire.size[axis])
        ]

    def stage_far(i):
        _, a, s, b, t, c, g, axis, lead = items[i]
        if i < 3:
            for copy in near[i] if i else nears_half[0] + nears_half[1]:
                copy.wait_recv()
            add_all(t, part(i, s, axis, wire.me[axis], leads_of(i)), b, t.shape)
        else:
            for copy in near[i]:
                copy.wait_recv()
            for copy in own[i]:
                copy.wait()
            add_all(t, b.at[0], b.at[pl.ds(1, b.shape[0] - 1)], t.shape)
        other = MP if axis == HID else HID
        left = tuple(x for x in leads_of(i) if x != axis)
        far[i] = []
        for q in range(1, wire.size[other]):
            to = wire.peer(other, q)
            far[i].append(wire.send(part(i, t, other, to[other], left), c.at[q - 1], to))

    def stage_end(i):
        _, a, s, b, t, c, g, axis, lead = items[i]
        other = MP if axis == HID else HID
        left = tuple(x for x in leads_of(i) if x != axis)
        for copy in far[i]:
            copy.wait_recv()
        value = part(i, t, other, wire.me[other], left)[...].astype(F32)
        for j in range(c.shape[0]):
            value = value + c[j].astype(F32)
        if i == 0:
            g1_ref[0] = value[:, :wide]
            g1_ref[1] = value[:, wide:]
        elif i == 1:
            g1_ref[2] = value
        else:
            g[...] = value

    moved, held = [], []

    def swap(src_ref, dst_ref):
        mine = pl.ds(pl.multiple_of(m * SEQ, SEQ), SEQ)
        for q in range(1, mp):
            to = wire.peer(MP, q)
            moved.append(wire.send(src_ref.at[pl.ds(pl.multiple_of(to[1] * rows, rows), rows)], dst_ref.at[:, mine], to))
        held.append(wire.keep(src_ref.at[pl.ds(pl.multiple_of(m * rows, rows), rows)], dst_ref.at[:, mine]))

    vec = {}

    def vec_send(axis, src):
        vec[axis] = [wire.send(src, v_in[axis].at[o - 1], wire.peer(axis, o)) for o in range(1, wire.size[axis])]

    def vec_sum(axis, src, dst):
        for copy in vec[axis]:
            copy.wait_recv()
        total = src[...]
        for j in range(wire.size[axis] - 1):
            total = total + v_in[axis][j]
        dst[...] = total

    stage_near(4)
    stage_near(3)
    stage_core(2)
    swap(o_ref, of_ref)
    fill_bias(bias, seg_ref, present_ref)
    low = lax.broadcasted_iota(jnp.int32, (QBB, PAIR), 1) < HD

    def pair_of(p, _):
        off = pl.multiple_of(p * PAIR, PAIR)
        lanes = pl.ds(off, PAIR)
        k_lanes = pl.ds(pl.multiple_of(off + D, PAIR), PAIR)
        v_lanes = pl.ds(pl.multiple_of(off + 2 * D, PAIR), PAIR)
        kt[...] = qkv[:, k_lanes].T
        dka[...] = jnp.zeros_like(dka)
        dva[...] = jnp.zeros_like(dva)

        def block(j, _):
            cols = pl.ds(pl.multiple_of(j * QBB, QBB), QBB)
            q = qkv[cols, lanes]
            g = do[cols, lanes]
            for hh in range(2):
                keep = low if hh == 0 else ~low
                qm = jnp.where(keep, q, jnp.zeros_like(q))
                gm = jnp.where(keep, g, jnp.zeros_like(g))
                e = jnp.exp(mm(qkv[:, k_lanes], qm, NT) + bias[:, cols] - lse_ref[p, hh : hh + 1, cols])
                t = e * mm(qkv[:, v_lanes], gm, NT)
                ds = (t - e * jnp.sum(t, axis=0, keepdims=True)).astype(BF16)
                dva[...] += mm(e.astype(BF16), gm)
                dka[...] += mm(ds, qm)
                dq = mm(kt[hh * HD : (hh + 1) * HD, :], ds) * HD**-0.5
                dqt[pl.ds(pl.multiple_of(off + hh * HD, HD), HD), cols] = dq.astype(BF16)
            return 0

        lax.fori_loop(0, SEQ // QBB, block, 0)
        dk[:, lanes] = dka[...].astype(BF16)
        dv[:, lanes] = dva[...].astype(BF16)
        return 0

    def pairs(first, last):
        for p in range(first, last):
            for copy in parts[p]:
                copy.wait()
        lax.fori_loop(first, last, pair_of, 0)

    span = D // 2
    each = hid // 2

    def weight_half(g):
        wide_k = mm(ft[...], dk[:, g * span : (g + 1) * span]).astype(BF16)
        wide_v = mm(ft[...], dv[:, g * span : (g + 1) * span]).astype(BF16)
        for hh in range(g * each, (g + 1) * each):
            lanes = slice((hh - g * each) * wide, (hh - g * each + 1) * wide)
            value_q = mm(ft[...], dqt[hh * wide : (hh + 1) * wide, :], NT).astype(BF16)
            for mm_ in range(mp):
                for dd in range(dp):
                    at_ = slice(mm_ * rows + dd * half, mm_ * rows + (dd + 1) * half)
                    o0[dd, hh, mm_, :, 0:wide] = value_q[at_, :]
                    o0[dd, hh, mm_, :, wide : 2 * wide] = wide_k[at_, lanes]
                    o1[dd, hh, mm_] = wide_v[at_, lanes]

    cores_half, nears_half = {}, {}

    def core_half(g):
        hs = pl.ds(g * each, each)
        cores_half[g] = [
            wire.send(o0.at[wire.peer(DP, r)[0], hs], a0.at[r - 1, hs], wire.peer(DP, r)) for r in range(1, dp)
        ]

    def near_half(g):
        hs = pl.ds(g * each, each)
        for copy in cores_half[g]:
            copy.wait_recv()
        add_all(o0.at[d, hs], o0.at[d, hs], a0.at[:, hs], (each,) + slab0[1:])
        nears_half[g] = []
        for q in range(1, mp):
            to = wire.peer(MP, q)
            nears_half[g].append(wire.send(o0.at[d, hs, to[1]], b0.at[q - 1, hs], to))

    pairs(0, PAIRS // 2)
    stage_near(2)
    for copy in others:
        copy.wait()
    weight_half(0)
    core_half(0)
    pairs(PAIRS // 2, PAIRS // 2 + 1)
    near_half(0)
    pairs(PAIRS // 2 + 1, PAIRS)
    w1 = qkv.at[pl.ds(0, D)]
    w_load = load(4 * PAIRS + 3, w_in, w1)
    weight_half(1)
    stage_core(1)
    core_half(1)
    df = bias.at[pl.ds(0, D)]
    w_load.wait()
    dx = ft

    def feature_cols(j, _):
        cols = pl.ds(pl.multiple_of(j * 256, 256), 256)
        value = mm(w1[:, 0:D], dqt[:, cols])
        value += mm(w1[:, D : 2 * D], dk[cols, :], NT)
        value += mm(w1[:, 2 * D : 3 * D], dv[cols, :], NT)
        df[:, cols] = value
        return 0

    lax.fori_loop(0, SEQ // 256, feature_cols, 0)
    stage_near(1)
    near_half(1)
    dgp[...] = jnp.zeros_like(dgp)

    def norm_cols(j, _):
        cols = pl.ds(pl.multiple_of(j * 256, 256), 256)
        e = et[:, cols]
        average, inv = norm_stats(e)
        normed = (e - average) * inv
        g = df[:, cols]
        scaled = g * p_ref[:, 0:1]
        total = jnp.sum(scaled, axis=0, keepdims=True) * (1.0 / D)
        crossed = jnp.sum(scaled * normed, axis=0, keepdims=True) * (1.0 / D)
        dx[:, cols] = (dmid[:, cols] + inv * (scaled - total - normed * crossed)).astype(BF16)
        dgp[0] += lane_sums(g * normed)
        dgp[1] += lane_sums(g)
        return 0

    lax.fori_loop(0, SEQ // 256, norm_cols, 0)
    swap(dx, xf_ref)
    for i in (3, 2, 4):
        stage_far(i)
    ones = jnp.ones((8, SEQ), BF16)
    v0[...] = jnp.zeros_like(v0)
    for n in range(2):
        v0[n : n + 1, :] = jnp.sum(dgp[n].T, axis=0, keepdims=True)
        v0[2 + n : 3 + n, :] = jnp.sum(dgs_ref[n].T, axis=0, keepdims=True)
        v0[6 + n : 7 + n, :] = dbf_ref[n, 0:1, :]
    v0[4:5, :] = mm(ones, dqt[...], NT)[0:1]
    v0[5:6, :] = mm(ones, dv[...])[0:1]
    for hh in range(hid):
        row, lane = divmod(hh * fcols, D)
        v0[8 + row : 9 + row, lane : lane + fcols] = dbe_ref[hh, 0:1, :]
    vec_send(DP, v0)
    vec_sum(DP, v0, v1)
    vec_send(MP, v1)
    stage_far(1)
    stage_far(0)
    vec_sum(MP, v1, v2)
    vec_send(HID, v2)
    stage_end(3)
    stage_end(2)
    stage_end(4)
    stage_end(1)
    stage_end(0)
    vec_sum(HID, v2, vecf_ref)
    for copy in held:
        copy.wait()
    for copy in moved:
        copy.wait_recv()
    wire.finish()


def backward(o, dw2, near_r, near_e, last_sum, qkv, do, lse, seg, present, ft, w1, et, dmid, cols, dbe, dbf, dgs):
    dp, mp, hid = lax.axis_size("dp"), lax.axis_size("mp"), lax.axis_size("hidden")
    sds = jax.ShapeDtypeStruct
    wide = D // hid
    half = D // mp // dp
    half2, c2 = dw2.shape[3:]
    fc = near_e.shape[3]
    ff = hid * fc
    out_shape = (
        sds((D // mp, mp * SEQ), BF16), sds((D // mp, mp * SEQ), BF16), sds((3, half, wide), F32),
        sds((half2, c2), F32), sds((half, fc), F32), sds((half, fc), F32), sds((16, D), F32),
    )
    vm = lambda *shape: pltpu.VMEM(shape, BF16)
    vf = lambda *shape: pltpu.VMEM(shape, F32)
    slabs = ((hid, mp, half, 2 * wide), (hid, mp, half, wide), (mp, hid, half2, c2))
    after = ((hid, half, 2 * wide), (mp, half, wide), (hid, half2, c2), (half, ff), (mp, half, fc))
    ends = ((half, 2 * wide), (half, wide), (half2, c2), (half, fc), (half, fc))
    near = (mp, hid, mp, mp, hid)
    far = (hid, mp, hid, hid, mp)
    scratch = [
        vm(SEQ, 3 * D), vm(SEQ, D), vf(SEQ, SEQ), vm(PAIR, SEQ), vm(D, SEQ), vm(SEQ, D), vm(SEQ, D),
        vf(SEQ, PAIR), vf(SEQ, PAIR), vm(D, SEQ), vf(D, SEQ), vf(D, SEQ), vf(2, D, 128),
    ]
    scratch += [vm(dp - 1, *s) for s in slabs]
    scratch += [vm(dp, *s) for s in slabs[:2]] + [vm(*s) for s in slabs[2:]]
    scratch += [vm(n - 1, *s) for n, s in zip(near[:3], after)] + [vm(n, *s) for n, s in zip(near[3:], after[3:])]
    scratch += [vm(*s) for s in after]
    scratch += [vm(n - 1, *s) for n, s in zip(far, ends)]
    scratch += [vf(16, D), vf(dp - 1, 16, D), vf(mp - 1, 16, D), vf(hid - 1, 16, D), vf(16, D), vf(16, D)]
    n = dp + mp + hid - 3 + 2 * mp + 4 * (dp - 1) + 1 + 6 * (mp + hid - 2)
    scratch += [pltpu.SemaphoreType.DMA((4 * PAIRS + 6 + hid,)), pltpu.SemaphoreType.DMA((n,)), pltpu.SemaphoreType.DMA((n,))]
    hbm = pl.BlockSpec(memory_space=pl.ANY)
    vmem = pl.BlockSpec(memory_space=pltpu.VMEM)
    return pl.pallas_call(
        backward_kernel,
        out_shape=out_shape,
        in_specs=[hbm] * 7 + [vmem] * 3 + [hbm] * 4 + [vmem] * 4,
        out_specs=(hbm, hbm) + (vmem,) * 5,
        scratch_shapes=scratch,
        compiler_params=params(collective_id=1, has_side_effects=True),
        name="backward",
    )(o, dw2, near_r, near_e, last_sum, qkv, do, lse, seg, present, ft, w1, et, dmid, cols, dbe, dbf, dgs)


def local(
    stored, positions, segments, present, norm_gains, norm_biases, input_proj, input_bias, output_proj,
    output_bias, expand_weight, expand_bias, reduce_weight, reduce_bias, cotangent,
):
    mp, hid, dp = lax.axis_size("mp"), lax.axis_size("hidden"), lax.axis_size("dp")
    m, h, d = lax.axis_index("mp"), lax.axis_index("hidden"), lax.axis_index("dp")
    rows_mp, hcols, fcols = D // mp, D // hid, expand_weight.shape[1]
    half = rows_mp // dp
    cols = [norm_gains[:1], norm_biases[:1], norm_gains[1:], norm_biases[1:], output_bias[None], reduce_bias[None]]
    cols = jnp.concatenate([c.astype(F32) for c in cols] + [jnp.zeros((2, rows_mp), F32)])
    cols = jnp.pad(cols, ((0, 0), (0, -rows_mp % 128)))
    rows = jnp.concatenate(
        [
            expand_bias.astype(F32)[None],
            jnp.pad(input_bias.astype(F32), ((0, 0), (0, fcols - hcols))),
            jnp.zeros((5, fcols), F32),
        ]
    )
    w1 = lax.dynamic_slice_in_dim(input_proj, d * half, half, 0)
    w2 = output_proj
    if hcols // dp % 16:
        w2 = lax.dynamic_slice_in_dim(output_proj, d * (hcols // dp), hcols // dp, 0)
    pos = positions[None]
    rate = np.exp(np.arange(D // 2, dtype=np.float32) * np.float32(-math.log(10000.0) / (D // 2)))[None]
    seg, present = segments[None], present[None]
    et, ft, w1f, qkv, out_t, dmid, do, near_r, near_e, last_sum, _, _, lse, cols, dbe, dw2, dbf, dgs = forward(
        stored, cotangent, w1[:, :2].reshape(half, 2 * hcols), w1[:, 2], w2, expand_weight, reduce_weight, cols, rows,
        pos, jnp.asarray(rate), seg, present,
    )
    output, d_stored, g1, d_output, d_expand, d_reduce, vec = backward(
        out_t,
        dw2.reshape(mp, hid, dp, hcols // dp, rows_mp),
        near_r,
        near_e,
        last_sum,
        qkv, do, lse, seg, present, ft, w1f, et, dmid, cols, dbe, dbf, dgs,
    )
    piece = D // (hid * mp * dp)
    cut = lambda x, at, size: lax.dynamic_slice_in_dim(x, at * size, size, x.ndim - 1)
    dg = cut(vec[:4].reshape(2, 2, D), (m * dp + d) * hid + h, piece)
    db_proj = cut(vec[4:6], h * dp + d, hcols // dp)
    db_feed = cut(vec[6:8], m * dp + d, half)
    dbe = cut(vec[8:].reshape(-1)[: hid * fcols], h * dp + d, fcols // dp)
    d_input = g1.transpose(1, 0, 2)
    return (
        output, d_stored.astype(F32), dg[:, 0], dg[:, 1], d_input, db_proj, d_output, db_feed[1], d_expand, dbe, d_reduce,
        db_feed[0],
    )


def solution(mesh):
    placed = (
        P("mp", ("dp", "hidden")),
        P(("dp", "hidden")),
        P(("dp", "hidden", "mp")),
        P(("dp", "hidden", "mp")),
        P(None, "mp"),
        P(None, "mp"),
        P("mp", None, "hidden"),
        P(None, "hidden"),
        P("hidden", "mp"),
        P("mp"),
        P("mp", "hidden"),
        P("hidden"),
        P("mp", "hidden"),
        P("mp"),
        P("mp", ("dp", "hidden")),
    )
    return jax.shard_map(
        local,
        mesh=mesh,
        in_specs=placed,
        out_specs=(
            P("mp", ("dp", "hidden")),
            P("mp", ("dp", "hidden")),
            P(None, ("mp", "dp", "hidden")),
            P(None, ("mp", "dp", "hidden")),
            P(("mp", "dp"), None, "hidden"),
            P(None, ("hidden", "dp")),
            P(("hidden", "dp"), "mp"),
            P(("mp", "dp")),
            P(("mp", "dp"), "hidden"),
            P(("hidden", "dp")),
            P(("mp", "dp"), "hidden"),
            P(("mp", "dp")),
        ),
        check_vma=False,
    )
```

```python
import functools
import math

import jax
import jax.numpy as jnp
import numpy as np
from jax import lax
from jax.experimental import pallas as pl
from jax.experimental.pallas import tpu as pltpu
from jax.sharding import PartitionSpec as P

D = 768
HEADS = 12
HD = 64
SEQ = 1024
QBB = 1024
PAIR = 2 * HD
PAIRS = HEADS // 2
EPS = 1e-06
MASKED = -1e30
F32 = jnp.float32
BF16 = jnp.bfloat16
VMEM_LIMIT = 60 * 1024 * 1024
PI_2 = (1.5703125, 4.837512969970703125e-4, 7.549789948768648e-8)

NN = (((1,), (0,)), ((), ()))
NT = (((1,), (1,)), ((), ()))


def mm(a, b, dims=NN):
    return lax.dot_general(a, b, dims, preferred_element_type=F32)


def whole(shape):
    return pl.BlockSpec(shape, lambda *_: (0,) * len(shape), pipeline_mode=pl.Buffered(1))


def params(**kw):
    return pltpu.CompilerParams(vmem_limit_bytes=VMEM_LIMIT, **kw)


def lane_sums(x):
    total = x[:, 0:128]
    for j in range(1, x.shape[1] // 128):
        total = total + x[:, j * 128 : (j + 1) * 128]
    return total


def norm_stats(e):
    average = jnp.sum(e, axis=0, keepdims=True) * (1.0 / D)
    spread = jnp.sum(e * e, axis=0, keepdims=True) * (1.0 / D) - average * average
    return average, lax.rsqrt(spread + EPS)


def fill_bias(bias_ref, seg_ref, present_ref):
    seg = seg_ref[...].astype(F32)
    key = jnp.where(present_ref[...] == 1, seg, -1.0)
    key_cols = jnp.broadcast_to(key, (8, SEQ)).T
    for i in range(SEQ // 256):
        same = key_cols[i * 256 : (i + 1) * 256, 0:1] == seg
        row_id = lax.broadcasted_iota(jnp.int32, (256, SEQ), 0) + i * 256
        col_id = lax.broadcasted_iota(jnp.int32, (256, SEQ), 1)
        bias_ref[i * 256 : (i + 1) * 256, :] = jnp.where(same | (row_id == col_id), 0.0, MASKED)


MESH = pl.DeviceIdType.MESH


class Wire:
    def __init__(self, send, recv):
        self.send_sem, self.recv_sem, self.count, self.sent = send, recv, 0, []
        self.me = (lax.axis_index("dp"), lax.axis_index("mp"), lax.axis_index("hidden"))
        self.size = (lax.axis_size("dp"), lax.axis_size("mp"), lax.axis_size("hidden"))

    def peer(self, axis, offset):
        where = list(self.me)
        where[axis] = lax.rem(where[axis] + offset, self.size[axis])
        return tuple(where)

    def origin(self, axis, offset):
        return lax.rem(self.me[axis] - offset + self.size[axis], self.size[axis])

    def meet(self):
        barrier = pltpu.get_barrier_semaphore()
        total = 0
        for axis in range(3):
            for offset in range(1, self.size[axis]):
                pl.semaphore_signal(barrier, 1, device_id=self.peer(axis, offset), device_id_type=MESH)
                total += 1
        pl.semaphore_wait(barrier, total)

    def send(self, src, dst, target):
        copy = pltpu.make_async_remote_copy(
            src, dst, self.send_sem.at[self.count], self.recv_sem.at[self.count], device_id=target, device_id_type=MESH
        )
        copy.start()
        self.count += 1
        self.sent.append(copy)
        return copy

    def keep(self, src, dst):
        copy = pltpu.make_async_copy(src, dst, self.send_sem.at[self.count])
        copy.start()
        self.count += 1
        return copy

    def finish(self):
        assert self.count <= self.send_sem.shape[0], self.count
        for copy in self.sent:
            copy.wait_send()


DP, MP, HID = 0, 1, 2


HALF = D // 2


def sin_cos(angles):
    turns = jnp.floor(angles * (2.0 / math.pi) + 0.5)
    r = ((angles - turns * PI_2[0]) - turns * PI_2[1]) - turns * PI_2[2]
    r2 = r * r
    s = r + r * r2 * (-1.6666654611e-1 + r2 * (8.3321608736e-3 + r2 * -1.9515295891e-4))
    c = 1.0 - 0.5 * r2 + r2 * r2 * (4.166664568298827e-2 + r2 * (-1.388731625493765e-3 + r2 * 2.443315711809948e-5))
    quarter = turns - 4.0 * jnp.floor(turns * 0.25)
    odd = (quarter == 1.0) | (quarter == 3.0)
    flip_s = quarter >= 2.0
    flip_c = (quarter == 1.0) | (quarter == 2.0)
    sine = jnp.where(odd, c, s)
    cosine = jnp.where(odd, s, c)
    return jnp.where(flip_s, -sine, sine), jnp.where(flip_c, -cosine, cosine)


def forward_kernel(
    x_ref, c_ref, w1a_ref, w1b_ref, w2_ref, we_ref, wr_ref, cols_ref, rows_ref, pos_ref, rate_ref, seg_ref, present_ref,
    et_out, ft_out, w1_out, qkv_out, out_out, dmid_out, do_out, near_r, near_e, last_sum, wef_ref, wrf_ref,
    lse_ref, p_ref, dbe_ref, dw2_ref, dbf_ref, dgs_ref,
    xt, ct, w1af, w1bf, w2f, rowsf, colsf, rates, tab, et, ft, f, w1, qkv, bias, vt, wb, at, out, wblk, dblk, w2c, theirs, sums,
    send, recv, z_send, z_recv, p_send, p_recv, c_send, c_recv, x_send, x_recv, n_send, n_recv, o_sem, local,
):
    wire = Wire(send, recv)
    d, m, h = wire.me
    dp, mp, hid = wire.size
    rows = D // mp
    wide = D // hid
    fcols = we_ref.shape[1]
    half = rows // dp
    offset = pl.multiple_of(d * half, half)
    half2 = wide // dp
    w2_part = w2_ref
    if w2_ref.shape[0] > half2:
        w2_part = w2_ref.at[pl.ds(pl.multiple_of(d * half2, half2), half2)]
    own = (
        (w1a_ref, lambda mm_, hh: w1af.at[hh, mm_, d], lambda: w1af.at[:, :, d], HID),
        (w1b_ref, lambda mm_, hh: w1bf.at[hh, mm_, d], lambda: w1bf.at[:, :, d], MP),
        (w2_part, lambda mm_, hh: w2f.at[mm_, hh, d], lambda: w2f.at[:, :, d], HID),
    )
    wire.meet()
    waits, stored = [], []
    first, second, third = {}, {}, {}

    def swap(src_ref, dst_ref):
        mine = pl.ds(pl.multiple_of(m * rows, rows), rows)
        moved = []
        for q in range(1, mp):
            to = wire.peer(MP, q)
            moved.append(wire.send(src_ref.at[:, pl.ds(pl.multiple_of(to[1] * SEQ, SEQ), SEQ)], dst_ref.at[mine], to))
        return moved, wire.keep(src_ref.at[:, pl.ds(pl.multiple_of(m * SEQ, SEQ), SEQ)], dst_ref.at[mine])

    def landed(pair):
        for copy in pair[0]:
            copy.wait_recv()
        pair[1].wait()

    def stage_one(i):
        src, dst, _, axis = own[i]
        first[i] = [wire.keep(src, dst(m, h))]
        first[i] += [wire.send(src, dst(m, h), wire.peer(axis, o)) for o in range(1, wire.size[axis])]

    def stage_two(i):
        _, dst, _, axis = own[i]
        other = MP if axis == HID else HID
        second[i] = []
        for o, copy in enumerate(first[i]):
            if o == 0:
                copy.wait()
            else:
                copy.wait_recv()
            at_ = wire.origin(axis, o)
            piece = dst(m, at_) if axis == HID else dst(at_, h)
            second[i] += [wire.send(piece, piece, wire.peer(other, q)) for q in range(1, wire.size[other])]

    def stage_three(i):
        for copy in second[i]:
            copy.wait_recv()
        third[i] = [wire.send(own[i][2](), own[i][2](), wire.peer(DP, r)) for r in range(1, dp)]

    def done(i):
        for copy in third[i]:
            copy.wait_recv()

    full = (wef_ref, wrf_ref)
    cut = tuple(ref.reshape(mp, dp, half, hid * fcols) for ref in full)
    part = (we_ref.at[pl.ds(offset, half)], wr_ref.at[pl.ds(offset, half)])
    whole_planes = ((1,), (1, hid - 1))
    order = [0, 1, hid - 1] + list(range(2, hid - 1))

    def plane_of(o):
        return lax.rem(h - o + hid, hid)

    def piece(j, mm_, dd, o):
        at_ = pl.ds(pl.multiple_of(mm_ * rows + dd * half, half), half)
        return full[j].at[at_, pl.ds(pl.multiple_of(plane_of(o) * fcols, fcols), fcols)]

    def remote(src, dst, sems, target):
        return pltpu.make_async_remote_copy(src, dst, sems[0], sems[1], device_id=target, device_id_type=MESH)

    def to_plane(j, o, q):
        src = part[j] if o == 0 else piece(j, m, d, o)
        return remote(src, piece(j, m, d, o), (p_send.at[j, o, q], p_recv.at[j, o, q]), wire.peer(MP, q))

    def slab(j, o):
        return cut[j].at[:, d, :, pl.ds(pl.multiple_of(plane_of(o) * fcols, fcols), fcols)]

    def to_depth(j, o):
        if o in whole_planes[j]:
            src = dst = slab(j, 0)
        else:
            src, dst = part[j], piece(j, m, d, 0)
        return remote(src, dst, (z_send.at[j, o], z_recv.at[j, o]), wire.peer(HID, o))

    def to_core(j, o, r):
        return remote(slab(j, o), slab(j, o), (c_send.at[j, o, r - 1], c_recv.at[j, o, r - 1]), wire.peer(DP, r))

    def keep_own(j):
        return pltpu.make_async_copy(part[j], piece(j, m, d, 0), local.at[j])

    def plane_start(j, o):
        if o:
            to_depth(j, o).wait_recv()
        else:
            keep_own(j).start()
        for q in range(1, mp):
            to_plane(j, o, q).start()

    def plane_wait(j, o):
        if o == 0:
            keep_own(j).wait()
        for q in range(1, mp):
            to_plane(j, o, q).wait_recv()

    def depth_start(j, o):
        to_depth(j, o).start()

    def apart(j):
        return [o for o in range(1, hid) if o not in whole_planes[j]]

    def core_start(j, o):
        if o in whole_planes[j]:
            to_depth(j, o).wait_recv()
        elif o:
            plane_wait(j, o)
        for r in range(1, dp):
            to_core(j, o, r).start()

    def arrived(j, o):
        for r in range(1, dp):
            to_core(j, o, r).wait_recv()

    small = [wire.send(cols_ref, colsf.at[m], wire.peer(MP, q)) for q in range(1, mp)]
    small += [wire.send(rows_ref, rowsf.at[h], wire.peer(HID, o)) for o in range(1, hid)]
    kept = [wire.keep(cols_ref, colsf.at[m]), wire.keep(rows_ref, rowsf.at[h])]
    stage_one(0)
    stage_one(1)
    x_in = swap(x_ref, xt)

    rates[...] = jnp.broadcast_to(rate_ref[...], (8, HALF)).T
    places = pos_ref[:, pl.ds(pl.multiple_of(m * SEQ, SEQ), SEQ)].astype(F32)

    def table_rows(j, _):
        at_ = pl.ds(pl.multiple_of(j * 64, 64), 64)
        sine, cosine = sin_cos(rates[at_, 0:1] * places)
        tab[at_, :] = sine
        tab[pl.ds(pl.multiple_of(j * 64 + HALF, 64), 64), :] = cosine
        return 0

    lax.fori_loop(0, 1, table_rows, 0)
    stage_two(0)
    stage_two(1)
    lax.fori_loop(1, HALF // 64, table_rows, 0)
    fill_bias(bias, seg_ref, present_ref)
    for copy in small:
        copy.wait_recv()
    for copy in kept:
        copy.wait()
    for mm_ in range(mp):
        p_ref[mm_ * rows : (mm_ + 1) * rows, 0:8] = colsf[mm_].T[:rows, :]
    wb[...] = jnp.zeros_like(wb)
    for hh in range(hid):
        wb[:, hh * wide : (hh + 1) * wide] = rowsf[hh, 1:2, :wide]
        wb[:, 2 * D + hh * wide : 2 * D + (hh + 1) * wide] = rowsf[hh, 2:3, :wide]
    landed(x_in)
    plane_start(1, 0)
    for j in (1, 0):
        for o in apart(j):
            depth_start(j, o)
    stage_one(2)

    def norm_cols(j, _):
        cols = pl.ds(pl.multiple_of(j * 256, 256), 256)
        e = xt[:, cols].astype(F32) + tab[:, cols]
        et[:, cols] = e
        average, inv = norm_stats(e)
        low = ((e - average) * inv * p_ref[:, 0:1] + p_ref[:, 1:2]).astype(BF16)
        ft[:, cols] = low
        f[cols, :] = low.T
        return 0

    lax.fori_loop(0, SEQ // 256, norm_cols, 0)
    stored += [wire.keep(et, et_out), wire.keep(ft, ft_out)]
    stage_three(0)
    stage_three(1)
    plane_start(0, 0)
    c_in = swap(c_ref, ct)
    def unpack(dd):
        for hh in range(hid):
            for mm_ in range(mp):
                at_ = slice(mm_ * rows + dd * half, mm_ * rows + (dd + 1) * half)
                for k in range(3):
                    if k < 2:
                        value = w1af[hh, mm_, dd, :, k * wide : (k + 1) * wide]
                    else:
                        value = w1bf[hh, mm_, dd]
                    w1[at_, k * D + hh * wide : k * D + (hh + 1) * wide] = value

    if dp == 2:
        for dd in range(dp):

            @pl.when(d == dd)
            def _():
                unpack(dd)

        done(0)
        done(1)
        for dd in range(dp):

            @pl.when(d == 1 - dd)
            def _():
                unpack(dd)

    else:
        done(0)
        done(1)
        for dd in range(dp):
            unpack(dd)
    stored.append(wire.keep(w1, w1_out))

    def cols_of(n, scale):
        cols = pl.ds(pl.multiple_of(n * 256, 256), 256)
        y = (mm(f[...], w1[:, cols]) + wb[:, cols]).astype(BF16)
        qkv[:, cols] = y * jnp.asarray(scale, BF16)
        return 0

    lax.fori_loop(0, D // 256, lambda n, c: cols_of(n, HD**-0.5), 0)
    stage_two(2)
    plane_wait(1, 0)
    for o in whole_planes[1]:
        depth_start(1, o)
    lax.fori_loop(D // 256, 3 * D // 256, lambda n, c: cols_of(n, 1.0), 0)
    stored.append(wire.keep(qkv, qkv_out))

    low = lax.broadcasted_iota(jnp.int32, (SEQ, PAIR), 1) < HD
    lse_ref[...] = jnp.zeros_like(lse_ref)

    def pair_of(p, _):
        lanes = pl.ds(pl.multiple_of(p * PAIR, PAIR), PAIR)
        k_lanes = pl.ds(pl.multiple_of(p * PAIR + D, PAIR), PAIR)
        v_lanes = pl.ds(pl.multiple_of(p * PAIR + 2 * D, PAIR), PAIR)
        vt[...] = qkv[:, v_lanes].T
        q = qkv[:, lanes]
        for hh in range(2):
            qm = jnp.where(low if hh == 0 else ~low, q, jnp.zeros_like(q))
            s = mm(qkv[:, k_lanes], qm, NT) + bias[...]
            top = jnp.max(s, axis=0, keepdims=True)
            e = jnp.exp(s - top)
            total = jnp.sum(e, axis=0, keepdims=True)
            o = mm(vt[hh * HD : (hh + 1) * HD, :], e.astype(BF16)) / total
            at[pl.ds(pl.multiple_of(p * PAIR + hh * HD, HD), HD), :] = o.astype(BF16)
            lse_ref[p, hh : hh + 1, :] = top + jnp.log(total)
        return 0

    lax.fori_loop(0, PAIRS // 3, pair_of, 0)
    plane_wait(0, 0)
    for o in whole_planes[0]:
        depth_start(0, o)
    for j in (1, 0):
        for o in apart(j):
            plane_start(j, o)
    lax.fori_loop(PAIRS // 3, 2 * PAIRS // 3, pair_of, 0)
    stage_three(2)
    for j in range(2):
        core_start(j, 0)
    lax.fori_loop(2 * PAIRS // 3, PAIRS, pair_of, 0)
    for copy in stored:
        copy.wait()
    landed(c_in)
    done(2)

    ot, ds_sum, st, bt, mid = bias.at[pl.ds(0, D)], tab, xt, ft, et
    tokens = [pl.ds(n * D, D) for n in range(3)]
    for mm_ in range(mp):
        for hh in range(hid):
            for dd in range(dp):
                at_ = hh * wide + dd * (wide // dp)
                w2c[at_ : at_ + wide // dp, mm_ * rows : (mm_ + 1) * rows] = w2f[mm_, hh, dd]
    w2t = w2c[...].T

    def middle_cols(j, _):
        cols = pl.ds(pl.multiple_of(j * 256, 256), 256)
        value = et[:, cols] + (mm(w2t, at[:, cols]) + p_ref[:, 4:5])
        mid[:, cols] = value
        ot[:, cols] = value + p_ref[:, 5:6]
        average, inv = norm_stats(value)
        s = ((value - average) * inv * p_ref[:, 2:3] + p_ref[:, 3:4]).astype(BF16)
        st[:, cols] = s
        qkv[cols, tokens[0]] = s.T
        qkv[cols, tokens[1]] = ct[:, cols].T
        return 0

    lax.fori_loop(0, SEQ // 256, middle_cols, 0)
    ds_sum[...] = jnp.zeros_like(ds_sum)

    def fetch(j, o):
        hcols = pl.ds(pl.multiple_of(plane_of(o) * fcols, fcols), fcols)
        return pltpu.make_async_copy(full[j].at[:, hcols], wblk.at[j], local.at[2 + j])

    def place(n):
        o = 0
        for k in range(1, hid):
            o = jnp.where(n == k, order[k], o)
        return o

    def swap_core(j, n, r):
        to = wire.peer(DP, r)
        return remote(
            dblk.at[j, :, to[0]], theirs.at[lax.rem(n, 2), j, r - 1], (x_send.at[j, n, r - 1], x_recv.at[j, n, r - 1]), to
        )

    def each_core(n, do):
        for j in range(2):
            for r in range(1, dp):
                do(swap_core(j, n, r))

    end = hid - 1

    def sum_depth(n):
        to = (d, m, plane_of(place(n)))
        return remote(sums.at[lax.rem(n, 2), 0], near_r.at[n], (n_send.at[n, 0], n_recv.at[n, 0]), to)

    def sum_plane(n, q):
        to = wire.peer(MP, q)
        return remote(sums.at[lax.rem(n, 2), 1, to[1]], near_e.at[n, q], (n_send.at[n, q], n_recv.at[n, q]), to)

    def save(j, n, last):
        slot = lax.rem(n, 2)
        if last:
            return pltpu.make_async_copy(sums.at[slot, j], last_sum.at[j], o_sem.at[j, n])
        if j == 0:
            return pltpu.make_async_copy(sums.at[0, 0], near_r.at[0], o_sem.at[0, 0])
        return pltpu.make_async_copy(sums.at[slot, 1, m], near_e.at[n, 0], o_sem.at[1, n])

    def add_cores(n, last=False):
        each_core(n, lambda copy: copy.wait_recv())
        slot = lax.rem(n, 2)
        for j in range(2):
            for k in range(mp):
                value = dblk[j, k, d].astype(F32)
                for r in range(1, dp):
                    value = value + theirs[slot, j, r - 1, k].astype(F32)
                sums[slot, j, k] = value.astype(BF16)
        if last:
            for j in range(2):
                save(j, n, True).start()
            return
        for q in range(1, mp):
            sum_plane(n, q).start()
        save(1, n, False).start()

    def gone(n):
        for q in range(1, mp):
            sum_plane(n, q).wait_send()
        save(1, n, False).wait()

    def block(n, _):
        o = place(n)
        hh = plane_of(o)
        for j in range(2):
            arrived(j, o)
        for j in range(2):
            fetch(j, o).start()
        for j in range(2):
            fetch(j, o).wait()

        pre = mm(qkv[:, tokens[0]], wblk[0]) + rowsf[hh, 0:1, :]
        cdf = 0.5 * (1.0 + lax.erf(pre * (1.0 / math.sqrt(2.0))))
        act = (pre * cdf).astype(BF16)
        slope = cdf + pre * jnp.exp(-0.5 * pre * pre) * (1.0 / math.sqrt(2.0 * math.pi))
        grad = (mm(qkv[:, tokens[1]], wblk[1]) * slope).astype(BF16)

        @pl.when(n == 3)
        def _():
            gone(0)
            save(0, 0, False).wait()

        @pl.when(n > 3)
        def _():
            gone(n - 3)
            sum_depth(n - 3).wait_send()

        @pl.when(n > 0)
        def _():
            add_cores(n - 1)
            each_core(n - 1, lambda copy: copy.wait_send())

        @pl.when(n == 1)
        def _():
            save(0, 0, False).start()

        @pl.when(n > 1)
        def _():
            sum_depth(n - 1).start()

        for j, value in enumerate((mm(ct[...], act), mm(st[...], grad))):
            for k in range(mp):
                for dd in range(dp):
                    at_ = k * rows + dd * half
                    dblk[j, k, dd] = value[at_ : at_ + half, :].astype(BF16)
        each_core(n, lambda copy: copy.start())
        dbe_ref[hh, 0:1, :] = jnp.sum(grad.astype(F32), axis=0, keepdims=True)
        ot[...] += mm(wblk[1], act, NT)
        ds_sum[...] += mm(wblk[0], grad, NT)

        for k in range(1, hid):

            @pl.when(n + 1 == k)
            def _():
                for j in range(2):
                    core_start(j, order[k])

        return 0

    lax.fori_loop(0, hid, block, 0)
    gone(end - 2)
    sum_depth(end - 2).wait_send()
    add_cores(end, True)
    dgs_ref[...] = jnp.zeros_like(dgs_ref)

    def back_cols(j, _):
        cols = pl.ds(pl.multiple_of(j * 256, 256), 256)
        value = mid[:, cols]
        out[:, cols] = ot[:, cols].astype(BF16)
        average, inv = norm_stats(value)
        normed = (value - average) * inv
        ds = ds_sum[:, cols]
        scaled = ds * p_ref[:, 2:3]
        total = jnp.sum(scaled, axis=0, keepdims=True) * (1.0 / D)
        crossed = jnp.sum(scaled * normed, axis=0, keepdims=True) * (1.0 / D)
        dmid = ct[:, cols].astype(F32) + inv * (scaled - total - normed * crossed)
        mid[:, cols] = dmid
        low_ = dmid.astype(BF16)
        bt[:, cols] = low_
        qkv[cols, tokens[2]] = mm(w2c[...], low_).astype(BF16).T
        dgs_ref[0] += lane_sums(ds * normed)
        dgs_ref[1] += lane_sums(ds)
        return 0

    lax.fori_loop(0, SEQ // 256, back_cols, 0)
    last = [wire.keep(out, out_out), wire.keep(mid, dmid_out), wire.keep(qkv.at[:, tokens[2]], do_out)]
    ones = jnp.ones((8, SEQ), BF16)
    dbf_ref[0] = mm(ones, ct[...], NT)
    dbf_ref[1] = mm(ones, bt[...], NT)
    for j in range(mp):
        dw2_ref[j] = mm(at[...], bt[j * rows : (j + 1) * rows, :], NT).astype(BF16)
    each_core(end, lambda copy: copy.wait_send())
    gone(end - 1)
    sum_depth(end - 1).wait_send()
    for j in range(2):
        save(j, end, True).wait()
    for n in range(end):
        if n:
            sum_depth(n).wait_recv()
        for q in range(1, mp):
            sum_plane(n, q).wait_recv()
    for copy in last:
        copy.wait()
    wire.finish()
    for j in range(2):
        for o in range(hid):
            if o:
                to_depth(j, o).wait_send()
            if o not in whole_planes[j]:
                for q in range(1, mp):
                    to_plane(j, o, q).wait_send()
            for r in range(1, dp):
                to_core(j, o, r).wait_send()


def forward(x, c, w1a, w1b, w2, we, wr, cols, rows, pos, rate, seg, present):
    dp, mp, hid = lax.axis_size("dp"), lax.axis_size("mp"), lax.axis_size("hidden")
    half = D // mp // dp
    fc = we.shape[1]
    ff = hid * fc
    sds = jax.ShapeDtypeStruct
    out_shape = (
        sds((D, SEQ), F32), sds((D, SEQ), BF16), sds((D, 3 * D), BF16), sds((SEQ, 3 * D), BF16),
        sds((D, SEQ), BF16), sds((D, SEQ), F32), sds((SEQ, D), BF16), sds((hid - 1, mp, half, fc), BF16),
        sds((hid - 1, mp, half, fc), BF16), sds((2, mp, half, fc), BF16), sds((D, ff), BF16), sds((D, ff), BF16),
        sds((PAIRS, 8, SEQ), F32), sds((D, 128), F32), sds((hid, 8, fc), F32), sds((mp, D, D // mp), BF16),
        sds((2, 8, D), F32), sds((2, D, 128), F32),
    )
    n = (mp - 1) + (hid - 1) + 2 + 2 * hid + mp + 2 * hid * (mp - 1) + mp * (hid - 1) + 3 * (dp - 1) + 2 * mp + 7
    hbm = pl.BlockSpec(memory_space=pl.ANY)
    vmem = pl.BlockSpec(memory_space=pltpu.VMEM)
    vm = lambda dtype, *shape: pltpu.VMEM(shape, dtype)
    sem = lambda *shape: pltpu.SemaphoreType.DMA(shape)
    return pl.pallas_call(
        forward_kernel,
        out_shape=out_shape,
        in_specs=[hbm] * 9 + [vmem] * 4,
        out_specs=(hbm,) * 12 + (vmem,) * 6,
        scratch_shapes=[
            vm(BF16, D, SEQ), vm(BF16, D, SEQ), vm(BF16, hid, mp, dp, half, w1a.shape[1]),
            vm(BF16, hid, mp, dp, half, w1b.shape[1]), vm(BF16, mp, hid, dp, D // hid // dp, w2.shape[1]), vm(F32, hid, *rows.shape),
            vm(F32, mp, *cols.shape), vm(F32, HALF, 8),
            vm(F32, D, SEQ), vm(F32, D, SEQ), vm(BF16, D, SEQ), vm(BF16, SEQ, D), vm(BF16, D, 3 * D),
            vm(BF16, SEQ, 3 * D), vm(F32, SEQ, SEQ), vm(BF16, PAIR, SEQ), vm(F32, 1, 3 * D),
            vm(BF16, D, SEQ), vm(BF16, D, SEQ), vm(BF16, 2, D, fc), vm(BF16, 2, mp, dp, half, fc), vm(BF16, D, D),
            vm(BF16, 2, 2, dp - 1, mp, half, fc), vm(BF16, 2, 2, mp, half, fc),
            sem(n), sem(n), sem(2, hid), sem(2, hid), sem(2, hid, mp), sem(2, hid, mp),
            sem(2, hid, dp - 1), sem(2, hid, dp - 1), sem(2, hid, dp - 1), sem(2, hid, dp - 1),
            sem(hid, mp), sem(hid, mp), sem(2, hid), sem(4),
        ],
        compiler_params=params(collective_id=0, has_side_effects=True),
        name="forward",
    )(x, c, w1a, w1b, w2, we, wr, cols, rows, pos, rate, seg, present)


def backward_kernel(
    o_ref, dw2_ref, near_r, near_e, last_sum, qkv_in, do_in, lse_ref, seg_ref, present_ref, ft_in, w_in, et_in, dmid_in, p_ref,
    dbe_ref, dbf_ref, dgs_ref,
    of_ref, xf_ref, g1_ref, g2_ref, ge_ref, gr_ref, vecf_ref,
    qkv, do, bias, kt, dqt, dk, dv, dka, dva, ft, et, dmid, dgp,
    a0, a1, a2, o0, o1, s2, b0, b1, b2, be, br, t0, t1, t2, t3, t4, c0, c1, c2, c3, c4,
    v0, va, vb, vc, v1, v2, loads, send, recv,
):
    wire = Wire(send, recv)
    d, m, h = wire.me
    dp, mp, hid = wire.size
    rows = D // mp
    wide = D // hid
    half = rows // dp
    fcols = ge_ref.shape[1]
    v_in = (va, vb, vc)
    slab0 = o0.shape[1:]
    hslice = lambda hh: pl.ds(pl.multiple_of(hh * fcols, fcols), fcols)

    def load(n, src, dst):
        copy = pltpu.make_async_copy(src, dst, loads.at[n])
        copy.start()
        return copy

    parts = []
    for p in range(PAIRS):
        got = []
        for k in range(3):
            lanes = slice(k * D + p * PAIR, k * D + (p + 1) * PAIR)
            got.append(load(4 * p + k, qkv_in.at[:, lanes], qkv.at[:, lanes]))
        lanes = slice(p * PAIR, (p + 1) * PAIR)
        got.append(load(4 * p + 3, do_in.at[:, lanes], do.at[:, lanes]))
        parts.append(got)
    others = [load(4 * PAIRS + i, a, b) for i, (a, b) in enumerate(((ft_in, ft), (et_in, et), (dmid_in, dmid)))]
    wire.meet()
    items = (
        (lambda dd: o0.at[dd], a0, o0.at[d], b0, t0, c0, None, MP, HID),
        (lambda dd: o1.at[dd], a1, o1.at[d], b1, t1, c1, None, HID, HID),
        (lambda dd: dw2_ref.at[:, :, dd], a2, s2, b2, t2, c2, g2_ref, MP, MP),
        (None, None, None, be, t3, c3, ge_ref, MP, None),
        (None, None, None, br, t4, c4, gr_ref, HID, None),
    )
    core, kept, near, far = {}, {}, {}, {}
    end = hid - 1
    plane = lambda o: lax.rem(h - o + hid, hid)
    order = [0, 1, hid - 1] + list(range(2, hid - 1))
    at = 4 * PAIRS + 4
    own = {
        4: [load(at, near_r, br.at[pl.ds(0, end)])],
        3: [load(at + 1 + n, near_e.at[n], be.at[:, :, hslice(plane(order[n]))]) for n in range(end)],
    }
    own[3].append(load(at + 1 + end, last_sum.at[1, m], be.at[0, :, hslice(plane(order[end]))]))

    def stage_core(i):
        src, a, s = items[i][:3]
        core[i] = [wire.send(src(wire.peer(DP, r)[0]), a.at[r - 1], wire.peer(DP, r)) for r in range(1, dp)]
        if i > 1:
            kept[i] = wire.keep(src(d), s)

    def add_all(dst, own, others, shape):
        lead = shape[:-2]

        def body(n, _):
            index = []
            for size in reversed(lead):
                index.insert(0, lax.rem(n, size))
                n = lax.div(n, size)
            index = tuple(index)
            value = own[index].astype(F32)
            for j in range(others.shape[0]):
                value = value + others[(j,) + index].astype(F32)
            dst[index] = value.astype(dst.dtype)
            return 0

        lax.fori_loop(0, math.prod(lead), body, 0)

    def part(i, ref, axis, at, leads):
        if items[i][8] is None:
            return ref.at[(slice(None),) * len(leads) + (slice(None), hslice(at))] if axis == HID else ref.at[at]
        return ref.at[at] if leads[0] == axis else ref.at[:, at]

    def leads_of(i):
        lead = items[i][8]
        return (MP,) if lead is None else ((HID, MP) if lead == HID else (MP, HID))

    def stage_near(i):
        if i == 4:
            near[4] = [wire.send(last_sum.at[0], br.at[end], wire.peer(HID, hid - order[end]))]
            return
        if i == 3:
            here = hslice(plane(order[end]))
            near[3] = []
            for q in range(1, mp):
                to = wire.peer(MP, q)
                near[3].append(wire.send(last_sum.at[1, to[1]], be.at[q, :, here], to))
            return
        _, a, s, b, t, c, g, axis, _ = items[i]
        for copy in core[i]:
            copy.wait_recv()
        if i in kept:
            kept[i].wait()
        add_all(s, s, a, s.shape)
        near[i] = [
            wire.send(part(i, s, axis, wire.peer(axis, q)[axis], leads_of(i)), b.at[q - 1], wire.peer(axis, q))
            for q in range(1, wire.size[axis])
        ]

    def stage_far(i):
        _, a, s, b, t, c, g, axis, lead = items[i]
        if i < 3:
            for copy in near[i] if i else nears_half[0] + nears_half[1]:
                copy.wait_recv()
            add_all(t, part(i, s, axis, wire.me[axis], leads_of(i)), b, t.shape)
        else:
            for copy in near[i]:
                copy.wait_recv()
            for copy in own[i]:
                copy.wait()
            add_all(t, b.at[0], b.at[pl.ds(1, b.shape[0] - 1)], t.shape)
        other = MP if axis == HID else HID
        left = tuple(x for x in leads_of(i) if x != axis)
        far[i] = []
        for q in range(1, wire.size[other]):
            to = wire.peer(other, q)
            far[i].append(wire.send(part(i, t, other, to[other], left), c.at[q - 1], to))

    def stage_end(i):
        _, a, s, b, t, c, g, axis, lead = items[i]
        other = MP if axis == HID else HID
        left = tuple(x for x in leads_of(i) if x != axis)
        for copy in far[i]:
            copy.wait_recv()
        value = part(i, t, other, wire.me[other], left)[...].astype(F32)
        for j in range(c.shape[0]):
            value = value + c[j].astype(F32)
        if i == 0:
            g1_ref[0] = value[:, :wide]
            g1_ref[1] = value[:, wide:]
        elif i == 1:
            g1_ref[2] = value
        else:
            g[...] = value

    moved, held = [], []

    def swap(src_ref, dst_ref):
        mine = pl.ds(pl.multiple_of(m * SEQ, SEQ), SEQ)
        for q in range(1, mp):
            to = wire.peer(MP, q)
            moved.append(wire.send(src_ref.at[pl.ds(pl.multiple_of(to[1] * rows, rows), rows)], dst_ref.at[:, mine], to))
        held.append(wire.keep(src_ref.at[pl.ds(pl.multiple_of(m * rows, rows), rows)], dst_ref.at[:, mine]))

    vec = {}

    def vec_send(axis, src):
        vec[axis] = [wire.send(src, v_in[axis].at[o - 1], wire.peer(axis, o)) for o in range(1, wire.size[axis])]

    def vec_sum(axis, src, dst):
        for copy in vec[axis]:
            copy.wait_recv()
        total = src[...]
        for j in range(wire.size[axis] - 1):
            total = total + v_in[axis][j]
        dst[...] = total

    stage_near(4)
    stage_near(3)
    stage_core(2)
    swap(o_ref, of_ref)
    fill_bias(bias, seg_ref, present_ref)
    low = lax.broadcasted_iota(jnp.int32, (QBB, PAIR), 1) < HD

    def pair_of(p, _):
        off = pl.multiple_of(p * PAIR, PAIR)
        lanes = pl.ds(off, PAIR)
        k_lanes = pl.ds(pl.multiple_of(off + D, PAIR), PAIR)
        v_lanes = pl.ds(pl.multiple_of(off + 2 * D, PAIR), PAIR)
        kt[...] = qkv[:, k_lanes].T
        dka[...] = jnp.zeros_like(dka)
        dva[...] = jnp.zeros_like(dva)

        def block(j, _):
            cols = pl.ds(pl.multiple_of(j * QBB, QBB), QBB)
            q = qkv[cols, lanes]
            g = do[cols, lanes]
            for hh in range(2):
                keep = low if hh == 0 else ~low
                qm = jnp.where(keep, q, jnp.zeros_like(q))
                gm = jnp.where(keep, g, jnp.zeros_like(g))
                e = jnp.exp(mm(qkv[:, k_lanes], qm, NT) + bias[:, cols] - lse_ref[p, hh : hh + 1, cols])
                t = e * mm(qkv[:, v_lanes], gm, NT)
                ds = (t - e * jnp.sum(t, axis=0, keepdims=True)).astype(BF16)
                dva[...] += mm(e.astype(BF16), gm)
                dka[...] += mm(ds, qm)
                dq = mm(kt[hh * HD : (hh + 1) * HD, :], ds) * HD**-0.5
                dqt[pl.ds(pl.multiple_of(off + hh * HD, HD), HD), cols] = dq.astype(BF16)
            return 0

        lax.fori_loop(0, SEQ // QBB, block, 0)
        dk[:, lanes] = dka[...].astype(BF16)
        dv[:, lanes] = dva[...].astype(BF16)
        return 0

    def pairs(first, last):
        for p in range(first, last):
            for copy in parts[p]:
                copy.wait()
        lax.fori_loop(first, last, pair_of, 0)

    span = D // 2
    each = hid // 2

    def weight_half(g):
        wide_k = mm(ft[...], dk[:, g * span : (g + 1) * span]).astype(BF16)
        wide_v = mm(ft[...], dv[:, g * span : (g + 1) * span]).astype(BF16)
        for hh in range(g * each, (g + 1) * each):
            lanes = slice((hh - g * each) * wide, (hh - g * each + 1) * wide)
            value_q = mm(ft[...], dqt[hh * wide : (hh + 1) * wide, :], NT).astype(BF16)
            for mm_ in range(mp):
                for dd in range(dp):
                    at_ = slice(mm_ * rows + dd * half, mm_ * rows + (dd + 1) * half)
                    o0[dd, hh, mm_, :, 0:wide] = value_q[at_, :]
                    o0[dd, hh, mm_, :, wide : 2 * wide] = wide_k[at_, lanes]
                    o1[dd, hh, mm_] = wide_v[at_, lanes]

    cores_half, nears_half = {}, {}

    def core_half(g):
        hs = pl.ds(g * each, each)
        cores_half[g] = [
            wire.send(o0.at[wire.peer(DP, r)[0], hs], a0.at[r - 1, hs], wire.peer(DP, r)) for r in range(1, dp)
        ]

    def near_half(g):
        hs = pl.ds(g * each, each)
        for copy in cores_half[g]:
            copy.wait_recv()
        add_all(o0.at[d, hs], o0.at[d, hs], a0.at[:, hs], (each,) + slab0[1:])
        nears_half[g] = []
        for q in range(1, mp):
            to = wire.peer(MP, q)
            nears_half[g].append(wire.send(o0.at[d, hs, to[1]], b0.at[q - 1, hs], to))

    pairs(0, PAIRS // 2)
    stage_near(2)
    for copy in others:
        copy.wait()
    weight_half(0)
    core_half(0)
    pairs(PAIRS // 2, PAIRS // 2 + 1)
    near_half(0)
    pairs(PAIRS // 2 + 1, PAIRS)
    w1 = qkv.at[pl.ds(0, D)]
    w_load = load(4 * PAIRS + 3, w_in, w1)
    weight_half(1)
    stage_core(1)
    core_half(1)
    df = bias.at[pl.ds(0, D)]
    w_load.wait()
    dx = ft

    def feature_cols(j, _):
        cols = pl.ds(pl.multiple_of(j * 256, 256), 256)
        value = mm(w1[:, 0:D], dqt[:, cols])
        value += mm(w1[:, D : 2 * D], dk[cols, :], NT)
        value += mm(w1[:, 2 * D : 3 * D], dv[cols, :], NT)
        df[:, cols] = value
        return 0

    lax.fori_loop(0, SEQ // 512, feature_cols, 0)
    stage_near(1)
    near_half(1)
    lax.fori_loop(SEQ // 512, SEQ // 256, feature_cols, 0)
    dgp[...] = jnp.zeros_like(dgp)

    def norm_cols(j, _):
        cols = pl.ds(pl.multiple_of(j * 256, 256), 256)
        e = et[:, cols]
        average, inv = norm_stats(e)
        normed = (e - average) * inv
        g = df[:, cols]
        scaled = g * p_ref[:, 0:1]
        total = jnp.sum(scaled, axis=0, keepdims=True) * (1.0 / D)
        crossed = jnp.sum(scaled * normed, axis=0, keepdims=True) * (1.0 / D)
        dx[:, cols] = (dmid[:, cols] + inv * (scaled - total - normed * crossed)).astype(BF16)
        dgp[0] += lane_sums(g * normed)
        dgp[1] += lane_sums(g)
        return 0

    lax.fori_loop(0, SEQ // 256, norm_cols, 0)
    swap(dx, xf_ref)
    for i in (3, 2, 4):
        stage_far(i)
    ones = jnp.ones((8, SEQ), BF16)
    v0[...] = jnp.zeros_like(v0)
    for n in range(2):
        v0[n : n + 1, :] = jnp.sum(dgp[n].T, axis=0, keepdims=True)
        v0[2 + n : 3 + n, :] = jnp.sum(dgs_ref[n].T, axis=0, keepdims=True)
        v0[6 + n : 7 + n, :] = dbf_ref[n, 0:1, :]
    v0[4:5, :] = mm(ones, dqt[...], NT)[0:1]
    v0[5:6, :] = mm(ones, dv[...])[0:1]
    for hh in range(hid):
        row, lane = divmod(hh * fcols, D)
        v0[8 + row : 9 + row, lane : lane + fcols] = dbe_ref[hh, 0:1, :]
    vec_send(DP, v0)
    stage_far(0)
    vec_sum(DP, v0, v1)
    vec_send(MP, v1)
    stage_far(1)
    vec_sum(MP, v1, v2)
    vec_send(HID, v2)
    stage_end(3)
    stage_end(2)
    stage_end(4)
    stage_end(1)
    stage_end(0)
    vec_sum(HID, v2, vecf_ref)
    for copy in held:
        copy.wait()
    for copy in moved:
        copy.wait_recv()
    wire.finish()


def backward(o, dw2, near_r, near_e, last_sum, qkv, do, lse, seg, present, ft, w1, et, dmid, cols, dbe, dbf, dgs):
    dp, mp, hid = lax.axis_size("dp"), lax.axis_size("mp"), lax.axis_size("hidden")
    sds = jax.ShapeDtypeStruct
    wide = D // hid
    half = D // mp // dp
    half2, c2 = dw2.shape[3:]
    fc = near_e.shape[3]
    ff = hid * fc
    out_shape = (
        sds((D // mp, mp * SEQ), BF16), sds((D // mp, mp * SEQ), BF16), sds((3, half, wide), F32),
        sds((half2, c2), F32), sds((half, fc), F32), sds((half, fc), F32), sds((16, D), F32),
    )
    vm = lambda *shape: pltpu.VMEM(shape, BF16)
    vf = lambda *shape: pltpu.VMEM(shape, F32)
    slabs = ((hid, mp, half, 2 * wide), (hid, mp, half, wide), (mp, hid, half2, c2))
    after = ((hid, half, 2 * wide), (mp, half, wide), (hid, half2, c2), (half, ff), (mp, half, fc))
    ends = ((half, 2 * wide), (half, wide), (half2, c2), (half, fc), (half, fc))
    near = (mp, hid, mp, mp, hid)
    far = (hid, mp, hid, hid, mp)
    scratch = [
        vm(SEQ, 3 * D), vm(SEQ, D), vf(SEQ, SEQ), vm(PAIR, SEQ), vm(D, SEQ), vm(SEQ, D), vm(SEQ, D),
        vf(SEQ, PAIR), vf(SEQ, PAIR), vm(D, SEQ), vf(D, SEQ), vf(D, SEQ), vf(2, D, 128),
    ]
    scratch += [vm(dp - 1, *s) for s in slabs]
    scratch += [vm(dp, *s) for s in slabs[:2]] + [vm(*s) for s in slabs[2:]]
    scratch += [vm(n - 1, *s) for n, s in zip(near[:3], after)] + [vm(n, *s) for n, s in zip(near[3:], after[3:])]
    scratch += [vm(*s) for s in after]
    scratch += [vm(n - 1, *s) for n, s in zip(far, ends)]
    scratch += [vf(16, D), vf(dp - 1, 16, D), vf(mp - 1, 16, D), vf(hid - 1, 16, D), vf(16, D), vf(16, D)]
    n = dp + mp + hid - 3 + 2 * mp + 4 * (dp - 1) + 1 + 6 * (mp + hid - 2)
    scratch += [pltpu.SemaphoreType.DMA((4 * PAIRS + 6 + hid,)), pltpu.SemaphoreType.DMA((n,)), pltpu.SemaphoreType.DMA((n,))]
    hbm = pl.BlockSpec(memory_space=pl.ANY)
    vmem = pl.BlockSpec(memory_space=pltpu.VMEM)
    return pl.pallas_call(
        backward_kernel,
        out_shape=out_shape,
        in_specs=[hbm] * 7 + [vmem] * 3 + [hbm] * 4 + [vmem] * 4,
        out_specs=(hbm, hbm) + (vmem,) * 5,
        scratch_shapes=scratch,
        compiler_params=params(collective_id=1, has_side_effects=True),
        name="backward",
    )(o, dw2, near_r, near_e, last_sum, qkv, do, lse, seg, present, ft, w1, et, dmid, cols, dbe, dbf, dgs)


def local(
    stored, positions, segments, present, norm_gains, norm_biases, input_proj, input_bias, output_proj,
    output_bias, expand_weight, expand_bias, reduce_weight, reduce_bias, cotangent,
):
    mp, hid, dp = lax.axis_size("mp"), lax.axis_size("hidden"), lax.axis_size("dp")
    m, h, d = lax.axis_index("mp"), lax.axis_index("hidden"), lax.axis_index("dp")
    rows_mp, hcols, fcols = D // mp, D // hid, expand_weight.shape[1]
    half = rows_mp // dp
    cols = [norm_gains[:1], norm_biases[:1], norm_gains[1:], norm_biases[1:], output_bias[None], reduce_bias[None]]
    cols = jnp.concatenate([c.astype(F32) for c in cols] + [jnp.zeros((2, rows_mp), F32)])
    cols = jnp.pad(cols, ((0, 0), (0, -rows_mp % 128)))
    rows = jnp.concatenate(
        [
            expand_bias.astype(F32)[None],
            jnp.pad(input_bias.astype(F32), ((0, 0), (0, fcols - hcols))),
            jnp.zeros((5, fcols), F32),
        ]
    )
    w1 = lax.dynamic_slice_in_dim(input_proj, d * half, half, 0)
    w2 = output_proj
    if hcols // dp % 16:
        w2 = lax.dynamic_slice_in_dim(output_proj, d * (hcols // dp), hcols // dp, 0)
    pos = positions[None]
    rate = np.exp(np.arange(D // 2, dtype=np.float32) * np.float32(-math.log(10000.0) / (D // 2)))[None]
    seg, present = segments[None], present[None]
    et, ft, w1f, qkv, out_t, dmid, do, near_r, near_e, last_sum, _, _, lse, cols, dbe, dw2, dbf, dgs = forward(
        stored, cotangent, w1[:, :2].reshape(half, 2 * hcols), w1[:, 2], w2, expand_weight, reduce_weight, cols, rows,
        pos, jnp.asarray(rate), seg, present,
    )
    output, d_stored, g1, d_output, d_expand, d_reduce, vec = backward(
        out_t,
        dw2.reshape(mp, hid, dp, hcols // dp, rows_mp),
        near_r,
        near_e,
        last_sum,
        qkv, do, lse, seg, present, ft, w1f, et, dmid, cols, dbe, dbf, dgs,
    )
    piece = D // (hid * mp * dp)
    cut = lambda x, at, size: lax.dynamic_slice_in_dim(x, at * size, size, x.ndim - 1)
    dg = cut(vec[:4].reshape(2, 2, D), (m * dp + d) * hid + h, piece)
    db_proj = cut(vec[4:6], h * dp + d, hcols // dp)
    db_feed = cut(vec[6:8], m * dp + d, half)
    dbe = cut(vec[8:].reshape(-1)[: hid * fcols], h * dp + d, fcols // dp)
    d_input = g1.transpose(1, 0, 2)
    return (
        output, d_stored.astype(F32), dg[:, 0], dg[:, 1], d_input, db_proj, d_output, db_feed[1], d_expand, dbe, d_reduce,
        db_feed[0],
    )


def solution(mesh):
    placed = (
        P("mp", ("dp", "hidden")),
        P(("dp", "hidden")),
        P(("dp", "hidden", "mp")),
        P(("dp", "hidden", "mp")),
        P(None, "mp"),
        P(None, "mp"),
        P("mp", None, "hidden"),
        P(None, "hidden"),
        P("hidden", "mp"),
        P("mp"),
        P("mp", "hidden"),
        P("hidden"),
        P("mp", "hidden"),
        P("mp"),
        P("mp", ("dp", "hidden")),
    )
    return jax.shard_map(
        local,
        mesh=mesh,
        in_specs=placed,
        out_specs=(
            P("mp", ("dp", "hidden")),
            P("mp", ("dp", "hidden")),
            P(None, ("mp", "dp", "hidden")),
            P(None, ("mp", "dp", "hidden")),
            P(("mp", "dp"), None, "hidden"),
            P(None, ("hidden", "dp")),
            P(("hidden", "dp"), "mp"),
            P(("mp", "dp")),
            P(("mp", "dp"), "hidden"),
            P(("hidden", "dp")),
            P(("mp", "dp"), "hidden"),
            P(("mp", "dp")),
        ),
        check_vma=False,
    )
```
